128 devices in a mesh: dom: 32 (over z, y, core), sub: 4 (over x).
Axes of the slice: x: 4, y: 4, z: 4, core: 2. Of those that a mesh axis runs over, the one named last changes fastest.
Arguments:
- charges: float32 [16384, 256], P(('dom', 'sub')), may hold values from -0.3 to 0.3
- points: float32 [3, 16384, 256], P(None, ('dom', 'sub')), may hold values from -1 to 1
- leaf_basis: float32 [16384, 64, 256], P(('dom', 'sub')), may hold values from -0.375 to 0.375
- child_transfer: float32 [16384, 64, 64], P(('dom', 'sub')), may hold values from -0.75 to 0.75
- parent_transfer: float32 [2048, 64, 64], P(('dom', 'sub')), may hold values from -0.75 to 0.75
- nodes_leaf: float32 [3, 16384, 64], P(None, ('dom', 'sub')), may hold values from -2 to 2
- nodes_mid: float32 [3, 2048, 64], P(None, ('dom', 'sub')), may hold values from -2 to 2
- nodes_top: float32 [3, 256, 64], P(None, ('dom', 'sub')), may hold values from -2 to 2
- near_list: int32 [16384, 6], P(('dom', 'sub')), may hold values from -1 to 16383, as said below
- far_leaf: int32 [16384, 16], P(('dom', 'sub')), may hold values from -1 to 16383, as said below
- far_mid: int32 [2048, 16], P(('dom', 'sub')), may hold values from -1 to 2047, as said below
- far_top: int32 [256, 16], P(('dom', 'sub')), may hold values from -1 to 255, as said below
Outputs:
- potential: float32 [16384, 256], P(('dom', 'sub'))
The draws below stay inside these ranges and needn't reach their ends.
Inputs may be any that keep to these rules, and one draw needn't show every extreme that they name: `near_list`: -1 marks an empty entry; a row's live entries come first, and its first entry is the leaf itself. Row l names only leaves of the aligned block of 128 leaves that holds l or of the blocks beside it. Some rows have all 6 entries live. `far_leaf`: -1 marks an empty entry; a row's live entries come first. Within each aligned block of 128 rows, the entries, empty ones counted, name clusters of each aligned block of 128 clusters exactly 16 times; in some row blocks all entries are live. `far_mid`: -1 marks an empty entry; a row's live entries come first. Within each aligned block of 16 rows, the entries, empty ones counted, name clusters of each aligned block of 16 clusters exactly 2 times; in some row blocks all entries are live. `far_top`: -1 marks an empty entry; a row's live entries come first; in some aligned blocks of 2 rows all entries are live.
All inputs are finite; a program needn't handle non-finite values.
Results may differ from the reference program's by a relative error of at most 0.0003.
Values sent between devices are 32-bit elements; how exact they have to be, the bound alone decides.
No kernel may reach another device: no remote copies, remote signals or barrier semaphores. Data moves between devices by JAX's collectives and lax.ppermute only.
A program may use at most 64 MiB of HBM per device.

```python
import jax
import jax.numpy as jnp
from jax import lax

P_SIZE = 256
R = 64
LEAF_DEV = 128
KN = 6
KF = 16
SHARDS = 128
LEAVES = 16384
CL1 = 2048
CL2 = 256


def device_counts(key, shards, rows, most):
    shifted = jax.random.randint(jax.random.fold_in(key, 1), (), 0, 4)
    heavy = (jnp.arange(shards) + shifted) % 4 == 0
    light = jax.random.randint(jax.random.fold_in(key, 2), (shards, rows), 1, most // 2 + 1)
    return jnp.where(heavy[:, None], most, light)


def far_lists(key, rows):
    orders = jax.vmap(lambda sub_key: jax.random.permutation(sub_key, SHARDS))(jax.random.split(jax.random.fold_in(key, 3), SHARDS))
    entries = jnp.arange(rows * KF)
    owners = (jnp.arange(SHARDS)[:, None] + orders[:, entries % SHARDS]) % SHARDS
    wanted = jax.random.randint(jax.random.fold_in(key, 4), (SHARDS, rows * KF), 0, rows)
    cluster_ids = (owners * rows + wanted).reshape(SHARDS, rows, KF)
    counts_live = device_counts(key, SHARDS, rows, KF)
    live = jnp.arange(KF)[None, None, :] < counts_live[:, :, None]
    return jnp.where(live, cluster_ids, -1).reshape(SHARDS * rows, KF).astype(jnp.int32)


def draw_far_leaf(key, part):
    return far_lists(jax.random.fold_in(key, 11), LEAF_DEV)


def draw_far_mid(key, part):
    return far_lists(jax.random.fold_in(key, 12), LEAF_DEV // 8)


def draw_far_top(key, part):
    rows = LEAF_DEV // 64
    base_key = jax.random.fold_in(key, 13)
    cluster_ids = jax.random.randint(jax.random.fold_in(base_key, 5), (SHARDS * rows, KF), 0, CL2)
    counts_live = device_counts(base_key, SHARDS, rows, KF).reshape(-1)
    live = jnp.arange(KF)[None, :] < counts_live[:, None]
    return jnp.where(live, cluster_ids, -1).astype(jnp.int32)


def draw_near_list(key, part):
    base_key = jax.random.fold_in(key, 14)
    leaves_all = jnp.arange(LEAVES)
    blocks = leaves_all // LEAF_DEV
    lower = jnp.maximum(blocks - 1, 0) * LEAF_DEV
    upper = jnp.minimum(blocks + 2, SHARDS) * LEAF_DEV
    raw_draw = jax.random.randint(jax.random.fold_in(base_key, 6), (LEAVES, KN), 0, 3 * LEAF_DEV)
    leaf_ids = lower[:, None] + raw_draw % (upper - lower)[:, None]
    leaf_ids = leaf_ids.at[:, 0].set(leaves_all)
    counts_live = device_counts(base_key, SHARDS, LEAF_DEV, KN).reshape(-1)
    live = jnp.arange(KN)[None, :] < counts_live[:, None]
    return jnp.where(live, leaf_ids, -1).astype(jnp.int32)


def levels(key, extent, cuts, smallest, top_value):
    def one(dim, shards_of):
        heights = jax.random.uniform(jax.random.fold_in(jax.random.fold_in(key, 6), dim), (shards_of,), jnp.float32, smallest / len(cuts), top_value / len(cuts))
        return jnp.repeat(jnp.exp(heights), extent[dim] // shards_of).reshape((-1,) + (1,) * (len(extent) - dim - 1))

    level = one(*cuts[0])
    for cut in cuts[1:]:
        level = level * one(*cut)
    return level


def noise(own_key, dims, scale, reach, cuts=(), dtype=jnp.bfloat16):
    loudness = levels(own_key, dims, cuts, -0.22, 0.18) if cuts else 1.0
    array = jax.random.normal(own_key, dims, jnp.float32) * scale * loudness
    return jnp.minimum(jnp.maximum(array, -reach), reach).astype(dtype)


def setup_inputs(seed: int = 0) -> dict:
    key_list = jax.random.split(jax.random.key(seed), 13)
    return {
        "charges": noise(key_list[0], (LEAVES, P_SIZE), 0.05, 0.3, ((0, 128),), jnp.float32),
        "points": jnp.clip(jax.random.uniform(key_list[1], (3, LEAVES, P_SIZE), jnp.float32, -1.0, 1.0) * levels(key_list[1], (3, LEAVES, P_SIZE), ((1, 128),), -0.4, 0.0), -1.0, 1.0),
        "leaf_basis": noise(key_list[2], (LEAVES, R, P_SIZE), P_SIZE ** -0.5, 0.375, ((0, 128),), jnp.float32),
        "child_transfer": noise(key_list[3], (LEAVES, R, R), R ** -0.5, 0.75, ((0, 128),), jnp.float32),
        "parent_transfer": noise(key_list[4], (CL1, R, R), R ** -0.5, 0.75, ((0, 128),), jnp.float32),
        "nodes_leaf": jnp.clip(jax.random.uniform(key_list[5], (3, LEAVES, R), jnp.float32, -2.0, 2.0) * levels(key_list[5], (3, LEAVES, R), ((1, 128),), -0.4, 0.0), -2.0, 2.0),
        "nodes_mid": jnp.clip(jax.random.uniform(key_list[6], (3, CL1, R), jnp.float32, -2.0, 2.0) * levels(key_list[6], (3, CL1, R), ((1, 128),), -0.4, 0.0), -2.0, 2.0),
        "nodes_top": jnp.clip(jax.random.uniform(key_list[7], (3, CL2, R), jnp.float32, -2.0, 2.0) * levels(key_list[7], (3, CL2, R), ((1, 128),), -0.4, 0.0), -2.0, 2.0),
        "near_list": draw_near_list(jax.random.fold_in(key_list[12], 71), 0),
        "far_leaf": draw_far_leaf(jax.random.fold_in(key_list[12], 71), 0),
        "far_mid": draw_far_mid(jax.random.fold_in(key_list[12], 71), 0),
        "far_top": draw_far_top(jax.random.fold_in(key_list[12], 71), 0),
    }


soften = 0.25
group_rows = 16
block_rows = 32

def kernel(delta_x, delta_y, delta_z):
    return lax.rsqrt(delta_x * delta_x + delta_y * delta_y + delta_z * delta_z + soften)

def near_field(targets, sources, picks_all, validity):
    row_count = targets.shape[1]
    width = targets.shape[2]
    groups = row_count // group_rows
    target_groups = jnp.transpose(targets.reshape(3, groups, group_rows, width), (1, 0, 2, 3))
    pick_groups = picks_all.reshape(groups, group_rows, -1)
    valid_groups = validity.reshape(groups, group_rows, -1).astype(jnp.float32)

    def one_group(pieces):
        target, picks, weights = pieces

        def accumulate(column, running):
            chosen = lax.dynamic_index_in_dim(picks, column, 1, keepdims=False)
            weight = lax.dynamic_index_in_dim(weights, column, 1, keepdims=False)
            nearby = jnp.take(sources, chosen, axis=1)
            values = kernel(target[0][:, :, None] - nearby[0][:, None, :], target[1][:, :, None] - nearby[1][:, None, :], target[2][:, :, None] - nearby[2][:, None, :])
            return running + lax.optimization_barrier(jnp.sum(values * nearby[3][:, None, :], axis=2)) * weight[:, None]
        return lax.fori_loop(0, picks.shape[1], accumulate, jnp.zeros((group_rows, width), jnp.float32))
    return lax.map(one_group, (target_groups, pick_groups, valid_groups)).reshape(row_count, width)

def couple(own_nodes, remote, validity):

    def accumulate(column, running):
        piece = lax.dynamic_index_in_dim(remote, column, 1, keepdims=False)
        weight = lax.dynamic_index_in_dim(validity, column, 1, keepdims=False)
        values = kernel(own_nodes[:, 0, :, None] - piece[:, 1, None, :], own_nodes[:, 1, :, None] - piece[:, 2, None, :], own_nodes[:, 2, :, None] - piece[:, 3, None, :])
        return running + lax.optimization_barrier(jnp.sum(values * piece[:, 0, None, :], axis=2)) * weight[:, None]
    return lax.fori_loop(0, remote.shape[1], accumulate, jnp.zeros((own_nodes.shape[0], own_nodes.shape[2]), jnp.float32))

def make_table(moments, nodes):
    return jnp.concatenate([moments[:, None, :], jnp.transpose(nodes, (1, 0, 2))], axis=1)

def far_level(moments, nodes, lists):
    table = make_table(moments, nodes)
    own_all = jnp.transpose(nodes, (1, 0, 2))
    blocks = lists.shape[0] // block_rows

    def one_block(pieces):
        own_block, list_block = pieces
        validity = (list_block >= 0).astype(jnp.float32)
        remote = jnp.take(table, jnp.maximum(list_block, 0), axis=0)
        return couple(own_block, remote, validity)
    result = lax.map(one_block, (own_all.reshape(blocks, block_rows, 3, -1), lists.reshape(blocks, block_rows, -1)))
    return result.reshape(lists.shape[0], -1)

def reference(charges, points, leaf_basis, child_transfer, parent_transfer, nodes_leaf, nodes_mid, nodes_top, near_list, far_leaf, far_mid, far_top):
    highest = lax.Precision.HIGHEST
    rank_width = leaf_basis.shape[1]
    leaf_moments = jnp.einsum('lrp,lp->lr', leaf_basis, charges, precision=highest)
    mid_moments = jnp.einsum('lij,lj->li', child_transfer, leaf_moments, precision=highest).reshape(-1, 8, rank_width).sum(axis=1)
    top_moments = jnp.einsum('lij,lj->li', parent_transfer, mid_moments, precision=highest).reshape(-1, 8, rank_width).sum(axis=1)
    leaf_local = far_level(leaf_moments, nodes_leaf, far_leaf)
    mid_local = far_level(mid_moments, nodes_mid, far_mid)
    top_local = far_level(top_moments, nodes_top, far_top)
    mid_down = mid_local + jnp.einsum('lji,lj->li', parent_transfer, jnp.repeat(top_local, 8, axis=0), precision=highest)
    leaf_down = leaf_local + jnp.einsum('lji,lj->li', child_transfer, jnp.repeat(mid_down, 8, axis=0), precision=highest)
    sources = jnp.concatenate([points, charges[None]], axis=0)
    near_sum = near_field(points, sources, jnp.maximum(near_list, 0).astype(jnp.int32), near_list >= 0)
    return jnp.einsum('lrp,lr->lp', leaf_basis, leaf_down, precision=highest) + near_sum
```

```python
import jax
import jax.numpy as jnp
from jax import lax
from jax.experimental import pallas as pl
from jax.experimental.pallas import tpu as pltpu
from jax.sharding import PartitionSpec as P

f32 = jnp.float32
bf16 = jnp.bfloat16
i32 = jnp.int32
soften = 0.25
AXES = ("dom", "sub")
NB = 2
TRANS = (((1,), (1,)), ((), ()))


def dot(a, b):
    return jnp.dot(a, b, preferred_element_type=f32)


def dot_t(a, b):
    return lax.dot_general(a, b, TRANS, preferred_element_type=f32)


def split3(v):
    h = v.astype(bf16).astype(f32)
    r = v - h
    m = r.astype(bf16).astype(f32)
    return h, m, (r - m).astype(bf16).astype(f32)


def iota(shape, dim):
    return lax.broadcasted_iota(i32, shape, dim)


def upper(n):
    return jnp.where(iota((n, n), 0) <= iota((n, n), 1), 1.0, 0.0).astype(bf16)


def slots(owner_rows, wanted_rows, ids, caps, oh_ref):
    count = len(owner_rows)
    width = owner_rows[0].shape[1]
    tri = upper(width)
    col = jnp.zeros((128, 2 * caps), f32)
    row = jnp.zeros((2 * caps, 128), f32)
    carry = jnp.zeros((128, 1), f32)
    for c in range(count):
        hit = jnp.where(owner_rows[c] == iota((128, width), 0), 1.0, 0.0)
        hit_b = hit.astype(bf16)
        cum = dot(hit_b, tri) + carry
        carry = cum[:, width - 1 : width]
        rank = jnp.sum(hit * cum, axis=0, keepdims=True).astype(i32) - 1
        place = jnp.where(rank == iota((caps, width), 0), 1.0, 0.0)
        vals = jnp.concatenate([place * (ids + 1.0), place * (wanted_rows[c] + 1.0)], axis=0).astype(bf16)
        col = col + dot_t(hit_b, vals)
        row = row + dot_t(vals, hit_b)
    return col, row, carry


def plan_kernel(me_ref, far_ref, mid_ref, near_ref, nl_ref, nm_ref, nt_ref, pts_ref, pay_ref, tab_ref, own_ref, hl_ref, hr_ref):
    me = me_ref[0]
    eye16 = jnp.where(iota((16, 16), 0) == iota((16, 16), 1), 1.0, 0.0).astype(bf16)

    def flip(x, n):
        return dot_t(eye16[:, :n] if n < 16 else eye16, x.astype(f32).astype(bf16))

    far = far_ref[...]
    own_t = flip(far >> 7, 16).astype(i32)
    want_t = flip(far & 127, 16)
    ids = iota((1, 128), 1).astype(f32)
    col, row, live = slots(
        [own_t[c : c + 1] for c in range(16)], [want_t[c : c + 1] for c in range(16)], ids, 16, None
    )
    mid = mid_ref[...]
    mown_t = flip(mid >> 4, 16).astype(i32)
    mwant_t = flip(mid & 15, 16)
    mids = iota((1, 16), 1).astype(f32)
    mcol, mrow, mlive = slots(
        [mown_t[c : c + 1] for c in range(16)], [mwant_t[c : c + 1] for c in range(16)], mids, 2, None
    )
    tab_ref[...] = jnp.zeros((32, 128), f32)
    tab_ref[0:16, :] = row[0:16]
    tab_ref[16:18, :] = mrow[0:2]
    lane = iota((1, 128), 1)
    scol = col[:, 0:16] - 1.0
    smid = mcol[:, 0:2] - 1.0
    oh = []
    lanef = lane.astype(f32)
    for g in range(8):
        a = jnp.where(scol[:, 2 * g : 2 * g + 1] == lanef, 1.0, 0.0)
        b = jnp.where(scol[:, 2 * g + 1 : 2 * g + 2] == lanef, 1.0, 0.0)
        oh.append(jnp.concatenate([a, b], axis=1).astype(bf16))
    oh = jnp.concatenate(oh, axis=0)
    la = jnp.where(smid[:, 0:1] == lanef[:, 0:16], 1.0, 0.0)
    lb = jnp.where(smid[:, 1:2] == lanef[:, 0:16], 1.0, 0.0)
    ohm = jnp.concatenate([la, lb], axis=1).astype(bf16)
    for c in range(3):
        x = nl_ref[c]
        z = jnp.zeros((128, 64), f32)
        big = jnp.concatenate([jnp.concatenate([x, z], axis=1), jnp.concatenate([z, x], axis=1)], axis=0)
        h, m, l = split3(big)
        res = dot(oh, h.astype(bf16)) + dot(oh, m.astype(bf16)) + dot(oh, l.astype(bf16))
        for g in range(8):
            pay_ref[pl.ds(c * 8 + g, 128, stride=32), :] = res[g * 128 : (g + 1) * 128]
        xm = nm_ref[c]
        zm = jnp.zeros((16, 64), f32)
        bigm = jnp.concatenate([jnp.concatenate([xm, zm], axis=1), jnp.concatenate([zm, xm], axis=1)], axis=0)
        h, m, l = split3(bigm)
        resm = dot(ohm, h.astype(bf16)) + dot(ohm, m.astype(bf16)) + dot(ohm, l.astype(bf16))
        pay_ref[pl.ds(24 + c, 128, stride=32), :] = resm
        nt = nt_ref[c]
        ntr = jnp.concatenate([nt[0:1], nt[1:2]], axis=1)
        pay_ref[pl.ds(28 + c, 128, stride=32), :] = jnp.broadcast_to(ntr, (128, 128))
    idrow = jnp.concatenate(
        [col[:, 16:32] - 1.0, mcol[:, 2:4] - 1.0, live, mlive, jnp.zeros((128, 108), f32)], axis=1
    )
    pay_ref[pl.ds(27, 128, stride=32), :] = idrow
    pay_ref[pl.ds(31, 128, stride=32), :] = jnp.zeros((128, 128), f32)
    near = near_ref[...]
    nown_t = flip(near >> 7, 6).astype(i32)
    nloc_t = flip(near & 127, 6)
    tri = upper(128)
    outs = []
    for d in (-1, 0, 1):
        hit = jnp.where((nown_t == me + d) & (nown_t >= 0), 1.0, 0.0)
        cum = dot(hit.astype(bf16), tri)
        base = jnp.zeros((1, 1), f32)
        acc = jnp.zeros((16, 128), f32)
        for c in range(6):
            pos = (cum[c : c + 1] + base).astype(i32) - 1
            base = base + cum[c : c + 1, 127:128]
            h = hit[c : c + 1]
            bm = jnp.where((pos & 127) == iota((128, 128), 0), h, 0.0).astype(bf16)
            am = jnp.where((pos >> 7) == iota((8, 128), 0), 1.0, 0.0)
            vals = jnp.concatenate([am * (ids + 1.0), am * nloc_t[c : c + 1]], axis=0).astype(bf16)
            acc = acc + dot_t(vals, bm)
        llist = jnp.where(iota((8, 128), 0) == 7, base, acc[0:8])
        outs.append((llist, acc[8:16]))
    own_ref[:, 0:128] = outs[1][0].astype(i32)
    own_ref[:, 128:256] = outs[1][1].astype(i32)
    for ref, k in ((hl_ref, 0), (hr_ref, 2)):
        for c in range(3):
            ref[c * 128 : (c + 1) * 128, :] = pts_ref[c]
        ref[384:392, 0:128] = outs[k][0]
        ref[384:392, 128:256] = outs[k][1]


def plan(me, far_leaf, far_mid, near_list, nodes_leaf, nodes_mid, nodes_top, points):
    vm = pl.BlockSpec(memory_space=pltpu.VMEM)
    return pl.pallas_call(
        plan_kernel,
        out_shape=(
            jax.ShapeDtypeStruct((128 * 32, 128), f32),
            jax.ShapeDtypeStruct((32, 128), f32),
            jax.ShapeDtypeStruct((8, 256), i32),
            jax.ShapeDtypeStruct((392, 256), f32),
            jax.ShapeDtypeStruct((392, 256), f32),
        ),
        in_specs=[pl.BlockSpec(memory_space=pltpu.SMEM)] + [vm] * 7,
        out_specs=(vm,) * 5,
        name="plan",
    )(me, far_leaf, far_mid, near_list, nodes_leaf, nodes_mid, nodes_top, points)


def tile_rows(x, y, z, a, b):
    r = iota((8, 256), 0)
    v = jnp.where(r == 0, x, jnp.where(r == 1, y, jnp.where(r == 2, z, jnp.where(r == 3, a, b))))
    return jnp.where(r < 5, v, 0.0)


def near_kernel(sets):
    def body(*refs):
        lists = refs[:sets]
        tgts = refs[sets : 2 * sets]
        pts_ref, q_ref = refs[2 * sets : 2 * sets + 2]
        outs = refs[2 * sets + 2 : 3 * sets + 2]
        sf_ref, qb_ref, acc_ref = refs[3 * sets + 2 :]

        def prepare(pair, carry):
            parts = []
            for par in range(2):
                n = pair * 2 + par
                x = pts_ref[0, pl.ds(n, 1), :]
                y = pts_ref[1, pl.ds(n, 1), :]
                z = pts_ref[2, pl.ds(n, 1), :]
                norm = x * x + y * y + z * z + soften
                h, m, l = split3(tile_rows(x, y, z, jnp.ones_like(x), norm))
                q = jnp.broadcast_to(q_ref[pl.ds(n, 1), :], (8, 256))
                parts += [h, m, l, h, m, h, q, jnp.zeros((8, 256), f32)]
            t = jnp.concatenate(parts, axis=0).T
            sf_ref[pair] = t.astype(bf16)
            for par in range(2):
                qb_ref[pair * 2 + par] = jnp.broadcast_to(t[:, 64 * par + 48 : 64 * par + 49], (256, 128))
            return carry

        lax.fori_loop(0, 64, prepare, 0)
        for s in range(sets):
            lst, tgt, out = lists[s], tgts[s], outs[s]
            acc_ref[...] = jnp.zeros((136, 256), f32)
            total = lst[7, 0]

            def one(i):
                lv = lst[i >> 7, i & 127]
                n = lst[i >> 7, 128 + (i & 127)]
                lrow = jnp.maximum(lv - 1, 0)
                orow = jnp.where(lv == 0, 128, lrow)
                x = tgt[pl.ds(lrow, 1), :]
                y = tgt[pl.ds(128 + lrow, 1), :]
                z = tgt[pl.ds(256 + lrow, 1), :]
                norm = x * x + y * y + z * z
                h, m, l = split3(tile_rows(-2.0 * x, -2.0 * y, -2.0 * z, norm, jnp.ones_like(x)))
                zero = jnp.zeros((16, 256), f32)
                tf = jnp.concatenate([h, h, h, m, m, l, zero], axis=0)
                odd = (n & 1) == 1
                rhs = jnp.concatenate([jnp.where(odd, 0.0, tf), jnp.where(odd, tf, 0.0)], axis=0).astype(bf16)
                sf = sf_ref.at[n >> 1]
                qb = qb_ref.at[n]
                acc = jnp.zeros((8, 256), f32)
                for j in range(0, 256, 64):
                    d = dot(sf[j : j + 64, :], rhs)
                    w = lax.rsqrt(d)
                    q = qb[j : j + 64, :]
                    wq = w * jnp.concatenate([q, q], axis=1)
                    acc = acc + jnp.sum(wq.reshape(8, 8, 256), axis=0)
                return orow, jnp.sum(acc, axis=0, keepdims=True)

            def step(it, carry):
                got = [one(it * NB + u) for u in range(NB)]
                for orow, val in got:
                    acc_ref[pl.ds(orow, 1), :] = acc_ref[pl.ds(orow, 1), :] + val
                return carry

            lax.fori_loop(0, (total + NB - 1) // NB, step, 0)
            out[...] = acc_ref[0:128, :]

    return body


def near(lists, targets, points, charges, name):
    sets = len(lists)
    vm = pl.BlockSpec(memory_space=pltpu.VMEM)
    return pl.pallas_call(
        near_kernel(sets),
        out_shape=tuple(jax.ShapeDtypeStruct((128, 256), f32) for _ in range(sets)),
        in_specs=[pl.BlockSpec(memory_space=pltpu.SMEM)] * sets + [vm] * (sets + 2),
        out_specs=tuple(vm for _ in range(sets)),
        scratch_shapes=[
            pltpu.VMEM((64, 256, 128), bf16),
            pltpu.VMEM((128, 256, 128), f32),
            pltpu.VMEM((136, 256), f32),
        ],
        compiler_params=pltpu.CompilerParams(vmem_limit_bytes=40 << 20),
        name=name,
    )(*lists, *targets, points, charges)


def far_kernel(ids_ref, r1_ref, nl_ref, nm_ref, lm_ref, mm_ref, top_ref, out_ref, v_ref, tab_ref):
    for grp in range(9):
        for c in range(3):
            src = nl_ref[c, grp * 16 : grp * 16 + 16, :] if grp < 8 else nm_ref[c]
            v_ref[pl.ds(grp * 128 + c, 16, stride=8), :] = src
        src = lm_ref[grp * 16 : grp * 16 + 16, :] if grp < 8 else mm_ref[...]
        v_ref[pl.ds(grp * 128 + 3, 16, stride=8), :] = src
        for c in range(4, 8):
            v_ref[pl.ds(grp * 128 + c, 16, stride=8), :] = jnp.zeros((16, 64), f32)

    def prepare(grp, carry):
        t = v_ref[pl.ds(grp * 128, 128), :].T
        for i in range(16):
            for c in range(4):
                tab_ref[grp * 16 + i, c] = jnp.broadcast_to(t[:, i * 8 + c : i * 8 + c + 1], (64, 128))
        return carry

    lax.fori_loop(0, 9, prepare, 0)
    low = iota((8, 128), 1) < 64

    def pair(t0, t1, x, y, z):
        a, b = tab_ref.at[jnp.maximum(t0, 0)], tab_ref.at[jnp.maximum(t1, 0)]
        x, y, z = (jnp.broadcast_to(v, (8, 128)) for v in (x, y, z))
        acc = jnp.zeros((8, 128), f32)
        for j in range(0, 64, 8):
            dx = jnp.where(low, a[0, j : j + 8, :], b[0, j : j + 8, :]) - x
            dy = jnp.where(low, a[1, j : j + 8, :], b[1, j : j + 8, :]) - y
            dz = jnp.where(low, a[2, j : j + 8, :], b[2, j : j + 8, :]) - z
            m = jnp.where(low, a[3, j : j + 8, :], b[3, j : j + 8, :])
            acc = acc + lax.rsqrt(dx * dx + dy * dy + dz * dz + soften) * m
        return jnp.sum(acc, axis=0, keepdims=True)

    out_ref[...] = jnp.zeros((128 * 16, 128), f32)
    out_ref[pl.ds(9, 128, stride=16), :] = jnp.broadcast_to(top_ref[...], (128, 128))

    def peer(p, carry):
        count = ids_ref[p, 18]

        def inner(g, c2):
            b = p * 32 + g
            out_ref[pl.ds(p * 16 + g, 1), :] = pair(
                ids_ref[p, 2 * g],
                ids_ref[p, 2 * g + 1],
                r1_ref[pl.ds(b, 1), :],
                r1_ref[pl.ds(b + 8, 1), :],
                r1_ref[pl.ds(b + 16, 1), :],
            )
            return c2

        lax.fori_loop(0, (count + 1) // 2, inner, 0)

        @pl.when(ids_ref[p, 19] > 0)
        def _():
            b = p * 32 + 24
            out_ref[pl.ds(p * 16 + 8, 1), :] = pair(
                128 + ids_ref[p, 16],
                128 + ids_ref[p, 17],
                r1_ref[pl.ds(b, 1), :],
                r1_ref[pl.ds(b + 1, 1), :],
                r1_ref[pl.ds(b + 2, 1), :],
            )

        return carry

    lax.fori_loop(0, 128, peer, 0)


def far(ids, r1, nodes_leaf, nodes_mid, leaf_moments, mid_moments, top_row):
    vm = pl.BlockSpec(memory_space=pltpu.VMEM)
    return pl.pallas_call(
        far_kernel,
        out_shape=jax.ShapeDtypeStruct((128 * 16, 128), f32),
        in_specs=[pl.BlockSpec(memory_space=pltpu.SMEM)] + [vm] * 6,
        out_specs=vm,
        scratch_shapes=[pltpu.VMEM((9 * 128, 64), f32), pltpu.VMEM((144, 4, 64, 128), f32)],
        compiler_params=pltpu.CompilerParams(vmem_limit_bytes=40 << 20),
        name="far",
    )(ids, r1, nodes_leaf, nodes_mid, leaf_moments, mid_moments, top_row)


def combine_kernel(top_ids, tab_ref, r1_ref, r2_ref, nt_ref, leaf_ref, mid_ref, top_out):
    acc = [jnp.zeros((128, 128), f32), jnp.zeros((128, 128), f32)]
    tag = (iota((128, 128), 0) + 1).astype(f32)
    for g in range(8):
        parts = [p.astype(bf16) for p in split3(r2_ref[pl.ds(g, 128, stride=16), :])]
        for h in range(2):
            oh = jnp.where(tab_ref[2 * g + h : 2 * g + h + 1, :] == tag, 1.0, 0.0).astype(bf16)
            acc[h] = acc[h] + (dot(oh, parts[0]) + dot(oh, parts[1]) + dot(oh, parts[2]))
    leaf_ref[...] = acc[0][:, 0:64] + acc[1][:, 64:128]
    parts = [p.astype(bf16) for p in split3(r2_ref[pl.ds(8, 128, stride=16), :])]
    res = []
    for h in range(2):
        oh = jnp.where(tab_ref[16 + h : 17 + h, :] == tag[0:16], 1.0, 0.0).astype(bf16)
        res.append(dot(oh, parts[0]) + dot(oh, parts[1]) + dot(oh, parts[2]))
    mid_ref[...] = res[0][:, 0:64] + res[1][:, 64:128]
    half = iota((1, 128), 1) >> 6
    pad = jnp.zeros((6, 64), f32)
    cols = [jnp.concatenate([nt_ref[c], pad], axis=0).T for c in range(3)]
    for g in range(2):
        tx, ty, tz = (jnp.broadcast_to(cols[c][:, g : g + 1], (64, 128)) for c in range(3))

        def entry(e, total):
            t = top_ids[g, e]
            p = jnp.maximum(t, 0) >> 1
            h = jnp.where(t < 0, 2, t & 1)
            m = jnp.where(half == h, r2_ref[pl.ds(p * 16 + 9, 1), :], 0.0)
            dx = tx - r1_ref[pl.ds(p * 32 + 28, 1), :]
            dy = ty - r1_ref[pl.ds(p * 32 + 29, 1), :]
            dz = tz - r1_ref[pl.ds(p * 32 + 30, 1), :]
            return total + lax.rsqrt(dx * dx + dy * dy + dz * dz + soften) * m

        total = lax.fori_loop(0, 16, entry, jnp.zeros((64, 128), f32))
        top_out[g * 64 : g * 64 + 64, :] = jnp.broadcast_to(jnp.sum(total, axis=1, keepdims=True), (64, 128))


def combine(far_top, tab, r1, r2, nodes_top):
    vm = pl.BlockSpec(memory_space=pltpu.VMEM)
    return pl.pallas_call(
        combine_kernel,
        out_shape=(
            jax.ShapeDtypeStruct((128, 64), f32),
            jax.ShapeDtypeStruct((16, 64), f32),
            jax.ShapeDtypeStruct((128, 128), f32),
        ),
        in_specs=[pl.BlockSpec(memory_space=pltpu.SMEM)] + [vm] * 4,
        out_specs=(vm,) * 3,
        name="combine",
    )(far_top, tab, r1, r2, nodes_top)


def swap(x):
    return lax.all_to_all(x, AXES, split_axis=0, concat_axis=0, tiled=True)


def local(
    charges,
    points,
    leaf_basis,
    child_transfer,
    parent_transfer,
    nodes_leaf,
    nodes_mid,
    nodes_top,
    near_list,
    far_leaf,
    far_mid,
    far_top,
):
    shards = lax.axis_size(AXES)
    me = lax.axis_index(AXES).astype(i32).reshape(1)
    down_perm = [(i + 1, i) for i in range(shards - 1)]
    up_perm = [(i, i + 1) for i in range(shards - 1)]
    pay, tab, own_list, to_left, to_right = plan(
        me, far_leaf, far_mid, near_list, nodes_leaf, nodes_mid, nodes_top, points
    )
    r1 = swap(pay.reshape(128, 32, 128))
    from_right = lax.ppermute(to_left, AXES, down_perm)
    from_left = lax.ppermute(to_right, AXES, up_perm)
    leaf_moments = jnp.sum(leaf_basis * charges[:, None, :], axis=2)
    mid_moments = jnp.sum(child_transfer * leaf_moments[:, None, :], axis=2).reshape(16, 8, 64).sum(axis=1)
    top_moments = jnp.sum(parent_transfer * mid_moments[:, None, :], axis=2).reshape(2, 8, 64).sum(axis=1)
    (near_own,) = near([own_list], [points.reshape(384, 256)], points, charges, "near_own")
    ids = r1[:, 27, :].astype(i32)
    r1 = r1.reshape(4096, 128)
    pay2 = far(ids, r1, nodes_leaf, nodes_mid, leaf_moments, mid_moments, top_moments.reshape(1, 128))
    r2 = swap(pay2.reshape(128, 16, 128)).reshape(2048, 128)
    near_l, near_r = near(
        [from_left[384:392].astype(i32), from_right[384:392].astype(i32)],
        [from_left, from_right],
        points,
        charges,
        "near_halo",
    )
    back = lax.ppermute(near_l, AXES, down_perm) + lax.ppermute(near_r, AXES, up_perm)
    leaf_local, mid_local, top_cols = combine(far_top, tab, r1, r2, nodes_top)
    top_local = top_cols[:, 0].reshape(2, 64)
    mid_down = mid_local + jnp.sum(parent_transfer * jnp.repeat(top_local, 8, axis=0)[:, :, None], axis=1)
    leaf_down = leaf_local + jnp.sum(child_transfer * jnp.repeat(mid_down, 8, axis=0)[:, :, None], axis=1)
    return jnp.sum(leaf_basis * leaf_down[:, :, None], axis=1) + near_own + back


def solution(mesh):
    placed = (
        P(AXES, None),
        P(None, AXES, None),
        P(AXES, None, None),
        P(AXES, None, None),
        P(AXES, None, None),
        P(None, AXES, None),
        P(None, AXES, None),
        P(None, AXES, None),
        P(AXES, None),
        P(AXES, None),
        P(AXES, None),
        P(AXES, None),
    )
    return jax.shard_map(local, mesh=mesh, in_specs=placed, out_specs=P(AXES, None), check_vma=False)
```

```python
import jax
import jax.numpy as jnp
from jax import lax
from jax.experimental import pallas as pl
from jax.experimental.pallas import tpu as pltpu
from jax.sharding import PartitionSpec as P


f32 = jnp.float32
bf16 = jnp.bfloat16
i32 = jnp.int32
soften = 0.25
AXES = ("dom", "sub")
NB = 4
TRANS = (((1,), (1,)), ((), ()))


def dot(a, b):
    return jnp.dot(a, b, preferred_element_type=f32)


def dot_t(a, b):
    return lax.dot_general(a, b, TRANS, preferred_element_type=f32)


def split3(v):
    h = v.astype(bf16).astype(f32)
    r = v - h
    m = r.astype(bf16).astype(f32)
    return h, m, (r - m).astype(bf16).astype(f32)


def iota(shape, dim):
    return lax.broadcasted_iota(i32, shape, dim)


def upper(n):
    return jnp.where(iota((n, n), 0) <= iota((n, n), 1), 1.0, 0.0).astype(bf16)


def slots(owner_rows, wanted_rows, ids, caps):
    width = owner_rows[0].shape[1]
    tri = upper(width)
    half = caps // 2
    r = iota((caps, width), 0)
    slot = jnp.where(r < half, 2 * r, 2 * (r - half) + 1)
    row = jnp.zeros((2 * caps, 128), f32)
    carry = jnp.zeros((128, 1), f32)
    for own, want in zip(owner_rows, wanted_rows):
        hit = jnp.where(own == iota((128, width), 0), 1.0, 0.0)
        hit_b = hit.astype(bf16)
        cum = dot(hit_b, tri) + carry
        carry = cum[:, width - 1 : width]
        rank = jnp.sum(hit * cum, axis=0, keepdims=True).astype(i32) - 1
        place = jnp.where(rank == slot, 1.0, 0.0)
        vals = jnp.concatenate([place * (ids + 1.0), place * (want + 1.0)], axis=0).astype(bf16)
        row = row + dot_t(vals, hit_b)
    return row, carry


def plan_kernel(
    me_ref, far_ref, mid_ref, near_ref, nl_ref, nm_ref, nt_ref, pts_ref, pay_ref, tab_ref, own_ref, hl_ref, hr_ref, oh_ref
):
    me = me_ref[0]
    lane = iota((1, 128), 1)
    ids = lane.astype(f32)
    far = far_ref[...]
    own = far >> 7
    want = (far & 127).astype(f32)
    row, live = slots([own[c : c + 1] for c in range(16)], [want[c : c + 1] for c in range(16)], ids, 16)
    eye = jnp.where(iota((16, 16), 0) == iota((16, 16), 1), 1.0, 0.0).astype(bf16)
    mid = mid_ref[...]
    mown = dot_t(eye, (mid >> 4).astype(f32).astype(bf16)).astype(i32)
    mwant = dot_t(eye, (mid & 15).astype(f32).astype(bf16))
    mrow, mlive = slots(
        [mown[c : c + 1] for c in range(16)], [mwant[c : c + 1] for c in range(16)], ids[:, 0:16], 2
    )
    col = jnp.concatenate([row, mrow, jnp.zeros((92, 128), f32)], axis=0).T
    mcol = col[:, 32:36]
    tab_ref[0:16, :] = row[0:16]
    tab_ref[16:18, :] = mrow[0:2]
    tab_ref[18:32, :] = jnp.zeros((14, 128), f32)
    even, odd = row[0:8], row[8:16]
    line = jnp.broadcast_to(ids + 1.0, (8, 128))
    for o in range(128):
        a = jnp.broadcast_to(even[:, o : o + 1], (8, 128))
        b = jnp.broadcast_to(odd[:, o : o + 1], (8, 128))
        oh_ref[o * 8 : o * 8 + 8, 0:128] = jnp.where(a == line, 1.0, 0.0)
        oh_ref[o * 8 : o * 8 + 8, 128:256] = jnp.where(b == line, 1.0, 0.0)
    oh = oh_ref[...].astype(bf16)
    z = jnp.zeros((64, 128), f32)
    blocks = []
    for c in range(3):
        x = nl_ref[c]
        big = jnp.concatenate([jnp.concatenate([x, z], axis=1), jnp.concatenate([z, x], axis=1)], axis=0)
        blocks += [v.astype(bf16) for v in split3(big)]
    for c in range(3):
        h, m, l = blocks[3 * c : 3 * c + 3]
        both = dot_t(oh, jnp.concatenate([h, m], axis=0))
        pay_ref[:, c * 8 : c * 8 + 8, :] = (both[:, 0:128] + both[:, 128:256]).reshape(128, 8, 128)
    both = dot_t(oh, jnp.concatenate([blocks[2], blocks[5]], axis=0))
    pay_ref[:, 0:8, :] = pay_ref[:, 0:8, :] + both[:, 0:128].reshape(128, 8, 128)
    pay_ref[:, 8:16, :] = pay_ref[:, 8:16, :] + both[:, 128:256].reshape(128, 8, 128)
    pay_ref[:, 16:24, :] = pay_ref[:, 16:24, :] + dot_t(oh, blocks[8]).reshape(128, 8, 128)
    tops = [jnp.concatenate([nt_ref[c, 0:1], nt_ref[c, 1:2]], axis=1) for c in range(3)]
    zero = jnp.zeros((1, 128), f32)
    last = jnp.concatenate([zero] * 4 + tops + [zero], axis=0)
    pay_ref[:, 24:32, :] = jnp.broadcast_to(last[None], (128, 8, 128))
    la = jnp.where(mcol[:, 0:1] == ids[:, 0:16] + 1.0, 1.0, 0.0)
    lb = jnp.where(mcol[:, 1:2] == ids[:, 0:16] + 1.0, 1.0, 0.0)
    ohm = jnp.concatenate([la, lb], axis=1).astype(bf16)
    for c in range(3):
        xm = nm_ref[c]
        zm = jnp.zeros((16, 64), f32)
        bigm = jnp.concatenate([jnp.concatenate([xm, zm], axis=1), jnp.concatenate([zm, xm], axis=1)], axis=0)
        h, m, l = split3(bigm)
        resm = dot(ohm, h.astype(bf16)) + dot(ohm, m.astype(bf16)) + dot(ohm, l.astype(bf16))
        pay_ref[:, 24 + c : 25 + c, :] = resm[:, None, :]
    idrow = jnp.concatenate(
        [col[:, 16:32] - 1.0, mcol[:, 2:4] - 1.0, live, mlive, jnp.zeros((128, 108), f32)], axis=1
    )
    pay_ref[:, 27:28, :] = idrow[:, None, :]
    near = near_ref[...]
    nown = near >> 7
    nloc = (near & 127).astype(f32)
    tri = upper(128)
    outs = []
    for d in (-1, 0, 1):
        hit = jnp.where((nown == me + d) & (near >= 0), 1.0, 0.0)
        cum = dot(hit.astype(bf16), tri)
        base = jnp.zeros((1, 1), f32)
        acc = jnp.zeros((16, 128), f32)
        for c in range(6):
            pos = (cum[c : c + 1] + base).astype(i32) - 1
            base = base + cum[c : c + 1, 127:128]
            bm = jnp.where((pos & 127) == iota((128, 128), 0), hit[c : c + 1], 0.0).astype(bf16)
            am = jnp.where((pos >> 7) == iota((8, 128), 0), 1.0, 0.0)
            vals = jnp.concatenate([am * (ids + 1.0), am * nloc[c : c + 1]], axis=0).astype(bf16)
            acc = acc + dot_t(vals, bm)
        outs.append((jnp.where(iota((8, 128), 0) == 7, base, acc[0:8]), acc[8:16]))
    own_ref[:, 0:128] = outs[1][0].astype(i32)
    own_ref[:, 128:256] = outs[1][1].astype(i32)
    for ref, k in ((hl_ref, 0), (hr_ref, 2)):
        for c in range(3):
            ref[c * 128 : (c + 1) * 128, :] = pts_ref[c]
        ref[384:392, 0:128] = outs[k][0]
        ref[384:392, 128:256] = outs[k][1]


def plan(me, far_t, far_mid, near_t, nodes_t, nodes_mid, nodes_top, points):
    vm = pl.BlockSpec(memory_space=pltpu.VMEM)
    return pl.pallas_call(
        plan_kernel,
        out_shape=(
            jax.ShapeDtypeStruct((128, 32, 128), f32),
            jax.ShapeDtypeStruct((32, 128), f32),
            jax.ShapeDtypeStruct((8, 256), i32),
            jax.ShapeDtypeStruct((392, 256), f32),
            jax.ShapeDtypeStruct((392, 256), f32),
        ),
        in_specs=[pl.BlockSpec(memory_space=pltpu.SMEM)] + [vm] * 7,
        out_specs=(vm,) * 5,
        scratch_shapes=[pltpu.VMEM((1024, 256), f32)],
        name="plan",
    )(me, far_t, far_mid, near_t, nodes_t, nodes_mid, nodes_top, points)


def tile_rows(x, y, z, a, b):
    r = iota((8, 256), 0)
    v = jnp.where(r == 0, x, jnp.where(r == 1, y, jnp.where(r == 2, z, jnp.where(r == 3, a, b))))
    return jnp.where(r < 5, v, 0.0)


def near_tables(pts_ref, q_ref, sf_ref, qb_ref):
    r = iota((64, 128), 0)
    spread = jnp.where((r >= 48) & (r < 51), 1.0, 0.0).astype(bf16)
    r8 = iota((8, 256), 0)

    def prepare(it, carry):
        for u in range(8):
            n = it * 8 + u
            x = pts_ref[pl.ds(n, 1), :]
            y = pts_ref[pl.ds(128 + n, 1), :]
            z = pts_ref[pl.ds(256 + n, 1), :]
            norm = x * x + y * y + z * z + soften
            h, m, l = split3(tile_rows(x, y, z, jnp.ones_like(x), norm))
            qh, qm, ql = split3(jnp.broadcast_to(q_ref[pl.ds(n, 1), :], (8, 256)))
            q = jnp.where(r8 == 0, qh, jnp.where(r8 == 1, qm, jnp.where(r8 == 2, ql, 0.0)))
            t = jnp.concatenate([h, m, l, h, m, h, q, jnp.zeros_like(q)], axis=0).T.astype(bf16)
            sf_ref[n] = t
            qb_ref[n] = dot(t, spread)
        return carry

    lax.fori_loop(0, 16, prepare, 0)


def near_pairs(lst, base, tgt, sf_ref, qb_ref, d_refs, acc_ref):
    def entry(i):
        return lst[base + i], lst[base + 1024 + i]

    def distances(i, u, ref):
        lv, n = entry(i)
        lrow = jnp.maximum(lv - 1, 0)
        x = tgt[pl.ds(lrow, 1), :]
        y = tgt[pl.ds(128 + lrow, 1), :]
        z = tgt[pl.ds(256 + lrow, 1), :]
        norm = x * x + y * y + z * z
        h, m, l = split3(tile_rows(-2.0 * x, -2.0 * y, -2.0 * z, norm, jnp.ones_like(x)))
        rhs = jnp.concatenate([h, h, h, m, m, l], axis=0).astype(bf16)
        ref[u] = dot(sf_ref[n, :, 0:48], rhs)

    def sums(i, u, ref):
        lv, n = entry(i)
        acc = jnp.zeros((8, 256), f32)
        for j in range(0, 256, 64):
            w = lax.rsqrt(ref[u, j : j + 64, :])
            q = qb_ref[n, j : j + 64, :]
            acc = acc + jnp.sum((w * jnp.concatenate([q, q], axis=1)).reshape(8, 8, 256), axis=0)
        row = jnp.where(lv > 0, lv - 1, 128)
        acc_ref[pl.ds(row, 1), :] = acc_ref[pl.ds(row, 1), :] + jnp.sum(acc, axis=0, keepdims=True)

    d0, d1 = d_refs
    for u in range(NB):
        distances(u, u, d0)

    def step(it, carry):
        i = it * (2 * NB)
        for u in range(NB):
            distances(i + NB + u, u, d1)
        for u in range(NB):
            sums(i + u, u, d0)
        for u in range(NB):
            distances(i + 2 * NB + u, u, d0)
        for u in range(NB):
            sums(i + NB + u, u, d1)
        return carry

    lax.fori_loop(0, (lst[base + 896] + 2 * NB - 1) // (2 * NB), step, 0)


def near_kernel(lst, tgt_l, tgt_r, pts_ref, q_ref, out_own, out_l, out_r, sf_ref, qb_ref, d0_ref, d1_ref, acc_ref):
    near_tables(pts_ref, q_ref, sf_ref, qb_ref)
    for k, (tgt, out) in enumerate(((pts_ref, out_own), (tgt_l, out_l), (tgt_r, out_r))):
        acc_ref[...] = jnp.zeros((136, 256), f32)
        near_pairs(lst, k * 2048, tgt, sf_ref, qb_ref, (d0_ref, d1_ref), acc_ref)
        out[...] = acc_ref[0:128, :]


def near(lists, arrays):
    vm = pl.BlockSpec(memory_space=pltpu.VMEM)
    return pl.pallas_call(
        near_kernel,
        out_shape=tuple(jax.ShapeDtypeStruct((128, 256), f32) for _ in range(3)),
        in_specs=[pl.BlockSpec(memory_space=pltpu.SMEM)] + [vm] * 4,
        out_specs=(vm,) * 3,
        scratch_shapes=[
            pltpu.VMEM((128, 256, 64), bf16),
            pltpu.VMEM((128, 256, 128), f32),
            pltpu.VMEM((NB, 256, 256), f32),
            pltpu.VMEM((NB, 256, 256), f32),
            pltpu.VMEM((136, 256), f32),
        ],
        compiler_params=pltpu.CompilerParams(vmem_limit_bytes=40 << 20),
        name="near",
    )(lists, *arrays)


def halves(x):
    h = x.astype(bf16).astype(f32)
    return h, (x - h).astype(bf16).astype(f32)


def features(x, y, z, source):
    parts = [halves(v) for v in (x, y, z)]
    norm = sum((h + m) * (h + m) for h, m in parts)
    one = jnp.ones_like(x)
    if source:
        nh, nm = halves(norm + soften)
        return [v for h, m in parts for v in (h, m, h, m)] + [one, one, nh, nm]
    nh, nm = halves(norm)
    return [v for h, m in parts for v in (-2.0 * h, -2.0 * h, -2.0 * m, -2.0 * m)] + [nh, nm, one, one]


def far_kernel(
    ids_ref, r1_ref, nl_ref, nm_ref, lm_ref, mm_ref, top_ref, out_ref, v_ref, u_ref, rep_ref, one_ref, mask_ref, ra_ref, mb_ref
):
    for c in range(8):
        r = iota((128, 128), 0) - c * 16
        k = iota((128, 128), 1)
        rep_ref[c] = jnp.where(r == (k >> 3), 1.0, 0.0).astype(bf16)
        one_ref[c] = jnp.where((r >= 0) & (r < 3), 1.0, 0.0).astype(bf16)
        mask_ref[c] = jnp.where((iota((64, 128), 1) & 7) == c, 1.0, 0.0).astype(bf16)
    u_ref[...] = jnp.zeros((18 * 128, 64), f32)
    leaf = features(nl_ref[0].T, nl_ref[1].T, nl_ref[2].T, True)
    mid = features(nm_ref[0], nm_ref[1], nm_ref[2], True)
    for f in range(16):
        for blk in range(16):
            v_ref[pl.ds(blk * 128 + f, 8, stride=16), :] = leaf[f][blk * 8 : blk * 8 + 8]
        for blk in range(2):
            v_ref[pl.ds((16 + blk) * 128 + f, 8, stride=16), :] = mid[f][blk * 8 : blk * 8 + 8]

    for blk in range(18):
        src = lm_ref[blk * 8 : blk * 8 + 8, :] if blk < 16 else mm_ref[blk * 8 - 128 : blk * 8 - 120, :]
        for f, v in enumerate(split3(src)):
            u_ref[pl.ds(blk * 128 + f, 8, stride=16), :] = v

    def prepare(blk, carry):
        rows = pl.ds(pl.multiple_of(blk * 128, 128), 128)
        t = v_ref[rows, :].T.astype(bf16)
        u = u_ref[rows, :].T.astype(bf16)
        for i in range(8):
            ra_ref[blk * 8 + i] = dot(t, rep_ref[i]).astype(bf16)
            mb_ref[blk * 8 + i] = dot(u, one_ref[i])
        return carry

    lax.fori_loop(0, 18, prepare, 0)
    low = iota((128, 128), 1) < 64
    low64 = iota((64, 128), 1) < 64

    def weights(x, y, z):
        tf = jnp.concatenate(features(x, y, z, False), axis=0)
        return jnp.concatenate([jnp.where(low, tf, 0.0), jnp.where(low, 0.0, tf)], axis=0).astype(bf16)

    def group(rhs, g, t0, t1):
        t0 = jnp.maximum(t0, 0)
        t1 = jnp.maximum(t1, 0)
        mask = mask_ref[g]
        lhs = jnp.concatenate([ra_ref[t0] * mask, ra_ref[t1] * mask], axis=1)
        m = jnp.where(low64, mb_ref[t0], mb_ref[t1])
        w = lax.rsqrt(dot(lhs, rhs)) * m
        return jnp.sum(jnp.sum(w.reshape(8, 8, 128), axis=0), axis=0, keepdims=True)

    def leaf_groups(p, groups):
        rhs = weights(*(r1_ref[pl.ds(pl.multiple_of(p * 32 + 8 * c, 8), 8), :] for c in range(3)))
        return [(p, g, group(rhs, g, ids_ref[p, g], ids_ref[p, 8 + g])) for g in groups]

    out_ref[...] = jnp.zeros((128 * 16, 128), f32)
    out_ref[pl.ds(9, 128, stride=16), :] = jnp.broadcast_to(top_ref[...], (128, 128))

    def first(it, carry):
        got = []
        for u in range(4):
            got += leaf_groups(it * 4 + u, range(4))
        for p, g, val in got:
            out_ref[pl.ds(p * 16 + g, 1), :] = val
        return carry

    lax.fori_loop(0, 32, first, 0)

    def second(p, carry):
        @pl.when(ids_ref[p, 18] > 8)
        def _():
            for q, g, val in leaf_groups(p, range(4, 8)):
                out_ref[pl.ds(q * 16 + g, 1), :] = val

        return carry

    lax.fori_loop(0, 128, second, 0)

    def mids(it, carry):
        got = []
        for u in range(2):
            b = (it * 2 + u) * 256 + 24
            rhs = weights(*(r1_ref[pl.ds(b + c, 8, stride=32), :] for c in range(3)))
            for g in range(8):
                p = (it * 2 + u) * 8 + g
                got.append((p, group(rhs, g, 128 + ids_ref[p, 16], 128 + ids_ref[p, 17])))
        for p, val in got:
            out_ref[pl.ds(p * 16 + 8, 1), :] = val
        return carry

    lax.fori_loop(0, 8, mids, 0)


def far(ids, r1, nodes_t, nodes_mid, moments, mid_moments, top_row):
    vm = pl.BlockSpec(memory_space=pltpu.VMEM)
    return pl.pallas_call(
        far_kernel,
        out_shape=jax.ShapeDtypeStruct((128 * 16, 128), f32),
        in_specs=[pl.BlockSpec(memory_space=pltpu.SMEM)] + [vm] * 6,
        out_specs=vm,
        scratch_shapes=[
            pltpu.VMEM((18 * 128, 64), f32),
            pltpu.VMEM((18 * 128, 64), f32),
            pltpu.VMEM((8, 128, 128), bf16),
            pltpu.VMEM((8, 128, 128), bf16),
            pltpu.VMEM((8, 64, 128), bf16),
            pltpu.VMEM((144, 64, 128), bf16),
            pltpu.VMEM((144, 64, 128), f32),
        ],
        compiler_params=pltpu.CompilerParams(vmem_limit_bytes=40 << 20),
        name="far",
    )(ids, r1, nodes_t, nodes_mid, moments, mid_moments, top_row)


def combine_kernel(top_ids, tab_ref, r1_ref, r2_ref, nt_ref, leaf_ref, mid_ref, top_out):
    acc = [jnp.zeros((128, 128), f32), jnp.zeros((128, 128), f32)]
    tag = (iota((128, 128), 0) + 1).astype(f32)
    for g in range(8):
        parts = [p.astype(bf16) for p in split3(r2_ref[pl.ds(g, 128, stride=16), :])]
        for h in range(2):
            oh = jnp.where(tab_ref[8 * h + g : 8 * h + g + 1, :] == tag, 1.0, 0.0).astype(bf16)
            acc[h] = acc[h] + (dot(oh, parts[0]) + dot(oh, parts[1]) + dot(oh, parts[2]))
    leaf_ref[...] = acc[0][:, 0:64] + acc[1][:, 64:128]
    parts = [p.astype(bf16) for p in split3(r2_ref[pl.ds(8, 128, stride=16), :])]
    res = []
    for h in range(2):
        oh = jnp.where(tab_ref[16 + h : 17 + h, :] == tag[0:16], 1.0, 0.0).astype(bf16)
        res.append(dot(oh, parts[0]) + dot(oh, parts[1]) + dot(oh, parts[2]))
    mid_ref[...] = res[0][:, 0:64] + res[1][:, 64:128]
    half = iota((1, 128), 1) >> 6
    pad = jnp.zeros((6, 64), f32)
    cols = [jnp.concatenate([nt_ref[c], pad], axis=0).T for c in range(3)]
    for g in range(2):
        tx, ty, tz = (jnp.broadcast_to(cols[c][:, g : g + 1], (64, 128)) for c in range(3))

        def entry(e, total):
            t = top_ids[g, e]
            p = jnp.maximum(t, 0) >> 1
            h = jnp.where(t < 0, 2, t & 1)
            m = jnp.where(half == h, r2_ref[pl.ds(p * 16 + 9, 1), :], 0.0)
            dx = tx - r1_ref[pl.ds(p * 32 + 28, 1), :]
            dy = ty - r1_ref[pl.ds(p * 32 + 29, 1), :]
            dz = tz - r1_ref[pl.ds(p * 32 + 30, 1), :]
            return total + lax.rsqrt(dx * dx + dy * dy + dz * dz + soften) * m

        total = lax.fori_loop(0, 16, entry, jnp.zeros((64, 128), f32))
        top_out[g * 64 : g * 64 + 64, :] = jnp.broadcast_to(jnp.sum(total, axis=1, keepdims=True), (64, 128))


def combine(far_top, tab, r1, r2, nodes_top):
    vm = pl.BlockSpec(memory_space=pltpu.VMEM)
    return pl.pallas_call(
        combine_kernel,
        out_shape=(
            jax.ShapeDtypeStruct((128, 64), f32),
            jax.ShapeDtypeStruct((16, 64), f32),
            jax.ShapeDtypeStruct((128, 128), f32),
        ),
        in_specs=[pl.BlockSpec(memory_space=pltpu.SMEM)] + [vm] * 4,
        out_specs=(vm,) * 3,
        name="combine",
    )(far_top, tab, r1, r2, nodes_top)


def swap(x):
    return lax.all_to_all(x, AXES, split_axis=0, concat_axis=0, tiled=True)


def local(
    charges,
    points,
    leaf_basis,
    child_transfer,
    parent_transfer,
    nodes_leaf,
    nodes_mid,
    nodes_top,
    near_list,
    far_leaf,
    far_mid,
    far_top,
):
    shards = lax.axis_size(AXES)
    me = lax.axis_index(AXES).astype(i32).reshape(1)
    down_perm = [(i + 1, i) for i in range(shards - 1)]
    up_perm = [(i, i + 1) for i in range(shards - 1)]
    nodes_t = jnp.transpose(nodes_leaf, (0, 2, 1))
    pay, tab, own_list, to_left, to_right = plan(
        me, far_leaf.T, far_mid, near_list.T, nodes_t, nodes_mid, nodes_top, points
    )
    from_right = lax.ppermute(to_left, AXES, down_perm)
    from_left = lax.ppermute(to_right, AXES, up_perm)
    r1 = swap(pay)
    leaf_moments = jnp.sum(leaf_basis * charges[:, None, :], axis=2)
    mid_moments = jnp.sum(child_transfer * leaf_moments[:, None, :], axis=2).reshape(16, 8, 64).sum(axis=1)
    top_moments = jnp.sum(parent_transfer * mid_moments[:, None, :], axis=2).reshape(2, 8, 64).sum(axis=1)
    lists = jnp.stack([own_list, from_left[384:392].astype(i32), from_right[384:392].astype(i32)])
    lists = jnp.transpose(lists.reshape(3, 8, 2, 128), (0, 2, 1, 3)).reshape(6144)
    flat = points.reshape(384, 256)
    near_own, near_l, near_r = near(lists, [from_left, from_right, flat, charges])
    back_l = lax.ppermute(near_l, AXES, down_perm)
    back_r = lax.ppermute(near_r, AXES, up_perm)
    r1, near_own, leaf_moments, mid_moments, top_moments = lax.optimization_barrier(
        (r1, near_own, leaf_moments, mid_moments, top_moments)
    )
    ids = r1[:, 27, :].astype(i32)
    r1 = r1.reshape(4096, 128)
    pay2 = far(ids, r1, nodes_t, nodes_mid, leaf_moments, mid_moments, top_moments.reshape(1, 128))
    r2 = swap(pay2.reshape(128, 16, 128)).reshape(2048, 128)
    back = back_l + back_r
    leaf_local, mid_local, top_cols = combine(far_top, tab, r1, r2, nodes_top)
    top_local = top_cols[:, 0].reshape(2, 64)
    mid_down = mid_local + jnp.sum(parent_transfer * jnp.repeat(top_local, 8, axis=0)[:, :, None], axis=1)
    leaf_down = leaf_local + jnp.sum(child_transfer * jnp.repeat(mid_down, 8, axis=0)[:, :, None], axis=1)
    return jnp.sum(leaf_basis * leaf_down[:, :, None], axis=1) + near_own + back


def solution(mesh):
    placed = (
        P(AXES, None),
        P(None, AXES, None),
        P(AXES, None, None),
        P(AXES, None, None),
        P(AXES, None, None),
        P(None, AXES, None),
        P(None, AXES, None),
        P(None, AXES, None),
        P(AXES, None),
        P(AXES, None),
        P(AXES, None),
        P(AXES, None),
    )
    return jax.shard_map(local, mesh=mesh, in_specs=placed, out_specs=P(AXES, None), check_vma=False)
```

```python
import jax
import jax.numpy as jnp
from jax import lax
from jax.experimental import pallas as pl
from jax.experimental.pallas import tpu as pltpu
from jax.sharding import PartitionSpec as P


f32 = jnp.float32
bf16 = jnp.bfloat16
i32 = jnp.int32
soften = 0.25
AXES = ("dom", "sub")
NB = 8
TRANS = (((1,), (1,)), ((), ()))


def dot(a, b):
    return jnp.dot(a, b, preferred_element_type=f32)


def dot_t(a, b):
    return lax.dot_general(a, b, TRANS, preferred_element_type=f32)


def split3(v):
    h = v.astype(bf16).astype(f32)
    r = v - h
    m = r.astype(bf16).astype(f32)
    return h, m, (r - m).astype(bf16).astype(f32)


def iota(shape, dim):
    return lax.broadcasted_iota(i32, shape, dim)


def upper(n):
    return jnp.where(iota((n, n), 0) <= iota((n, n), 1), 1.0, 0.0).astype(bf16)


def slots(owner_rows, wanted_rows, ids, caps):
    width = owner_rows[0].shape[1]
    tri = upper(width)
    half = caps // 2
    r = iota((caps, width), 0)
    slot = jnp.where(r < half, 2 * r, 2 * (r - half) + 1)
    row = jnp.zeros((2 * caps, 128), f32)
    carry = jnp.zeros((128, 1), f32)
    for own, want in zip(owner_rows, wanted_rows):
        hit = jnp.where(own == iota((128, width), 0), 1.0, 0.0)
        hit_b = hit.astype(bf16)
        cum = dot(hit_b, tri) + carry
        carry = cum[:, width - 1 : width]
        rank = jnp.sum(hit * cum, axis=0, keepdims=True).astype(i32) - 1
        place = jnp.where(rank == slot, 1.0, 0.0)
        vals = jnp.concatenate([place * (ids + 1.0), place * (want + 1.0)], axis=0).astype(bf16)
        row = row + dot_t(vals, hit_b)
    return row, carry


def plan_kernel(
    me_ref, far_ref, mid_ref, near_ref, nl_ref, nm_ref, nt_ref, pts_ref, pay_ref, tab_ref, own_ref, hl_ref, hr_ref, oh_ref
):
    me = me_ref[0]
    lane = iota((1, 128), 1)
    ids = lane.astype(f32)
    far = far_ref[...]
    own = far >> 7
    want = (far & 127).astype(f32)
    row, live = slots([own[c : c + 1] for c in range(16)], [want[c : c + 1] for c in range(16)], ids, 16)
    eye = jnp.where(iota((16, 16), 0) == iota((16, 16), 1), 1.0, 0.0).astype(bf16)
    mid = mid_ref[...]
    mown = dot_t(eye, (mid >> 4).astype(f32).astype(bf16)).astype(i32)
    mwant = dot_t(eye, (mid & 15).astype(f32).astype(bf16))
    mrow, mlive = slots(
        [mown[c : c + 1] for c in range(16)], [mwant[c : c + 1] for c in range(16)], ids[:, 0:16], 2
    )
    col = jnp.concatenate([row, mrow, jnp.zeros((92, 128), f32)], axis=0).T
    mcol = col[:, 32:36]
    tab_ref[0:16, :] = row[0:16]
    tab_ref[16:18, :] = mrow[0:2]
    tab_ref[18:32, :] = jnp.zeros((14, 128), f32)
    even, odd = row[0:8], row[8:16]
    line = jnp.broadcast_to(ids + 1.0, (8, 128))
    for o in range(128):
        a = jnp.broadcast_to(even[:, o : o + 1], (8, 128))
        b = jnp.broadcast_to(odd[:, o : o + 1], (8, 128))
        oh_ref[o * 8 : o * 8 + 8, 0:128] = jnp.where(a == line, 1.0, 0.0)
        oh_ref[o * 8 : o * 8 + 8, 128:256] = jnp.where(b == line, 1.0, 0.0)
    oh = oh_ref[...].astype(bf16)
    z = jnp.zeros((64, 128), f32)
    blocks = []
    for c in range(3):
        x = nl_ref[c]
        big = jnp.concatenate([jnp.concatenate([x, z], axis=1), jnp.concatenate([z, x], axis=1)], axis=0)
        blocks += [v.astype(bf16) for v in split3(big)]
    for c in range(3):
        h, m, l = blocks[3 * c : 3 * c + 3]
        both = dot_t(oh, jnp.concatenate([h, m], axis=0))
        pay_ref[:, c * 8 : c * 8 + 8, :] = (both[:, 0:128] + both[:, 128:256]).reshape(128, 8, 128)
    both = dot_t(oh, jnp.concatenate([blocks[2], blocks[5]], axis=0))
    pay_ref[:, 0:8, :] = pay_ref[:, 0:8, :] + both[:, 0:128].reshape(128, 8, 128)
    pay_ref[:, 8:16, :] = pay_ref[:, 8:16, :] + both[:, 128:256].reshape(128, 8, 128)
    pay_ref[:, 16:24, :] = pay_ref[:, 16:24, :] + dot_t(oh, blocks[8]).reshape(128, 8, 128)
    tops = [jnp.concatenate([nt_ref[c, 0:1], nt_ref[c, 1:2]], axis=1) for c in range(3)]
    zero = jnp.zeros((1, 128), f32)
    last = jnp.concatenate([zero] * 4 + tops + [zero], axis=0)
    pay_ref[:, 24:32, :] = jnp.broadcast_to(last[None], (128, 8, 128))
    la = jnp.where(mcol[:, 0:1] == ids[:, 0:16] + 1.0, 1.0, 0.0)
    lb = jnp.where(mcol[:, 1:2] == ids[:, 0:16] + 1.0, 1.0, 0.0)
    ohm = jnp.concatenate([la, lb], axis=1).astype(bf16)
    for c in range(3):
        xm = nm_ref[c]
        zm = jnp.zeros((16, 64), f32)
        bigm = jnp.concatenate([jnp.concatenate([xm, zm], axis=1), jnp.concatenate([zm, xm], axis=1)], axis=0)
        h, m, l = split3(bigm)
        resm = dot(ohm, h.astype(bf16)) + dot(ohm, m.astype(bf16)) + dot(ohm, l.astype(bf16))
        pay_ref[:, 24 + c : 25 + c, :] = resm[:, None, :]
    idrow = jnp.concatenate(
        [col[:, 16:32] - 1.0, mcol[:, 2:4] - 1.0, live, mlive, jnp.zeros((128, 108), f32)], axis=1
    )
    pay_ref[:, 27:28, :] = idrow[:, None, :]
    near = near_ref[...]
    nown = near >> 7
    nloc = (near & 127).astype(f32)
    tri = upper(128)
    outs = []
    for d in (-1, 0, 1):
        hit = jnp.where((nown == me + d) & (near >= 0), 1.0, 0.0)
        cum = dot(hit.astype(bf16), tri)
        base = jnp.zeros((1, 1), f32)
        acc = jnp.zeros((16, 128), f32)
        for c in range(6):
            pos = (cum[c : c + 1] + base).astype(i32) - 1
            base = base + cum[c : c + 1, 127:128]
            bm = jnp.where((pos & 127) == iota((128, 128), 0), hit[c : c + 1], 0.0).astype(bf16)
            am = jnp.where((pos >> 7) == iota((8, 128), 0), 1.0, 0.0)
            vals = jnp.concatenate([am * (ids + 1.0), am * nloc[c : c + 1]], axis=0).astype(bf16)
            acc = acc + dot_t(vals, bm)
        outs.append((jnp.where(iota((8, 128), 0) == 7, base, acc[0:8]), acc[8:16]))
    own_ref[:, 0:128] = outs[1][0].astype(i32)
    own_ref[:, 128:256] = outs[1][1].astype(i32)
    for ref, k in ((hl_ref, 0), (hr_ref, 2)):
        for c in range(3):
            ref[c * 128 : (c + 1) * 128, :] = pts_ref[c]
        ref[384:392, 0:128] = outs[k][0]
        ref[384:392, 128:256] = outs[k][1]


def plan(me, far_t, far_mid, near_t, nodes_t, nodes_mid, nodes_top, points):
    vm = pl.BlockSpec(memory_space=pltpu.VMEM)
    return pl.pallas_call(
        plan_kernel,
        out_shape=(
            jax.ShapeDtypeStruct((128, 32, 128), f32),
            jax.ShapeDtypeStruct((32, 128), f32),
            jax.ShapeDtypeStruct((8, 256), i32),
            jax.ShapeDtypeStruct((392, 256), f32),
            jax.ShapeDtypeStruct((392, 256), f32),
        ),
        in_specs=[pl.BlockSpec(memory_space=pltpu.SMEM)] + [vm] * 7,
        out_specs=(vm,) * 5,
        scratch_shapes=[pltpu.VMEM((1024, 256), f32)],
        compiler_params=pltpu.CompilerParams(vmem_limit_bytes=60 << 20),
        name="plan",
    )(me, far_t, far_mid, near_t, nodes_t, nodes_mid, nodes_top, points)


def dot3(a, b):
    return sum(dot(v.astype(bf16), b) for v in split3(a))


def moments_kernel(q_ref, lb_hbm, ct_hbm, pt_ref, lm_ref, mm_ref, top_ref, lb_ref, ct_ref, sem):
    def part(k):
        rows = pl.ds(k * 16, 16)
        return pltpu.make_async_copy(lb_hbm.at[rows], lb_ref.at[rows], sem.at[k])

    child = pltpu.make_async_copy(ct_hbm, ct_ref, sem.at[8])
    for k in range(8):
        part(k).start()
    child.start()
    lane = iota((64, 128), 1)
    lmt = jnp.zeros((64, 128), f32)
    for k in range(8):
        part(k).wait()

        def leaf(it, acc):
            for u in range(4):
                n = k * 16 + it * 4 + u
                prod = lb_ref[n] * q_ref[pl.ds(n, 1), :]
                col = jnp.sum(prod[:, 0:128] + prod[:, 128:256], axis=1, keepdims=True)
                acc = jnp.where(lane == n, col, acc)
            return acc

        lmt = lax.fori_loop(0, 4, leaf, lmt)
    lm_ref[...] = lmt.T
    child.wait()
    rows = []
    for i in range(64):
        rows.append(jnp.sum(ct_ref[i] * lmt, axis=0, keepdims=True))
    per_leaf = jnp.concatenate(rows, axis=0)
    group = jnp.where((iota((128, 128), 0) >> 3) == iota((128, 128), 1), 1.0, 0.0).astype(bf16)
    mm = dot3(per_leaf, group).T
    mm_ref[...] = mm[0:16, :]
    tops = []
    for g in range(2):
        acc = jnp.zeros((64, 64), f32)
        for c in range(g * 8, g * 8 + 8):
            acc = acc + pt_ref[c] * mm[c : c + 1, :]
        tops.append(jnp.broadcast_to(jnp.sum(acc, axis=1, keepdims=True), (64, 128)).T[0:1])
    top_ref[...] = jnp.concatenate(tops, axis=1)


def moments(charges, leaf_basis, child, parent_transfer):
    vm = pl.BlockSpec(memory_space=pltpu.VMEM)
    hbm = pl.BlockSpec(memory_space=pl.ANY)
    return pl.pallas_call(
        moments_kernel,
        out_shape=(
            jax.ShapeDtypeStruct((128, 64), f32),
            jax.ShapeDtypeStruct((16, 64), f32),
            jax.ShapeDtypeStruct((1, 128), f32),
        ),
        in_specs=[vm, hbm, hbm, vm],
        out_specs=(vm,) * 3,
        scratch_shapes=[
            pltpu.VMEM((128, 64, 256), f32),
            pltpu.VMEM((64, 64, 128), f32),
            pltpu.SemaphoreType.DMA((9,)),
        ],
        compiler_params=pltpu.CompilerParams(vmem_limit_bytes=60 << 20),
        name="moments",
    )(charges, leaf_basis, child, parent_transfer)


def tile_rows(x, y, z, a, b):
    r = iota((8, 256), 0)
    v = jnp.where(r == 0, x, jnp.where(r == 1, y, jnp.where(r == 2, z, jnp.where(r == 3, a, b))))
    return jnp.where(r < 5, v, 0.0)


def near_tables(pts_ref, q_ref, sf_ref, qb_ref):
    r = iota((64, 128), 0)
    spread = jnp.where((r >= 48) & (r < 51), 1.0, 0.0).astype(bf16)
    r8 = iota((8, 256), 0)

    def prepare(it, carry):
        for u in range(8):
            n = it * 8 + u
            x = pts_ref[pl.ds(n, 1), :]
            y = pts_ref[pl.ds(128 + n, 1), :]
            z = pts_ref[pl.ds(256 + n, 1), :]
            norm = x * x + y * y + z * z + soften
            h, m, l = split3(tile_rows(x, y, z, jnp.ones_like(x), norm))
            qh, qm, ql = split3(jnp.broadcast_to(q_ref[pl.ds(n, 1), :], (8, 256)))
            q = jnp.where(r8 == 0, qh, jnp.where(r8 == 1, qm, jnp.where(r8 == 2, ql, 0.0)))
            t = jnp.concatenate([h, m, l, h, m, h, q, jnp.zeros_like(q)], axis=0).T.astype(bf16)
            sf_ref[n] = t
            qb_ref[n] = dot(t, spread)
        return carry

    lax.fori_loop(0, 16, prepare, 0)


def near_pairs(lst, base, tgt, sf_ref, qb_ref, rhs_ref, d_ref, acc_ref):
    def entry(i):
        return lst[base + i], lst[base + 1024 + i]

    def factors(i, u):
        lv, _ = entry(i)
        lrow = jnp.maximum(lv - 1, 0)
        x = tgt[pl.ds(lrow, 1), :]
        y = tgt[pl.ds(128 + lrow, 1), :]
        z = tgt[pl.ds(256 + lrow, 1), :]
        norm = x * x + y * y + z * z
        h, m, l = split3(tile_rows(-2.0 * x, -2.0 * y, -2.0 * z, norm, jnp.ones_like(x)))
        rhs_ref[u] = jnp.concatenate([h, h, h, m, m, l], axis=0).astype(bf16)

    def distances(i, u):
        _, n = entry(i)
        d_ref[u] = dot(sf_ref[n, :, 0:48], rhs_ref[u])

    def sums(i, u):
        lv, n = entry(i)
        acc = jnp.zeros((8, 256), f32)
        for j in range(0, 256, 64):
            w = lax.rsqrt(d_ref[u, j : j + 64, :])
            q = qb_ref[n, j : j + 64, :]
            acc = acc + jnp.sum((w * jnp.concatenate([q, q], axis=1)).reshape(8, 8, 256), axis=0)
        row = jnp.where(lv > 0, lv - 1, 128)
        return row, jnp.sum(acc, axis=0, keepdims=True)

    for u in range(NB):
        factors(u, u)
    for u in range(NB):
        distances(u, u)
        factors(NB + u, u)

    def step(it, carry):
        i = it * NB
        got = [sums(i + u, u) for u in range(NB)]
        for u in range(NB):
            distances(i + NB + u, u)
        for u in range(NB):
            factors(i + 2 * NB + u, u)
        for row, val in got:
            acc_ref[pl.ds(row, 1), :] = acc_ref[pl.ds(row, 1), :] + val
        return carry

    lax.fori_loop(0, (lst[base + 896] + NB - 1) // NB, step, 0)


def near_kernel(lst, tgt_l, tgt_r, pts_ref, q_ref, out_own, out_l, out_r, sf_ref, qb_ref, rhs_ref, d_ref, acc_ref):
    near_tables(pts_ref, q_ref, sf_ref, qb_ref)
    for k, (tgt, out) in enumerate(((pts_ref, out_own), (tgt_l, out_l), (tgt_r, out_r))):
        acc_ref[...] = jnp.zeros((136, 256), f32)
        near_pairs(lst, k * 2048, tgt, sf_ref, qb_ref, rhs_ref, d_ref, acc_ref)
        out[...] = acc_ref[0:128, :]


def near(lists, arrays):
    vm = pl.BlockSpec(memory_space=pltpu.VMEM)
    return pl.pallas_call(
        near_kernel,
        out_shape=tuple(jax.ShapeDtypeStruct((128, 256), f32) for _ in range(3)),
        in_specs=[pl.BlockSpec(memory_space=pltpu.SMEM)] + [vm] * 4,
        out_specs=(vm,) * 3,
        scratch_shapes=[
            pltpu.VMEM((128, 256, 64), bf16),
            pltpu.VMEM((128, 256, 128), f32),
            pltpu.VMEM((NB, 48, 256), bf16),
            pltpu.VMEM((NB, 256, 256), f32),
            pltpu.VMEM((136, 256), f32),
        ],
        compiler_params=pltpu.CompilerParams(vmem_limit_bytes=60 << 20),
        name="near",
    )(lists, *arrays)


def halves(x):
    h = x.astype(bf16).astype(f32)
    return h, (x - h).astype(bf16).astype(f32)


def features(x, y, z, source):
    parts = [halves(v) for v in (x, y, z)]
    norm = sum((h + m) * (h + m) for h, m in parts)
    one = jnp.ones_like(x)
    if source:
        nh, nm = halves(norm + soften)
        return [v for h, m in parts for v in (h, m, h, m)] + [one, one, nh, nm]
    nh, nm = halves(norm)
    return [v for h, m in parts for v in (-2.0 * h, -2.0 * h, -2.0 * m, -2.0 * m)] + [nh, nm, one, one]


def far_kernel(
    ids_ref, r1_ref, nl_ref, nm_ref, lm_ref, mm_ref, top_ref, out_ref, v_ref, u_ref, rep_ref, one_ref, mask_ref, ra_ref, mb_ref
):
    for c in range(8):
        r = iota((128, 128), 0) - c * 16
        k = iota((128, 128), 1)
        lanes = slice((c % 2) * 128, (c % 2) * 128 + 128)
        rep_ref[c // 2, :, lanes] = jnp.where(r == (k >> 3), 1.0, 0.0).astype(bf16)
        one_ref[c // 2, :, lanes] = jnp.where((r >= 0) & (r < 3), 1.0, 0.0).astype(bf16)
        mask_ref[c] = jnp.where((iota((64, 128), 1) & 7) == c, 1.0, 0.0).astype(bf16)
    u_ref[...] = jnp.zeros((18 * 128, 64), f32)
    leaf = features(nl_ref[0].T, nl_ref[1].T, nl_ref[2].T, True)
    mid = features(nm_ref[0], nm_ref[1], nm_ref[2], True)
    for f in range(16):
        for blk in range(16):
            v_ref[pl.ds(blk * 128 + f, 8, stride=16), :] = leaf[f][blk * 8 : blk * 8 + 8]
        for blk in range(2):
            v_ref[pl.ds((16 + blk) * 128 + f, 8, stride=16), :] = mid[f][blk * 8 : blk * 8 + 8]

    for blk in range(18):
        src = lm_ref[blk * 8 : blk * 8 + 8, :] if blk < 16 else mm_ref[blk * 8 - 128 : blk * 8 - 120, :]
        for f, v in enumerate(split3(src)):
            u_ref[pl.ds(blk * 128 + f, 8, stride=16), :] = v

    def prepare(it, carry):
        for blk in (it * 2, it * 2 + 1):
            rows = pl.ds(pl.multiple_of(blk * 128, 128), 128)
            v = v_ref[rows, :].T.astype(bf16)
            u = u_ref[rows, :].T.astype(bf16)
            for i in range(4):
                both = dot(v, rep_ref[i]).astype(bf16)
                ra_ref[blk * 8 + 2 * i] = both[:, 0:128]
                ra_ref[blk * 8 + 2 * i + 1] = both[:, 128:256]
                both = dot(u, one_ref[i])
                mb_ref[blk * 8 + 2 * i] = both[:, 0:128]
                mb_ref[blk * 8 + 2 * i + 1] = both[:, 128:256]
        return carry

    lax.fori_loop(0, 9, prepare, 0)
    low = iota((128, 128), 1) < 64
    low64 = iota((64, 128), 1) < 64

    def weights(x, y, z):
        tf = jnp.concatenate(features(x, y, z, False), axis=0)
        return jnp.concatenate([jnp.where(low, tf, 0.0), jnp.where(low, 0.0, tf)], axis=0).astype(bf16)

    def group(rhs, g, t0, t1):
        t0 = jnp.maximum(t0, 0)
        t1 = jnp.maximum(t1, 0)
        mask = mask_ref[g]
        lhs = jnp.concatenate([ra_ref[t0] * mask, ra_ref[t1] * mask], axis=1)
        m = jnp.where(low64, mb_ref[t0], mb_ref[t1])
        w = lax.rsqrt(dot(lhs, rhs)) * m
        return jnp.sum(jnp.sum(w.reshape(8, 8, 128), axis=0), axis=0, keepdims=True)

    def leaf_groups(p, groups):
        rhs = weights(*(r1_ref[pl.ds(pl.multiple_of(p * 32 + 8 * c, 8), 8), :] for c in range(3)))
        return [(p, g, group(rhs, g, ids_ref[p * 24 + g], ids_ref[p * 24 + 8 + g])) for g in groups]

    out_ref[...] = jnp.zeros((1280, 128), f32)
    out_ref[pl.ds(9, 128, stride=10), :] = jnp.broadcast_to(top_ref[...], (128, 128))

    def first(it, carry):
        got = []
        for u in range(4):
            got += leaf_groups(it * 4 + u, range(4))
        for p, g, val in got:
            out_ref[pl.ds(p * 10 + g, 1), :] = val
        return carry

    lax.fori_loop(0, 32, first, 0)

    def second(p, carry):
        @pl.when(ids_ref[p * 24 + 18] > 8)
        def _():
            for q, g, val in leaf_groups(p, range(4, 8)):
                out_ref[pl.ds(q * 10 + g, 1), :] = val

        return carry

    lax.fori_loop(0, 128, second, 0)

    def mids(it, carry):
        got = []
        for u in range(2):
            b = (it * 2 + u) * 256 + 24
            rhs = weights(*(r1_ref[pl.ds(b + c, 8, stride=32), :] for c in range(3)))
            for g in range(8):
                p = (it * 2 + u) * 8 + g
                got.append((p, group(rhs, g, 128 + ids_ref[p * 24 + 16], 128 + ids_ref[p * 24 + 17])))
        for p, val in got:
            out_ref[pl.ds(p * 10 + 8, 1), :] = val
        return carry

    lax.fori_loop(0, 8, mids, 0)


def far(ids, r1, nodes_t, nodes_mid, moments, mid_moments, top_row):
    vm = pl.BlockSpec(memory_space=pltpu.VMEM)
    return pl.pallas_call(
        far_kernel,
        out_shape=jax.ShapeDtypeStruct((1280, 128), f32),
        in_specs=[pl.BlockSpec(memory_space=pltpu.SMEM)] + [vm] * 6,
        out_specs=vm,
        scratch_shapes=[
            pltpu.VMEM((18 * 128, 64), f32),
            pltpu.VMEM((18 * 128, 64), f32),
            pltpu.VMEM((4, 128, 256), bf16),
            pltpu.VMEM((4, 128, 256), bf16),
            pltpu.VMEM((8, 64, 128), bf16),
            pltpu.VMEM((144, 64, 128), bf16),
            pltpu.VMEM((144, 64, 128), f32),
        ],
        compiler_params=pltpu.CompilerParams(vmem_limit_bytes=60 << 20),
        name="far",
    )(ids, r1, nodes_t, nodes_mid, moments, mid_moments, top_row)


def final_kernel(
    top_ids, tab_ref, r1_ref, r2_ref, nt_ref, pt_ref, near_ref, bl_ref, br_ref, lb_hbm, ct_hbm, out_ref, lb_ref, ct_ref, sem
):
    def part(k):
        rows = pl.ds(k * 16, 16)
        return pltpu.make_async_copy(lb_hbm.at[rows], lb_ref.at[rows], sem.at[k])

    child = pltpu.make_async_copy(ct_hbm, ct_ref, sem.at[8])
    child.start()
    for k in range(8):
        part(k).start()
    tag = (iota((128, 128), 0) + 1).astype(f32)

    def lines(k, rows):
        return jnp.where(tab_ref[k : k + 1, :] == tag[0:rows], 1.0, 0.0)

    def two(x):
        return jnp.concatenate(halves(x), axis=1).astype(bf16)

    acc = [jnp.zeros((128, 256), f32), jnp.zeros((128, 256), f32)]
    for g in range(0, 8, 2):
        vals = jnp.concatenate([two(r2_ref[pl.ds(g + k, 128, stride=10), :]) for k in range(2)], axis=0)
        for h in range(2):
            oh = jnp.concatenate([lines(8 * h + g, 128), lines(8 * h + g + 1, 128)], axis=1).astype(bf16)
            acc[h] = acc[h] + dot(oh, vals)
    acc = [a[:, 0:128] + a[:, 128:256] for a in acc]
    local_t = acc[0].T[0:64] + acc[1].T[64:128]
    vals = two(r2_ref[pl.ds(8, 128, stride=10), :])
    res = [dot(lines(16 + h, 16).astype(bf16), vals) for h in range(2)]
    res = [a[:, 0:128] + a[:, 128:256] for a in res]
    mid_local = res[0][:, 0:64] + res[1][:, 64:128]
    half = iota((1, 128), 1) >> 6
    pad = jnp.zeros((6, 64), f32)
    cols = [jnp.concatenate([nt_ref[c], pad], axis=0).T for c in range(3)]
    rows = []
    for g in range(2):
        tx, ty, tz = (jnp.broadcast_to(cols[c][:, g : g + 1], (64, 128)) for c in range(3))

        def entry(it, total):
            for u in range(4):
                t = top_ids[g, it * 4 + u]
                p = jnp.maximum(t, 0) >> 1
                h = jnp.where(t < 0, 2, t & 1)
                m = jnp.where(half == h, r2_ref[pl.ds(p * 10 + 9, 1), :], 0.0)
                dx = tx - r1_ref[pl.ds(p * 32 + 28, 1), :]
                dy = ty - r1_ref[pl.ds(p * 32 + 29, 1), :]
                dz = tz - r1_ref[pl.ds(p * 32 + 30, 1), :]
                total = total + lax.rsqrt(dx * dx + dy * dy + dz * dz + soften) * m
            return total

        total = lax.fori_loop(0, 4, entry, jnp.zeros((64, 128), f32))
        top = jnp.broadcast_to(jnp.sum(total, axis=1, keepdims=True), (64, 64))
        for c in range(g * 8, g * 8 + 8):
            rows.append(jnp.sum(pt_ref[c] * top, axis=0, keepdims=True))
    mid_down = mid_local + jnp.concatenate(rows, axis=0)
    mid_t = jnp.concatenate([mid_down, jnp.zeros((112, 64), f32)], axis=0).T
    spread = jnp.where(iota((128, 128), 0) == (iota((128, 128), 1) >> 3), 1.0, 0.0).astype(bf16)
    mid_t = dot3(mid_t, spread)
    child.wait()
    down = local_t
    for i in range(64):
        down = down + ct_ref[i] * mid_t[i : i + 1, :]
    h, m = halves(down)
    pick = jnp.where((iota((32, 2048), 0) & 15) == (iota((32, 2048), 1) >> 7), 1.0, 0.0).astype(bf16)
    for k in range(8):
        part(k).wait()
        ks = slice(16 * k, 16 * k + 16)
        cols16 = dot(jnp.concatenate([h[:, ks], m[:, ks]], axis=1).astype(bf16), pick)
        for u in range(16):
            d = cols16[:, u * 128 : u * 128 + 128]
            n = 16 * k + u
            out_ref[n : n + 1, :] = jnp.sum(lb_ref[n] * jnp.concatenate([d, d], axis=1), axis=0, keepdims=True)
    out_ref[...] = out_ref[...] + near_ref[...] + bl_ref[...] + br_ref[...]


def final(far_top, arrays, leaf_basis, child):
    vm = pl.BlockSpec(memory_space=pltpu.VMEM)
    hbm = pl.BlockSpec(memory_space=pl.ANY)
    return pl.pallas_call(
        final_kernel,
        out_shape=jax.ShapeDtypeStruct((128, 256), f32),
        in_specs=[pl.BlockSpec(memory_space=pltpu.SMEM)] + [vm] * 8 + [hbm] * 2,
        out_specs=vm,
        scratch_shapes=[
            pltpu.VMEM((128, 64, 256), f32),
            pltpu.VMEM((64, 64, 128), f32),
            pltpu.SemaphoreType.DMA((9,)),
        ],
        compiler_params=pltpu.CompilerParams(vmem_limit_bytes=60 << 20),
        name="final",
    )(far_top, *arrays, leaf_basis, child)


def swap(x):
    return lax.all_to_all(x, AXES, split_axis=0, concat_axis=0, tiled=True)


def local(
    charges,
    points,
    leaf_basis,
    child_transfer,
    parent_transfer,
    nodes_leaf,
    nodes_mid,
    nodes_top,
    near_list,
    far_leaf,
    far_mid,
    far_top,
):
    shards = lax.axis_size(AXES)
    me = lax.axis_index(AXES).astype(i32).reshape(1)
    down_perm = [(i + 1, i) for i in range(shards - 1)]
    up_perm = [(i, i + 1) for i in range(shards - 1)]
    nodes_t = jnp.transpose(nodes_leaf, (0, 2, 1))
    pay, tab, own_list, to_left, to_right = plan(
        me, far_leaf.T, far_mid, near_list.T, nodes_t, nodes_mid, nodes_top, points
    )
    from_right = lax.ppermute(to_left, AXES, down_perm)
    from_left = lax.ppermute(to_right, AXES, up_perm)
    r1 = swap(pay)
    child = jnp.transpose(child_transfer, (1, 2, 0))
    leaf_moments, mid_moments, top_moments = moments(charges, leaf_basis, child, parent_transfer)
    lists = jnp.stack([own_list, from_left[384:392].astype(i32), from_right[384:392].astype(i32)])
    lists = jnp.transpose(lists.reshape(3, 8, 2, 128), (0, 2, 1, 3)).reshape(6144)
    flat = points.reshape(384, 256)
    near_own, near_l, near_r = near(lists, [from_left, from_right, flat, charges])
    back_l = lax.ppermute(near_l, AXES, down_perm)
    back_r = lax.ppermute(near_r, AXES, up_perm)
    r1, near_own, leaf_moments, mid_moments, top_moments = lax.optimization_barrier(
        (r1, near_own, leaf_moments, mid_moments, top_moments)
    )
    ids = r1[:, 27, 0:24].astype(i32).reshape(3072)
    r1 = r1.reshape(4096, 128)
    pay2 = far(ids, r1, nodes_t, nodes_mid, leaf_moments, mid_moments, top_moments)
    r2 = swap(pay2.reshape(128, 5, 2, 128)).reshape(1280, 128)
    return final(far_top, [tab, r1, r2, nodes_top, parent_transfer, near_own, back_l, back_r], leaf_basis, child)


def solution(mesh):
    placed = (
        P(AXES, None),
        P(None, AXES, None),
        P(AXES, None, None),
        P(AXES, None, None),
        P(AXES, None, None),
        P(None, AXES, None),
        P(None, AXES, None),
        P(None, AXES, None),
        P(AXES, None),
        P(AXES, None),
        P(AXES, None),
        P(AXES, None),
    )
    return jax.shard_map(local, mesh=mesh, in_specs=placed, out_specs=P(AXES, None), check_vma=False)
```

```python
import jax
import jax.numpy as jnp
from jax import lax
from jax.experimental import pallas as pl
from jax.experimental.pallas import tpu as pltpu
from jax.sharding import PartitionSpec as P


f32 = jnp.float32
bf16 = jnp.bfloat16
i32 = jnp.int32
soften = 0.25
AXES = ("dom", "sub")
NB = 8
TRANS = (((1,), (1,)), ((), ()))


def dot(a, b):
    return jnp.dot(a, b, preferred_element_type=f32)


def dot_t(a, b):
    return lax.dot_general(a, b, TRANS, preferred_element_type=f32)


def split3(v):
    h = v.astype(bf16).astype(f32)
    r = v - h
    m = r.astype(bf16).astype(f32)
    return h, m, (r - m).astype(bf16).astype(f32)


def iota(shape, dim):
    return lax.broadcasted_iota(i32, shape, dim)


def upper(n):
    return jnp.where(iota((n, n), 0) <= iota((n, n), 1), 1.0, 0.0).astype(bf16)


def slots(owner_rows, wanted_rows, ids, caps):
    width = owner_rows[0].shape[1]
    tri = upper(width)
    half = caps // 2
    r = iota((caps, width), 0)
    slot = jnp.where(r < half, 2 * r, 2 * (r - half) + 1)
    row = jnp.zeros((2 * caps, 128), f32)
    carry = jnp.zeros((128, 1), f32)
    for own, want in zip(owner_rows, wanted_rows):
        hit = jnp.where(own == iota((128, width), 0), 1.0, 0.0)
        hit_b = hit.astype(bf16)
        cum = dot(hit_b, tri) + carry
        carry = cum[:, width - 1 : width]
        rank = jnp.sum(hit * cum, axis=0, keepdims=True).astype(i32) - 1
        place = jnp.where(rank == slot, 1.0, 0.0)
        vals = jnp.concatenate([place * (ids + 1.0), place * (want + 1.0)], axis=0).astype(bf16)
        row = row + dot_t(vals, hit_b)
    return row, carry


def plan_kernel(
    me_ref, far_ref, mid_ref, near_ref, nl_ref, nm_ref, nt_ref, pts_ref, pay_ref, tab_ref, own_ref, hl_ref, hr_ref, oh_ref
):
    me = me_ref[0]
    lane = iota((1, 128), 1)
    ids = lane.astype(f32)
    far = far_ref[...]
    own = far >> 7
    want = (far & 127).astype(f32)
    row, live = slots([own[c : c + 1] for c in range(16)], [want[c : c + 1] for c in range(16)], ids, 16)
    eye = jnp.where(iota((16, 16), 0) == iota((16, 16), 1), 1.0, 0.0).astype(bf16)
    mid = mid_ref[...]
    mown = dot_t(eye, (mid >> 4).astype(f32).astype(bf16)).astype(i32)
    mwant = dot_t(eye, (mid & 15).astype(f32).astype(bf16))
    mrow, mlive = slots(
        [mown[c : c + 1] for c in range(16)], [mwant[c : c + 1] for c in range(16)], ids[:, 0:16], 2
    )
    col = jnp.concatenate([row, mrow, jnp.zeros((92, 128), f32)], axis=0).T
    mcol = col[:, 32:36]
    tab_ref[0:16, :] = row[0:16]
    tab_ref[16:18, :] = mrow[0:2]
    tab_ref[18:32, :] = jnp.zeros((14, 128), f32)
    even, odd = row[0:8], row[8:16]
    line = jnp.broadcast_to(ids + 1.0, (8, 128))
    for o in range(128):
        a = jnp.broadcast_to(even[:, o : o + 1], (8, 128))
        b = jnp.broadcast_to(odd[:, o : o + 1], (8, 128))
        oh_ref[o * 8 : o * 8 + 8, 0:128] = jnp.where(a == line, 1.0, 0.0)
        oh_ref[o * 8 : o * 8 + 8, 128:256] = jnp.where(b == line, 1.0, 0.0)
    oh = oh_ref[...].astype(bf16)
    z = jnp.zeros((64, 128), f32)
    blocks = []
    for c in range(3):
        x = nl_ref[c]
        big = jnp.concatenate([jnp.concatenate([x, z], axis=1), jnp.concatenate([z, x], axis=1)], axis=0)
        blocks += [v.astype(bf16) for v in split3(big)]
    for c in range(3):
        h, m, l = blocks[3 * c : 3 * c + 3]
        both = dot_t(oh, jnp.concatenate([h, m], axis=0))
        pay_ref[:, c * 8 : c * 8 + 8, :] = (both[:, 0:128] + both[:, 128:256]).reshape(128, 8, 128)
    both = dot_t(oh, jnp.concatenate([blocks[2], blocks[5]], axis=0))
    pay_ref[:, 0:8, :] = pay_ref[:, 0:8, :] + both[:, 0:128].reshape(128, 8, 128)
    pay_ref[:, 8:16, :] = pay_ref[:, 8:16, :] + both[:, 128:256].reshape(128, 8, 128)
    pay_ref[:, 16:24, :] = pay_ref[:, 16:24, :] + dot_t(oh, blocks[8]).reshape(128, 8, 128)
    tops = [jnp.concatenate([nt_ref[c, 0:1], nt_ref[c, 1:2]], axis=1) for c in range(3)]
    zero = jnp.zeros((1, 128), f32)
    last = jnp.concatenate([zero] * 4 + tops + [zero], axis=0)
    pay_ref[:, 24:32, :] = jnp.broadcast_to(last[None], (128, 8, 128))
    la = jnp.where(mcol[:, 0:1] == ids[:, 0:16] + 1.0, 1.0, 0.0)
    lb = jnp.where(mcol[:, 1:2] == ids[:, 0:16] + 1.0, 1.0, 0.0)
    ohm = jnp.concatenate([la, lb], axis=1).astype(bf16)
    for c in range(3):
        xm = nm_ref[c]
        zm = jnp.zeros((16, 64), f32)
        bigm = jnp.concatenate([jnp.concatenate([xm, zm], axis=1), jnp.concatenate([zm, xm], axis=1)], axis=0)
        h, m, l = split3(bigm)
        resm = dot(ohm, h.astype(bf16)) + dot(ohm, m.astype(bf16)) + dot(ohm, l.astype(bf16))
        pay_ref[:, 24 + c : 25 + c, :] = resm[:, None, :]
    idrow = jnp.concatenate(
        [col[:, 16:32] - 1.0, mcol[:, 2:4] - 1.0, live, mlive, jnp.zeros((128, 108), f32)], axis=1
    )
    pay_ref[:, 27:28, :] = idrow[:, None, :]
    near = near_ref[...]
    nown = near >> 7
    nloc = (near & 127).astype(f32)
    tri = upper(128)
    outs = []
    for d in (-1, 0, 1):
        hit = jnp.where((nown == me + d) & (near >= 0), 1.0, 0.0)
        cum = dot(hit.astype(bf16), tri)
        base = jnp.zeros((1, 1), f32)
        acc = jnp.zeros((16, 128), f32)
        for c in range(6):
            pos = (cum[c : c + 1] + base).astype(i32) - 1
            base = base + cum[c : c + 1, 127:128]
            bm = jnp.where((pos & 127) == iota((128, 128), 0), hit[c : c + 1], 0.0).astype(bf16)
            am = jnp.where((pos >> 7) == iota((8, 128), 0), 1.0, 0.0)
            vals = jnp.concatenate([am * (ids + 1.0), am * nloc[c : c + 1]], axis=0).astype(bf16)
            acc = acc + dot_t(vals, bm)
        outs.append((jnp.where(iota((8, 128), 0) == 7, base, acc[0:8]), acc[8:16]))
    own_ref[:, 0:128] = outs[1][0].astype(i32)
    own_ref[:, 128:256] = outs[1][1].astype(i32)
    for ref, k in ((hl_ref, 0), (hr_ref, 2)):
        for c in range(3):
            ref[c * 128 : (c + 1) * 128, :] = pts_ref[c]
        ref[384:392, 0:128] = outs[k][0]
        ref[384:392, 128:256] = outs[k][1]


def plan(me, far_t, far_mid, near_t, nodes_t, nodes_mid, nodes_top, points):
    vm = pl.BlockSpec(memory_space=pltpu.VMEM)
    return pl.pallas_call(
        plan_kernel,
        out_shape=(
            jax.ShapeDtypeStruct((128, 32, 128), f32),
            jax.ShapeDtypeStruct((32, 128), f32),
            jax.ShapeDtypeStruct((8, 256), i32),
            jax.ShapeDtypeStruct((392, 256), f32),
            jax.ShapeDtypeStruct((392, 256), f32),
        ),
        in_specs=[pl.BlockSpec(memory_space=pltpu.SMEM)] + [vm] * 7,
        out_specs=(vm,) * 5,
        scratch_shapes=[pltpu.VMEM((1024, 256), f32)],
        compiler_params=pltpu.CompilerParams(vmem_limit_bytes=60 << 20),
        name="plan",
    )(me, far_t, far_mid, near_t, nodes_t, nodes_mid, nodes_top, points)


def dot3(a, b):
    return sum(dot(v.astype(bf16), b) for v in split3(a))


def moments_kernel(q_ref, lb_hbm, ct_hbm, pt_ref, lm_ref, mm_ref, top_ref, lb_ref, ct_ref, sem):
    def part(k):
        rows = pl.ds(k * 16, 16)
        return pltpu.make_async_copy(lb_hbm.at[rows], lb_ref.at[rows], sem.at[k])

    child = pltpu.make_async_copy(ct_hbm, ct_ref, sem.at[8])
    for k in range(8):
        part(k).start()
    child.start()
    lane = iota((64, 128), 1)
    lmt = jnp.zeros((64, 128), f32)
    for k in range(8):
        part(k).wait()

        def leaf(it, acc):
            for u in range(4):
                n = k * 16 + it * 4 + u
                prod = lb_ref[n] * q_ref[pl.ds(n, 1), :]
                col = jnp.sum(prod[:, 0:128] + prod[:, 128:256], axis=1, keepdims=True)
                acc = jnp.where(lane == n, col, acc)
            return acc

        lmt = lax.fori_loop(0, 4, leaf, lmt)
    lm_ref[...] = lmt.T
    child.wait()
    rows = []
    for i in range(64):
        rows.append(jnp.sum(ct_ref[i] * lmt, axis=0, keepdims=True))
    per_leaf = jnp.concatenate(rows, axis=0)
    group = jnp.where((iota((128, 128), 0) >> 3) == iota((128, 128), 1), 1.0, 0.0).astype(bf16)
    mm = dot3(per_leaf, group).T
    mm_ref[...] = mm[0:16, :]
    tops = []
    for g in range(2):
        acc = jnp.zeros((64, 64), f32)
        for c in range(g * 8, g * 8 + 8):
            acc = acc + pt_ref[c] * mm[c : c + 1, :]
        tops.append(jnp.broadcast_to(jnp.sum(acc, axis=1, keepdims=True), (64, 128)).T[0:1])
    top_ref[...] = jnp.concatenate(tops, axis=1)


def moments(charges, leaf_basis, child, parent_transfer):
    vm = pl.BlockSpec(memory_space=pltpu.VMEM)
    hbm = pl.BlockSpec(memory_space=pl.ANY)
    return pl.pallas_call(
        moments_kernel,
        out_shape=(
            jax.ShapeDtypeStruct((128, 64), f32),
            jax.ShapeDtypeStruct((16, 64), f32),
            jax.ShapeDtypeStruct((1, 128), f32),
        ),
        in_specs=[vm, hbm, hbm, vm],
        out_specs=(vm,) * 3,
        scratch_shapes=[
            pltpu.VMEM((128, 64, 256), f32),
            pltpu.VMEM((64, 64, 128), f32),
            pltpu.SemaphoreType.DMA((9,)),
        ],
        compiler_params=pltpu.CompilerParams(vmem_limit_bytes=60 << 20),
        name="moments",
    )(charges, leaf_basis, child, parent_transfer)


def tile_rows(x, y, z, a, b):
    r = iota((8, 256), 0)
    v = jnp.where(r == 0, x, jnp.where(r == 1, y, jnp.where(r == 2, z, jnp.where(r == 3, a, b))))
    return jnp.where(r < 5, v, 0.0)


def near_tables(pts_ref, q_ref, sf_ref, qb_ref):
    r = iota((64, 128), 0)
    spread = jnp.where((r >= 48) & (r < 51), 1.0, 0.0).astype(bf16)
    r8 = iota((8, 256), 0)

    def prepare(it, carry):
        for u in range(8):
            n = it * 8 + u
            x = pts_ref[pl.ds(n, 1), :]
            y = pts_ref[pl.ds(128 + n, 1), :]
            z = pts_ref[pl.ds(256 + n, 1), :]
            norm = x * x + y * y + z * z + soften
            h, m, l = split3(tile_rows(x, y, z, jnp.ones_like(x), norm))
            qh, qm, ql = split3(jnp.broadcast_to(q_ref[pl.ds(n, 1), :], (8, 256)))
            q = jnp.where(r8 == 0, qh, jnp.where(r8 == 1, qm, jnp.where(r8 == 2, ql, 0.0)))
            t = jnp.concatenate([h, m, l, h, m, h, q, jnp.zeros_like(q)], axis=0).T.astype(bf16)
            sf_ref[n] = t
            qb_ref[n] = dot(t, spread)
        return carry

    lax.fori_loop(0, 16, prepare, 0)


def near_pairs(lst, base, tgt, sf_ref, qb_ref, rhs_ref, d_ref, acc_ref):
    def entry(i):
        return lst[base + i], lst[base + 1024 + i]

    def factors(i, u):
        lv, _ = entry(i)
        lrow = jnp.maximum(lv - 1, 0)
        x = tgt[pl.ds(lrow, 1), :]
        y = tgt[pl.ds(128 + lrow, 1), :]
        z = tgt[pl.ds(256 + lrow, 1), :]
        norm = x * x + y * y + z * z
        h, m, l = split3(tile_rows(-2.0 * x, -2.0 * y, -2.0 * z, norm, jnp.ones_like(x)))
        rhs_ref[u] = jnp.concatenate([h, h, h, m, m, l], axis=0).astype(bf16)

    def distances(i, u):
        _, n = entry(i)
        d_ref[u] = dot(sf_ref[n, :, 0:48], rhs_ref[u])

    def sums(i, u):
        lv, n = entry(i)
        acc = jnp.zeros((8, 256), f32)
        for j in range(0, 256, 64):
            w = lax.rsqrt(d_ref[u, j : j + 64, :])
            q = qb_ref[n, j : j + 64, :]
            acc = acc + jnp.sum((w * jnp.concatenate([q, q], axis=1)).reshape(8, 8, 256), axis=0)
        row = jnp.where(lv > 0, lv - 1, 128)
        return row, jnp.sum(acc, axis=0, keepdims=True)

    for u in range(NB):
        factors(u, u)
    for u in range(NB):
        distances(u, u)
        factors(NB + u, u)

    def step(it, carry):
        i = it * NB
        got = [sums(i + u, u) for u in range(NB)]
        for u in range(NB):
            distances(i + NB + u, u)
        for u in range(NB):
            factors(i + 2 * NB + u, u)
        for row, val in got:
            acc_ref[pl.ds(row, 1), :] = acc_ref[pl.ds(row, 1), :] + val
        return carry

    lax.fori_loop(0, (lst[base + 896] + NB - 1) // NB, step, 0)


def near_kernel(lst, tgt_l, tgt_r, pts_ref, q_ref, out_own, out_l, out_r, sf_ref, qb_ref, rhs_ref, d_ref, acc_ref):
    near_tables(pts_ref, q_ref, sf_ref, qb_ref)
    for k, (tgt, out) in enumerate(((pts_ref, out_own), (tgt_l, out_l), (tgt_r, out_r))):
        acc_ref[...] = jnp.zeros((136, 256), f32)
        near_pairs(lst, k * 2048, tgt, sf_ref, qb_ref, rhs_ref, d_ref, acc_ref)
        out[...] = acc_ref[0:128, :]


def near(lists, arrays):
    vm = pl.BlockSpec(memory_space=pltpu.VMEM)
    return pl.pallas_call(
        near_kernel,
        out_shape=tuple(jax.ShapeDtypeStruct((128, 256), f32) for _ in range(3)),
        in_specs=[pl.BlockSpec(memory_space=pltpu.SMEM)] + [vm] * 4,
        out_specs=(vm,) * 3,
        scratch_shapes=[
            pltpu.VMEM((128, 256, 64), bf16),
            pltpu.VMEM((128, 256, 128), f32),
            pltpu.VMEM((NB, 48, 256), bf16),
            pltpu.VMEM((NB, 256, 256), f32),
            pltpu.VMEM((136, 256), f32),
        ],
        compiler_params=pltpu.CompilerParams(vmem_limit_bytes=60 << 20),
        name="near",
    )(lists, *arrays)


def halves(x):
    h = x.astype(bf16).astype(f32)
    return h, (x - h).astype(bf16).astype(f32)


def features(x, y, z, source):
    parts = [halves(v) for v in (x, y, z)]
    norm = sum((h + m) * (h + m) for h, m in parts)
    one = jnp.ones_like(x)
    if source:
        nh, nm = halves(norm + soften)
        return [v for h, m in parts for v in (h, m, h, m)] + [one, one, nh, nm]
    nh, nm = halves(norm)
    return [v for h, m in parts for v in (-2.0 * h, -2.0 * h, -2.0 * m, -2.0 * m)] + [nh, nm, one, one]


def far_kernel(
    ids_ref, r1_ref, nl_ref, nm_ref, lm_ref, mm_ref, top_ref, out_ref, v_ref, u_ref, rep_ref, one_ref, mask_ref, ra_ref, mb_ref, full_ref
):
    for c in range(8):
        r = iota((128, 128), 0) - c * 16
        k = iota((128, 128), 1)
        lanes = slice((c % 2) * 128, (c % 2) * 128 + 128)
        rep_ref[c // 2, :, lanes] = jnp.where(r == (k >> 3), 1.0, 0.0).astype(bf16)
        one_ref[c // 2, :, lanes] = jnp.where((r >= 0) & (r < 3), 1.0, 0.0).astype(bf16)
        mask_ref[c] = jnp.where((iota((64, 128), 1) & 7) == c, 1.0, 0.0).astype(bf16)
    u_ref[...] = jnp.zeros((18 * 128, 64), f32)
    leaf = features(nl_ref[0].T, nl_ref[1].T, nl_ref[2].T, True)
    mid = features(nm_ref[0], nm_ref[1], nm_ref[2], True)
    for f in range(16):
        for blk in range(16):
            v_ref[pl.ds(blk * 128 + f, 8, stride=16), :] = leaf[f][blk * 8 : blk * 8 + 8]
        for blk in range(2):
            v_ref[pl.ds((16 + blk) * 128 + f, 8, stride=16), :] = mid[f][blk * 8 : blk * 8 + 8]

    for blk in range(18):
        src = lm_ref[blk * 8 : blk * 8 + 8, :] if blk < 16 else mm_ref[blk * 8 - 128 : blk * 8 - 120, :]
        for f, v in enumerate(split3(src)):
            u_ref[pl.ds(blk * 128 + f, 8, stride=16), :] = v

    def prepare(it, carry):
        for blk in (it * 3, it * 3 + 1, it * 3 + 2):
            rows = pl.ds(pl.multiple_of(blk * 128, 128), 128)
            v = v_ref[rows, :].T.astype(bf16)
            u = u_ref[rows, :].T.astype(bf16)
            for i in range(4):
                both = dot(v, rep_ref[i]).astype(bf16)
                ra_ref[blk * 8 + 2 * i] = both[:, 0:128]
                ra_ref[blk * 8 + 2 * i + 1] = both[:, 128:256]
                both = dot(u, one_ref[i])
                mb_ref[blk * 8 + 2 * i] = both[:, 0:128]
                mb_ref[blk * 8 + 2 * i + 1] = both[:, 128:256]
        return carry

    lax.fori_loop(0, 6, prepare, 0)
    low = iota((128, 128), 1) < 64
    low64 = iota((64, 128), 1) < 64

    def weights(x, y, z):
        tf = jnp.concatenate(features(x, y, z, False), axis=0)
        return jnp.concatenate([jnp.where(low, tf, 0.0), jnp.where(low, 0.0, tf)], axis=0).astype(bf16)

    def group(rhs, g, t0, t1):
        t0 = jnp.maximum(t0, 0)
        t1 = jnp.maximum(t1, 0)
        mask = mask_ref[g]
        lhs = jnp.concatenate([ra_ref[t0] * mask, ra_ref[t1] * mask], axis=1)
        m = jnp.where(low64, mb_ref[t0], mb_ref[t1])
        w = lax.rsqrt(dot(lhs, rhs)) * m
        return jnp.sum(jnp.sum(w.reshape(8, 8, 128), axis=0), axis=0, keepdims=True)

    def leaf_groups(p, groups):
        rhs = weights(*(r1_ref[pl.ds(pl.multiple_of(p * 32 + 8 * c, 8), 8), :] for c in range(3)))
        return [(p, g, group(rhs, g, ids_ref[p * 24 + g], ids_ref[p * 24 + 8 + g])) for g in groups]

    out_ref[...] = jnp.zeros((1280, 128), f32)
    out_ref[pl.ds(9, 128, stride=10), :] = jnp.broadcast_to(top_ref[...], (128, 128))

    def first(it, carry):
        got = []
        for u in range(4):
            got += leaf_groups(it * 4 + u, range(4))
        for p, g, val in got:
            out_ref[pl.ds(p * 10 + g, 1), :] = val
        return carry

    lax.fori_loop(0, 32, first, 0)

    def scan(it, pos):
        for u in range(8):
            p = it * 8 + u
            full_ref[pos] = p
            pos = pos + (ids_ref[p * 24 + 18] > 8).astype(i32)
        return pos

    full = lax.fori_loop(0, 16, scan, jnp.int32(0))
    full_ref[full] = 0

    def second(it, carry):
        got = []
        for u in range(2):
            got += leaf_groups(full_ref[it * 2 + u], range(4, 8))
        for p, g, val in got:
            out_ref[pl.ds(p * 10 + g, 1), :] = val
        return carry

    lax.fori_loop(0, (full + 1) // 2, second, 0)

    def mids(it, carry):
        got = []
        for u in range(2):
            b = (it * 2 + u) * 256 + 24
            rhs = weights(*(r1_ref[pl.ds(b + c, 8, stride=32), :] for c in range(3)))
            for g in range(8):
                p = (it * 2 + u) * 8 + g
                got.append((p, group(rhs, g, 128 + ids_ref[p * 24 + 16], 128 + ids_ref[p * 24 + 17])))
        for p, val in got:
            out_ref[pl.ds(p * 10 + 8, 1), :] = val
        return carry

    lax.fori_loop(0, 8, mids, 0)


def far(ids, r1, nodes_t, nodes_mid, moments, mid_moments, top_row):
    vm = pl.BlockSpec(memory_space=pltpu.VMEM)
    return pl.pallas_call(
        far_kernel,
        out_shape=jax.ShapeDtypeStruct((1280, 128), f32),
        in_specs=[pl.BlockSpec(memory_space=pltpu.SMEM)] + [vm] * 6,
        out_specs=vm,
        scratch_shapes=[
            pltpu.VMEM((18 * 128, 64), f32),
            pltpu.VMEM((18 * 128, 64), f32),
            pltpu.VMEM((4, 128, 256), bf16),
            pltpu.VMEM((4, 128, 256), bf16),
            pltpu.VMEM((8, 64, 128), bf16),
            pltpu.VMEM((144, 64, 128), bf16),
            pltpu.VMEM((144, 64, 128), f32),
            pltpu.SMEM((136,), i32),
        ],
        compiler_params=pltpu.CompilerParams(vmem_limit_bytes=60 << 20),
        name="far",
    )(ids, r1, nodes_t, nodes_mid, moments, mid_moments, top_row)


def final_kernel(
    top_ids, tab_ref, r1_ref, r2_ref, nt_ref, pt_ref, near_ref, bl_ref, br_ref, lb_hbm, ct_hbm, out_ref, lb_ref, ct_ref, sem
):
    def part(k):
        rows = pl.ds(k * 16, 16)
        return pltpu.make_async_copy(lb_hbm.at[rows], lb_ref.at[rows], sem.at[k])

    child = pltpu.make_async_copy(ct_hbm, ct_ref, sem.at[8])
    child.start()
    for k in range(8):
        part(k).start()
    tag = (iota((128, 128), 0) + 1).astype(f32)

    def lines(k, rows):
        return jnp.where(tab_ref[k : k + 1, :] == tag[0:rows], 1.0, 0.0)

    def two(x):
        return jnp.concatenate(halves(x), axis=1).astype(bf16)

    acc = [jnp.zeros((128, 256), f32), jnp.zeros((128, 256), f32)]
    for g in range(0, 8, 2):
        vals = jnp.concatenate([two(r2_ref[pl.ds(g + k, 128, stride=10), :]) for k in range(2)], axis=0)
        for h in range(2):
            oh = jnp.concatenate([lines(8 * h + g, 128), lines(8 * h + g + 1, 128)], axis=1).astype(bf16)
            acc[h] = acc[h] + dot(oh, vals)
    acc = [a[:, 0:128] + a[:, 128:256] for a in acc]
    local_t = acc[0].T[0:64] + acc[1].T[64:128]
    vals = two(r2_ref[pl.ds(8, 128, stride=10), :])
    res = [dot(lines(16 + h, 16).astype(bf16), vals) for h in range(2)]
    res = [a[:, 0:128] + a[:, 128:256] for a in res]
    mid_local = res[0][:, 0:64] + res[1][:, 64:128]
    half = iota((1, 128), 1) >> 6
    pad = jnp.zeros((6, 64), f32)
    cols = [jnp.concatenate([nt_ref[c], pad], axis=0).T for c in range(3)]
    rows = []
    for g in range(2):
        tx, ty, tz = (jnp.broadcast_to(cols[c][:, g : g + 1], (64, 128)) for c in range(3))

        def entry(it, total):
            for u in range(4):
                t = top_ids[g, it * 4 + u]
                p = jnp.maximum(t, 0) >> 1
                h = jnp.where(t < 0, 2, t & 1)
                m = jnp.where(half == h, r2_ref[pl.ds(p * 10 + 9, 1), :], 0.0)
                dx = tx - r1_ref[pl.ds(p * 32 + 28, 1), :]
                dy = ty - r1_ref[pl.ds(p * 32 + 29, 1), :]
                dz = tz - r1_ref[pl.ds(p * 32 + 30, 1), :]
                total = total + lax.rsqrt(dx * dx + dy * dy + dz * dz + soften) * m
            return total

        total = lax.fori_loop(0, 4, entry, jnp.zeros((64, 128), f32))
        top = jnp.broadcast_to(jnp.sum(total, axis=1, keepdims=True), (64, 64))
        for c in range(g * 8, g * 8 + 8):
            rows.append(jnp.sum(pt_ref[c] * top, axis=0, keepdims=True))
    mid_down = mid_local + jnp.concatenate(rows, axis=0)
    mid_t = jnp.concatenate([mid_down, jnp.zeros((112, 64), f32)], axis=0).T
    spread = jnp.where(iota((128, 128), 0) == (iota((128, 128), 1) >> 3), 1.0, 0.0).astype(bf16)
    mid_t = dot3(mid_t, spread)
    child.wait()
    down = local_t
    for i in range(64):
        down = down + ct_ref[i] * mid_t[i : i + 1, :]
    h, m = halves(down)
    pick = jnp.where((iota((32, 2048), 0) & 15) == (iota((32, 2048), 1) >> 7), 1.0, 0.0).astype(bf16)
    for k in range(8):
        part(k).wait()
        ks = slice(16 * k, 16 * k + 16)
        cols16 = dot(jnp.concatenate([h[:, ks], m[:, ks]], axis=1).astype(bf16), pick)
        for u in range(16):
            d = cols16[:, u * 128 : u * 128 + 128]
            n = 16 * k + u
            out_ref[n : n + 1, :] = jnp.sum(lb_ref[n] * jnp.concatenate([d, d], axis=1), axis=0, keepdims=True)
    out_ref[...] = out_ref[...] + near_ref[...] + bl_ref[...] + br_ref[...]


def final(far_top, arrays, leaf_basis, child):
    vm = pl.BlockSpec(memory_space=pltpu.VMEM)
    hbm = pl.BlockSpec(memory_space=pl.ANY)
    return pl.pallas_call(
        final_kernel,
        out_shape=jax.ShapeDtypeStruct((128, 256), f32),
        in_specs=[pl.BlockSpec(memory_space=pltpu.SMEM)] + [vm] * 8 + [hbm] * 2,
        out_specs=vm,
        scratch_shapes=[
            pltpu.VMEM((128, 64, 256), f32),
            pltpu.VMEM((64, 64, 128), f32),
            pltpu.SemaphoreType.DMA((9,)),
        ],
        compiler_params=pltpu.CompilerParams(vmem_limit_bytes=60 << 20),
        name="final",
    )(far_top, *arrays, leaf_basis, child)


def swap(x):
    return lax.all_to_all(x, AXES, split_axis=0, concat_axis=0, tiled=True)


def local(
    charges,
    points,
    leaf_basis,
    child_transfer,
    parent_transfer,
    nodes_leaf,
    nodes_mid,
    nodes_top,
    near_list,
    far_leaf,
    far_mid,
    far_top,
):
    shards = lax.axis_size(AXES)
    me = lax.axis_index(AXES).astype(i32).reshape(1)
    down_perm = [(i + 1, i) for i in range(shards - 1)]
    up_perm = [(i, i + 1) for i in range(shards - 1)]
    nodes_t = jnp.transpose(nodes_leaf, (0, 2, 1))
    pay, tab, own_list, to_left, to_right = plan(
        me, far_leaf.T, far_mid, near_list.T, nodes_t, nodes_mid, nodes_top, points
    )
    from_right = lax.ppermute(to_left, AXES, down_perm)
    from_left = lax.ppermute(to_right, AXES, up_perm)
    r1 = swap(pay)
    child = jnp.transpose(child_transfer, (1, 2, 0))
    leaf_moments, mid_moments, top_moments = moments(charges, leaf_basis, child, parent_transfer)
    lists = jnp.stack([own_list, from_left[384:392].astype(i32), from_right[384:392].astype(i32)])
    lists = jnp.transpose(lists.reshape(3, 8, 2, 128), (0, 2, 1, 3)).reshape(6144)
    flat = points.reshape(384, 256)
    near_own, near_l, near_r = near(lists, [from_left, from_right, flat, charges])
    back_l = lax.ppermute(near_l, AXES, down_perm)
    back_r = lax.ppermute(near_r, AXES, up_perm)
    r1, near_own, leaf_moments, mid_moments, top_moments = lax.optimization_barrier(
        (r1, near_own, leaf_moments, mid_moments, top_moments)
    )
    ids = r1[:, 27, 0:24].astype(i32).reshape(3072)
    r1 = r1.reshape(4096, 128)
    pay2 = far(ids, r1, nodes_t, nodes_mid, leaf_moments, mid_moments, top_moments)
    r2 = swap(pay2.reshape(128, 5, 2, 128)).reshape(1280, 128)
    return final(far_top, [tab, r1, r2, nodes_top, parent_transfer, near_own, back_l, back_r], leaf_basis, child)


def solution(mesh):
    placed = (
        P(AXES, None),
        P(None, AXES, None),
        P(AXES, None, None),
        P(AXES, None, None),
        P(AXES, None, None),
        P(None, AXES, None),
        P(None, AXES, None),
        P(None, AXES, None),
        P(AXES, None),
        P(AXES, None),
        P(AXES, None),
        P(AXES, None),
    )
    return jax.shard_map(local, mesh=mesh, in_specs=placed, out_specs=P(AXES, None), check_vma=False)
```

```python
import jax
import jax.numpy as jnp
from jax import lax
from jax.experimental import pallas as pl
from jax.experimental.pallas import tpu as pltpu
from jax.sharding import PartitionSpec as P


f32 = jnp.float32
bf16 = jnp.bfloat16
i32 = jnp.int32
soften = 0.25
AXES = ("dom", "sub")
NB = 8
TRANS = (((1,), (1,)), ((), ()))


def dot(a, b):
    return jnp.dot(a, b, preferred_element_type=f32)


def dot_t(a, b):
    return lax.dot_general(a, b, TRANS, preferred_element_type=f32)


def split3(v):
    h = v.astype(bf16).astype(f32)
    r = v - h
    m = r.astype(bf16).astype(f32)
    return h, m, (r - m).astype(bf16).astype(f32)


def iota(shape, dim):
    return lax.broadcasted_iota(i32, shape, dim)


def upper(n):
    return jnp.where(iota((n, n), 0) <= iota((n, n), 1), 1.0, 0.0).astype(bf16)


def slots(owner_rows, wanted_rows, ids, caps):
    width = owner_rows[0].shape[1]
    tri = upper(width)
    half = caps // 2
    r = iota((caps, width), 0)
    slot = jnp.where(r < half, 2 * r, 2 * (r - half) + 1)
    row = jnp.zeros((2 * caps, 128), f32)
    carry = jnp.zeros((128, 1), f32)
    for own, want in zip(owner_rows, wanted_rows):
        hit = jnp.where(own == iota((128, width), 0), 1.0, 0.0)
        hit_b = hit.astype(bf16)
        cum = dot(hit_b, tri) + carry
        carry = cum[:, width - 1 : width]
        rank = jnp.sum(hit * cum, axis=0, keepdims=True).astype(i32) - 1
        place = jnp.where(rank == slot, 1.0, 0.0)
        vals = jnp.concatenate([place * (ids + 1.0), place * (want + 1.0)], axis=0).astype(bf16)
        row = row + dot_t(vals, hit_b)
    return row, carry


def plan_kernel(
    me_ref, far_ref, mid_ref, near_ref, nl_ref, nm_ref, nt_ref, pts_ref, pay_ref, tab_ref, own_ref, hl_ref, hr_ref, oh_ref
):
    me = me_ref[0]
    lane = iota((1, 128), 1)
    ids = lane.astype(f32)
    far = far_ref[...]
    own = far >> 7
    want = (far & 127).astype(f32)
    row, live = slots([own[c : c + 1] for c in range(16)], [want[c : c + 1] for c in range(16)], ids, 16)
    eye = jnp.where(iota((16, 16), 0) == iota((16, 16), 1), 1.0, 0.0).astype(bf16)
    mid = mid_ref[...]
    mown = dot_t(eye, (mid >> 4).astype(f32).astype(bf16)).astype(i32)
    mwant = dot_t(eye, (mid & 15).astype(f32).astype(bf16))
    mrow, mlive = slots(
        [mown[c : c + 1] for c in range(16)], [mwant[c : c + 1] for c in range(16)], ids[:, 0:16], 2
    )
    col = jnp.concatenate([row, mrow, jnp.zeros((92, 128), f32)], axis=0).T
    mcol = col[:, 32:36]
    tab_ref[0:16, :] = row[0:16]
    tab_ref[16:18, :] = mrow[0:2]
    tab_ref[18:32, :] = jnp.zeros((14, 128), f32)
    even, odd = row[0:8], row[8:16]
    line = jnp.broadcast_to(ids + 1.0, (8, 128))
    for o in range(128):
        a = jnp.broadcast_to(even[:, o : o + 1], (8, 128))
        b = jnp.broadcast_to(odd[:, o : o + 1], (8, 128))
        oh_ref[o * 8 : o * 8 + 8, 0:128] = jnp.where(a == line, 1.0, 0.0)
        oh_ref[o * 8 : o * 8 + 8, 128:256] = jnp.where(b == line, 1.0, 0.0)
    oh = oh_ref[...].astype(bf16)
    z = jnp.zeros((64, 128), f32)
    blocks = []
    for c in range(3):
        x = nl_ref[c]
        big = jnp.concatenate([jnp.concatenate([x, z], axis=1), jnp.concatenate([z, x], axis=1)], axis=0)
        blocks += [v.astype(bf16) for v in split3(big)]
    for c in range(3):
        h, m, l = blocks[3 * c : 3 * c + 3]
        both = dot_t(oh, jnp.concatenate([h, m], axis=0))
        pay_ref[:, c * 8 : c * 8 + 8, :] = (both[:, 0:128] + both[:, 128:256]).reshape(128, 8, 128)
    both = dot_t(oh, jnp.concatenate([blocks[2], blocks[5]], axis=0))
    pay_ref[:, 0:8, :] = pay_ref[:, 0:8, :] + both[:, 0:128].reshape(128, 8, 128)
    pay_ref[:, 8:16, :] = pay_ref[:, 8:16, :] + both[:, 128:256].reshape(128, 8, 128)
    pay_ref[:, 16:24, :] = pay_ref[:, 16:24, :] + dot_t(oh, blocks[8]).reshape(128, 8, 128)
    tops = [jnp.concatenate([nt_ref[c, 0:1], nt_ref[c, 1:2]], axis=1) for c in range(3)]
    zero = jnp.zeros((1, 128), f32)
    last = jnp.concatenate([zero] * 4 + tops + [zero], axis=0)
    pay_ref[:, 24:32, :] = jnp.broadcast_to(last[None], (128, 8, 128))
    la = jnp.where(mcol[:, 0:1] == ids[:, 0:16] + 1.0, 1.0, 0.0)
    lb = jnp.where(mcol[:, 1:2] == ids[:, 0:16] + 1.0, 1.0, 0.0)
    ohm = jnp.concatenate([la, lb], axis=1).astype(bf16)
    for c in range(3):
        xm = nm_ref[c]
        zm = jnp.zeros((16, 64), f32)
        bigm = jnp.concatenate([jnp.concatenate([xm, zm], axis=1), jnp.concatenate([zm, xm], axis=1)], axis=0)
        h, m, l = split3(bigm)
        resm = dot(ohm, h.astype(bf16)) + dot(ohm, m.astype(bf16)) + dot(ohm, l.astype(bf16))
        pay_ref[:, 24 + c : 25 + c, :] = resm[:, None, :]
    idrow = jnp.concatenate(
        [col[:, 16:32] - 1.0, mcol[:, 2:4] - 1.0, live, mlive, jnp.zeros((128, 108), f32)], axis=1
    )
    pay_ref[:, 27:28, :] = idrow[:, None, :]
    near = near_ref[...]
    nown = near >> 7
    nloc = (near & 127).astype(f32)
    tri = upper(128)
    outs = []
    for d in (-1, 0, 1):
        hit = jnp.where((nown == me + d) & (near >= 0), 1.0, 0.0)
        cum = dot(hit.astype(bf16), tri)
        base = jnp.zeros((1, 1), f32)
        acc = jnp.zeros((16, 128), f32)
        for c in range(6):
            pos = (cum[c : c + 1] + base).astype(i32) - 1
            base = base + cum[c : c + 1, 127:128]
            bm = jnp.where((pos & 127) == iota((128, 128), 0), hit[c : c + 1], 0.0).astype(bf16)
            am = jnp.where((pos >> 7) == iota((8, 128), 0), 1.0, 0.0)
            vals = jnp.concatenate([am * (ids + 1.0), am * nloc[c : c + 1]], axis=0).astype(bf16)
            acc = acc + dot_t(vals, bm)
        outs.append((jnp.where(iota((8, 128), 0) == 7, base, acc[0:8]), acc[8:16]))
    own_ref[:, 0:128] = outs[1][0].astype(i32)
    own_ref[:, 128:256] = outs[1][1].astype(i32)
    for ref, k in ((hl_ref, 0), (hr_ref, 2)):
        for c in range(3):
            ref[c * 128 : (c + 1) * 128, :] = pts_ref[c]
        ref[384:392, 0:128] = outs[k][0]
        ref[384:392, 128:256] = outs[k][1]


def plan(me, far_t, far_mid, near_t, nodes_t, nodes_mid, nodes_top, points):
    vm = pl.BlockSpec(memory_space=pltpu.VMEM)
    return pl.pallas_call(
        plan_kernel,
        out_shape=(
            jax.ShapeDtypeStruct((128, 32, 128), f32),
            jax.ShapeDtypeStruct((32, 128), f32),
            jax.ShapeDtypeStruct((8, 256), i32),
            jax.ShapeDtypeStruct((392, 256), f32),
            jax.ShapeDtypeStruct((392, 256), f32),
        ),
        in_specs=[pl.BlockSpec(memory_space=pltpu.SMEM)] + [vm] * 7,
        out_specs=(vm,) * 5,
        scratch_shapes=[pltpu.VMEM((1024, 256), f32)],
        compiler_params=pltpu.CompilerParams(vmem_limit_bytes=60 << 20),
        name="plan",
    )(me, far_t, far_mid, near_t, nodes_t, nodes_mid, nodes_top, points)


def dot3(a, b):
    return sum(dot(v.astype(bf16), b) for v in split3(a))


def moments_tail(part, child, q_ref, pt_ref, lm_ref, mm_ref, top_ref, lb_ref, ct_ref):
    lane = iota((64, 128), 1)
    lmt = jnp.zeros((64, 128), f32)
    for k in range(8):
        part(k).wait()

        def leaf(it, acc):
            for u in range(4):
                n = k * 16 + it * 4 + u
                prod = lb_ref[n] * q_ref[pl.ds(n, 1), :]
                col = jnp.sum(prod[:, 0:128] + prod[:, 128:256], axis=1, keepdims=True)
                acc = jnp.where(lane == n, col, acc)
            return acc

        lmt = lax.fori_loop(0, 4, leaf, lmt)
    lm_ref[...] = lmt.T
    child.wait()
    rows = []
    for i in range(64):
        rows.append(jnp.sum(ct_ref[i] * lmt, axis=0, keepdims=True))
    per_leaf = jnp.concatenate(rows, axis=0)
    group = jnp.where((iota((128, 128), 0) >> 3) == iota((128, 128), 1), 1.0, 0.0).astype(bf16)
    mm = dot3(per_leaf, group).T
    mm_ref[...] = mm[0:16, :]
    tops = []
    for g in range(2):
        acc = jnp.zeros((64, 64), f32)
        for c in range(g * 8, g * 8 + 8):
            acc = acc + pt_ref[c] * mm[c : c + 1, :]
        tops.append(jnp.broadcast_to(jnp.sum(acc, axis=1, keepdims=True), (64, 128)).T[0:1])
    top_ref[...] = jnp.concatenate(tops, axis=1)


def tile_rows(x, y, z, a, b):
    r = iota((8, 256), 0)
    v = jnp.where(r == 0, x, jnp.where(r == 1, y, jnp.where(r == 2, z, jnp.where(r == 3, a, b))))
    return jnp.where(r < 5, v, 0.0)


def near_tables(pts_ref, q_ref, sf_ref, qb_ref):
    r = iota((64, 128), 0)
    spread = jnp.where((r >= 48) & (r < 51), 1.0, 0.0).astype(bf16)
    r8 = iota((8, 256), 0)

    def prepare(it, carry):
        for u in range(8):
            n = it * 8 + u
            x = pts_ref[pl.ds(n, 1), :]
            y = pts_ref[pl.ds(128 + n, 1), :]
            z = pts_ref[pl.ds(256 + n, 1), :]
            norm = x * x + y * y + z * z + soften
            h, m, l = split3(tile_rows(x, y, z, jnp.ones_like(x), norm))
            qh, qm, ql = split3(jnp.broadcast_to(q_ref[pl.ds(n, 1), :], (8, 256)))
            q = jnp.where(r8 == 0, qh, jnp.where(r8 == 1, qm, jnp.where(r8 == 2, ql, 0.0)))
            t = jnp.concatenate([h, m, l, h, m, h, q, jnp.zeros_like(q)], axis=0).T.astype(bf16)
            sf_ref[n] = t
            qb_ref[n] = dot(t, spread)
        return carry

    lax.fori_loop(0, 16, prepare, 0)


def near_pairs(entry, total, tgt, sf_ref, qb_ref, rhs_ref, d_ref, acc_ref):
    def factors(i, u):
        lv, _ = entry(i)
        lrow = jnp.maximum(lv - 1, 0)
        x = tgt[pl.ds(lrow, 1), :]
        y = tgt[pl.ds(128 + lrow, 1), :]
        z = tgt[pl.ds(256 + lrow, 1), :]
        norm = x * x + y * y + z * z
        h, m, l = split3(tile_rows(-2.0 * x, -2.0 * y, -2.0 * z, norm, jnp.ones_like(x)))
        rhs_ref[u] = jnp.concatenate([h, h, h, m, m, l], axis=0).astype(bf16)

    def distances(i, u):
        _, n = entry(i)
        d_ref[u] = dot(sf_ref[n, :, 0:48], rhs_ref[u])

    def sums(i, u):
        lv, n = entry(i)
        acc = jnp.zeros((8, 256), f32)
        for j in range(0, 256, 64):
            w = lax.rsqrt(d_ref[u, j : j + 64, :])
            q = qb_ref[n, j : j + 64, :]
            acc = acc + jnp.sum((w * jnp.concatenate([q, q], axis=1)).reshape(8, 8, 256), axis=0)
        row = jnp.where(lv > 0, lv - 1, 128)
        return row, jnp.sum(acc, axis=0, keepdims=True)

    for u in range(NB):
        factors(u, u)
    for u in range(NB):
        distances(u, u)
        factors(NB + u, u)

    def step(it, carry):
        i = it * NB
        got = [sums(i + u, u) for u in range(NB)]
        for u in range(NB):
            distances(i + NB + u, u)
        for u in range(NB):
            factors(i + 2 * NB + u, u)
        for row, val in got:
            acc_ref[pl.ds(row, 1), :] = acc_ref[pl.ds(row, 1), :] + val
        return carry

    lax.fori_loop(0, (total + NB - 1) // NB, step, 0)


def near_kernel(
    lst, tgt_l, tgt_r, pts_ref, q_ref, pt_ref, lb_hbm, ct_hbm,
    out_own, out_l, out_r, lm_ref, mm_ref, top_ref,
    sf_ref, qb_ref, rhs_ref, d_ref, acc_ref, lb_ref, ct_ref, sem,
):
    def part(k):
        rows = pl.ds(k * 16, 16)
        return pltpu.make_async_copy(lb_hbm.at[rows], lb_ref.at[rows], sem.at[k])

    child = pltpu.make_async_copy(ct_hbm, ct_ref, sem.at[8])
    for k in range(8):
        part(k).start()
    child.start()
    near_tables(pts_ref, q_ref, sf_ref, qb_ref)
    for k, (tgt, out) in enumerate(((pts_ref, out_own), (tgt_l, out_l), (tgt_r, out_r))):
        acc_ref[...] = jnp.zeros((136, 256), f32)
        skip = 128 if k == 0 else 0

        def entry(i, first=k * 2048 + skip):
            return lst[first + i], lst[first + 1024 + i]

        near_pairs(entry, lst[k * 2048 + 896] - skip, tgt, sf_ref, qb_ref, rhs_ref, d_ref, acc_ref)
        out[...] = acc_ref[0:128, :]
    moments_tail(part, child, q_ref, pt_ref, lm_ref, mm_ref, top_ref, lb_ref, ct_ref)


def near(lists, arrays, leaf_basis, child):
    vm = pl.BlockSpec(memory_space=pltpu.VMEM)
    hbm = pl.BlockSpec(memory_space=pl.ANY)
    return pl.pallas_call(
        near_kernel,
        out_shape=tuple(jax.ShapeDtypeStruct((128, 256), f32) for _ in range(3))
        + (
            jax.ShapeDtypeStruct((128, 64), f32),
            jax.ShapeDtypeStruct((16, 64), f32),
            jax.ShapeDtypeStruct((1, 128), f32),
        ),
        in_specs=[pl.BlockSpec(memory_space=pltpu.SMEM)] + [vm] * 5 + [hbm] * 2,
        out_specs=(vm,) * 6,
        scratch_shapes=[
            pltpu.VMEM((128, 256, 64), bf16),
            pltpu.VMEM((128, 256, 128), f32),
            pltpu.VMEM((NB, 48, 256), bf16),
            pltpu.VMEM((NB, 256, 256), f32),
            pltpu.VMEM((136, 256), f32),
            pltpu.VMEM((128, 64, 256), f32),
            pltpu.VMEM((64, 64, 128), f32),
            pltpu.SemaphoreType.DMA((9,)),
        ],
        compiler_params=pltpu.CompilerParams(vmem_limit_bytes=60 << 20),
        name="near",
    )(lists, *arrays, leaf_basis, child)


def near_self_kernel(pts_ref, q_ref, part_ref, out, sf_ref, qb_ref, rhs_ref, d_ref, acc_ref):
    near_tables(pts_ref, q_ref, sf_ref, qb_ref)
    acc_ref[0:128, :] = part_ref[...]
    acc_ref[128:136, :] = jnp.zeros((8, 256), f32)

    def entry(i):
        n = jnp.minimum(i, 127)
        return n + 1, n

    near_pairs(entry, 128, pts_ref, sf_ref, qb_ref, rhs_ref, d_ref, acc_ref)
    out[...] = acc_ref[0:128, :]


def near_self(points, charges, part):
    vm = pl.BlockSpec(memory_space=pltpu.VMEM)
    return pl.pallas_call(
        near_self_kernel,
        out_shape=jax.ShapeDtypeStruct((128, 256), f32),
        in_specs=[vm] * 3,
        out_specs=vm,
        scratch_shapes=[
            pltpu.VMEM((128, 256, 64), bf16),
            pltpu.VMEM((128, 256, 128), f32),
            pltpu.VMEM((NB, 48, 256), bf16),
            pltpu.VMEM((NB, 256, 256), f32),
            pltpu.VMEM((136, 256), f32),
        ],
        compiler_params=pltpu.CompilerParams(vmem_limit_bytes=60 << 20),
        name="near_self",
    )(points, charges, part)


def halves(x):
    h = x.astype(bf16).astype(f32)
    return h, (x - h).astype(bf16).astype(f32)


def features(x, y, z, source):
    parts = [halves(v) for v in (x, y, z)]
    norm = sum((h + m) * (h + m) for h, m in parts)
    one = jnp.ones_like(x)
    if source:
        nh, nm = halves(norm + soften)
        return [v for h, m in parts for v in (h, m, h, m)] + [one, one, nh, nm]
    nh, nm = halves(norm)
    return [v for h, m in parts for v in (-2.0 * h, -2.0 * h, -2.0 * m, -2.0 * m)] + [nh, nm, one, one]


def far_kernel(
    ids_ref, r1_ref, nl_ref, nm_ref, lm_ref, mm_ref, top_ref, out_ref, v_ref, u_ref, rep_ref, one_ref, mask_ref, ra_ref, mb_ref, full_ref
):
    for c in range(8):
        r = iota((128, 128), 0) - c * 16
        k = iota((128, 128), 1)
        lanes = slice((c % 2) * 128, (c % 2) * 128 + 128)
        rep_ref[c // 2, :, lanes] = jnp.where(r == (k >> 3), 1.0, 0.0).astype(bf16)
        one_ref[c // 2, :, lanes] = jnp.where((r >= 0) & (r < 3), 1.0, 0.0).astype(bf16)
        mask_ref[c] = jnp.where((iota((64, 128), 1) & 7) == c, 1.0, 0.0).astype(bf16)
    u_ref[...] = jnp.zeros((18 * 128, 64), f32)
    leaf = features(nl_ref[0].T, nl_ref[1].T, nl_ref[2].T, True)
    mid = features(nm_ref[0], nm_ref[1], nm_ref[2], True)
    for f in range(16):
        for blk in range(16):
            v_ref[pl.ds(blk * 128 + f, 8, stride=16), :] = leaf[f][blk * 8 : blk * 8 + 8]
        for blk in range(2):
            v_ref[pl.ds((16 + blk) * 128 + f, 8, stride=16), :] = mid[f][blk * 8 : blk * 8 + 8]

    for blk in range(18):
        src = lm_ref[blk * 8 : blk * 8 + 8, :] if blk < 16 else mm_ref[blk * 8 - 128 : blk * 8 - 120, :]
        for f, v in enumerate(split3(src)):
            u_ref[pl.ds(blk * 128 + f, 8, stride=16), :] = v

    def prepare(it, carry):
        for blk in (it * 3, it * 3 + 1, it * 3 + 2):
            rows = pl.ds(pl.multiple_of(blk * 128, 128), 128)
            v = v_ref[rows, :].T.astype(bf16)
            u = u_ref[rows, :].T.astype(bf16)
            for i in range(4):
                both = dot(v, rep_ref[i]).astype(bf16)
                ra_ref[blk * 8 + 2 * i] = both[:, 0:128]
                ra_ref[blk * 8 + 2 * i + 1] = both[:, 128:256]
                both = dot(u, one_ref[i])
                mb_ref[blk * 8 + 2 * i] = both[:, 0:128]
                mb_ref[blk * 8 + 2 * i + 1] = both[:, 128:256]
        return carry

    lax.fori_loop(0, 6, prepare, 0)
    low = iota((128, 128), 1) < 64
    low64 = iota((64, 128), 1) < 64

    def weights(x, y, z):
        tf = jnp.concatenate(features(x, y, z, False), axis=0)
        return jnp.concatenate([jnp.where(low, tf, 0.0), jnp.where(low, 0.0, tf)], axis=0).astype(bf16)

    def group(rhs, g, t0, t1):
        t0 = jnp.maximum(t0, 0)
        t1 = jnp.maximum(t1, 0)
        mask = mask_ref[g]
        lhs = jnp.concatenate([ra_ref[t0] * mask, ra_ref[t1] * mask], axis=1)
        m = jnp.where(low64, mb_ref[t0], mb_ref[t1])
        w = lax.rsqrt(dot(lhs, rhs)) * m
        return jnp.sum(jnp.sum(w.reshape(8, 8, 128), axis=0), axis=0, keepdims=True)

    def leaf_groups(p, groups):
        rhs = weights(*(r1_ref[pl.ds(pl.multiple_of(p * 32 + 8 * c, 8), 8), :] for c in range(3)))
        return [(p, g, group(rhs, g, ids_ref[p * 24 + g], ids_ref[p * 24 + 8 + g])) for g in groups]

    out_ref[...] = jnp.zeros((1280, 128), f32)
    out_ref[pl.ds(9, 128, stride=10), :] = jnp.broadcast_to(top_ref[...], (128, 128))

    def first(it, carry):
        got = []
        for u in range(4):
            got += leaf_groups(it * 4 + u, range(4))
        for p, g, val in got:
            out_ref[pl.ds(p * 10 + g, 1), :] = val
        return carry

    lax.fori_loop(0, 32, first, 0)

    def scan(it, pos):
        for u in range(8):
            p = it * 8 + u
            full_ref[pos] = p
            pos = pos + (ids_ref[p * 24 + 18] > 8).astype(i32)
        return pos

    full = lax.fori_loop(0, 16, scan, jnp.int32(0))
    full_ref[full] = 0

    def second(it, carry):
        got = []
        for u in range(2):
            got += leaf_groups(full_ref[it * 2 + u], range(4, 8))
        for p, g, val in got:
            out_ref[pl.ds(p * 10 + g, 1), :] = val
        return carry

    lax.fori_loop(0, (full + 1) // 2, second, 0)

    def mids(it, carry):
        got = []
        for u in range(2):
            b = (it * 2 + u) * 256 + 24
            rhs = weights(*(r1_ref[pl.ds(b + c, 8, stride=32), :] for c in range(3)))
            for g in range(8):
                p = (it * 2 + u) * 8 + g
                got.append((p, group(rhs, g, 128 + ids_ref[p * 24 + 16], 128 + ids_ref[p * 24 + 17])))
        for p, val in got:
            out_ref[pl.ds(p * 10 + 8, 1), :] = val
        return carry

    lax.fori_loop(0, 8, mids, 0)


def far(ids, r1, nodes_t, nodes_mid, moments, mid_moments, top_row):
    vm = pl.BlockSpec(memory_space=pltpu.VMEM)
    return pl.pallas_call(
        far_kernel,
        out_shape=jax.ShapeDtypeStruct((1280, 128), f32),
        in_specs=[pl.BlockSpec(memory_space=pltpu.SMEM)] + [vm] * 6,
        out_specs=vm,
        scratch_shapes=[
            pltpu.VMEM((18 * 128, 64), f32),
            pltpu.VMEM((18 * 128, 64), f32),
            pltpu.VMEM((4, 128, 256), bf16),
            pltpu.VMEM((4, 128, 256), bf16),
            pltpu.VMEM((8, 64, 128), bf16),
            pltpu.VMEM((144, 64, 128), bf16),
            pltpu.VMEM((144, 64, 128), f32),
            pltpu.SMEM((136,), i32),
        ],
        compiler_params=pltpu.CompilerParams(vmem_limit_bytes=60 << 20),
        name="far",
    )(ids, r1, nodes_t, nodes_mid, moments, mid_moments, top_row)


def final_kernel(
    top_ids, tab_ref, r1_ref, r2_ref, nt_ref, pt_ref, near_ref, bl_ref, br_ref, lb_hbm, ct_hbm, out_ref, lb_ref, ct_ref, sem
):
    def part(k):
        rows = pl.ds(k * 16, 16)
        return pltpu.make_async_copy(lb_hbm.at[rows], lb_ref.at[rows], sem.at[k])

    child = pltpu.make_async_copy(ct_hbm, ct_ref, sem.at[8])
    child.start()
    for k in range(8):
        part(k).start()
    tag = (iota((128, 128), 0) + 1).astype(f32)

    def lines(k, rows):
        return jnp.where(tab_ref[k : k + 1, :] == tag[0:rows], 1.0, 0.0)

    def two(x):
        return jnp.concatenate(halves(x), axis=1).astype(bf16)

    acc = [jnp.zeros((128, 256), f32), jnp.zeros((128, 256), f32)]
    for g in range(0, 8, 2):
        vals = jnp.concatenate([two(r2_ref[pl.ds(g + k, 128, stride=10), :]) for k in range(2)], axis=0)
        for h in range(2):
            oh = jnp.concatenate([lines(8 * h + g, 128), lines(8 * h + g + 1, 128)], axis=1).astype(bf16)
            acc[h] = acc[h] + dot(oh, vals)
    acc = [a[:, 0:128] + a[:, 128:256] for a in acc]
    local_t = acc[0].T[0:64] + acc[1].T[64:128]
    vals = two(r2_ref[pl.ds(8, 128, stride=10), :])
    res = [dot(lines(16 + h, 16).astype(bf16), vals) for h in range(2)]
    res = [a[:, 0:128] + a[:, 128:256] for a in res]
    mid_local = res[0][:, 0:64] + res[1][:, 64:128]
    half = iota((1, 128), 1) >> 6
    pad = jnp.zeros((6, 64), f32)
    cols = [jnp.concatenate([nt_ref[c], pad], axis=0).T for c in range(3)]
    rows = []
    for g in range(2):
        tx, ty, tz = (jnp.broadcast_to(cols[c][:, g : g + 1], (64, 128)) for c in range(3))

        def entry(it, total):
            for u in range(4):
                t = top_ids[g, it * 4 + u]
                p = jnp.maximum(t, 0) >> 1
                h = jnp.where(t < 0, 2, t & 1)
                m = jnp.where(half == h, r2_ref[pl.ds(p * 10 + 9, 1), :], 0.0)
                dx = tx - r1_ref[pl.ds(p * 32 + 28, 1), :]
                dy = ty - r1_ref[pl.ds(p * 32 + 29, 1), :]
                dz = tz - r1_ref[pl.ds(p * 32 + 30, 1), :]
                total = total + lax.rsqrt(dx * dx + dy * dy + dz * dz + soften) * m
            return total

        total = lax.fori_loop(0, 4, entry, jnp.zeros((64, 128), f32))
        top = jnp.broadcast_to(jnp.sum(total, axis=1, keepdims=True), (64, 64))
        for c in range(g * 8, g * 8 + 8):
            rows.append(jnp.sum(pt_ref[c] * top, axis=0, keepdims=True))
    mid_down = mid_local + jnp.concatenate(rows, axis=0)
    mid_t = jnp.concatenate([mid_down, jnp.zeros((112, 64), f32)], axis=0).T
    spread = jnp.where(iota((128, 128), 0) == (iota((128, 128), 1) >> 3), 1.0, 0.0).astype(bf16)
    mid_t = dot3(mid_t, spread)
    child.wait()
    down = local_t
    for i in range(64):
        down = down + ct_ref[i] * mid_t[i : i + 1, :]
    h, m = halves(down)
    pick = jnp.where((iota((32, 2048), 0) & 15) == (iota((32, 2048), 1) >> 7), 1.0, 0.0).astype(bf16)
    for k in range(8):
        part(k).wait()
        ks = slice(16 * k, 16 * k + 16)
        cols16 = dot(jnp.concatenate([h[:, ks], m[:, ks]], axis=1).astype(bf16), pick)
        for u in range(16):
            d = cols16[:, u * 128 : u * 128 + 128]
            n = 16 * k + u
            out_ref[n : n + 1, :] = jnp.sum(lb_ref[n] * jnp.concatenate([d, d], axis=1), axis=0, keepdims=True)
    out_ref[...] = out_ref[...] + near_ref[...] + bl_ref[...] + br_ref[...]


def final(far_top, arrays, leaf_basis, child):
    vm = pl.BlockSpec(memory_space=pltpu.VMEM)
    hbm = pl.BlockSpec(memory_space=pl.ANY)
    return pl.pallas_call(
        final_kernel,
        out_shape=jax.ShapeDtypeStruct((128, 256), f32),
        in_specs=[pl.BlockSpec(memory_space=pltpu.SMEM)] + [vm] * 8 + [hbm] * 2,
        out_specs=vm,
        scratch_shapes=[
            pltpu.VMEM((128, 64, 256), f32),
            pltpu.VMEM((64, 64, 128), f32),
            pltpu.SemaphoreType.DMA((9,)),
        ],
        compiler_params=pltpu.CompilerParams(vmem_limit_bytes=60 << 20),
        name="final",
    )(far_top, *arrays, leaf_basis, child)


def swap(x):
    return lax.all_to_all(x, AXES, split_axis=0, concat_axis=0, tiled=True)


def local(
    charges,
    points,
    leaf_basis,
    child_transfer,
    parent_transfer,
    nodes_leaf,
    nodes_mid,
    nodes_top,
    near_list,
    far_leaf,
    far_mid,
    far_top,
):
    shards = lax.axis_size(AXES)
    me = lax.axis_index(AXES).astype(i32).reshape(1)
    down_perm = [(i + 1, i) for i in range(shards - 1)]
    up_perm = [(i, i + 1) for i in range(shards - 1)]
    nodes_t = jnp.transpose(nodes_leaf, (0, 2, 1))
    pay, tab, own_list, to_left, to_right = plan(
        me, far_leaf.T, far_mid, near_list.T, nodes_t, nodes_mid, nodes_top, points
    )
    from_right = lax.ppermute(to_left, AXES, down_perm)
    from_left = lax.ppermute(to_right, AXES, up_perm)
    r1 = swap(pay)
    child = jnp.transpose(child_transfer, (1, 2, 0))
    lists = jnp.stack([own_list, from_left[384:392].astype(i32), from_right[384:392].astype(i32)])
    lists = jnp.transpose(lists.reshape(3, 8, 2, 128), (0, 2, 1, 3)).reshape(6144)
    flat = points.reshape(384, 256)
    near_own, near_l, near_r, leaf_moments, mid_moments, top_moments = near(
        lists, [from_left, from_right, flat, charges, parent_transfer], leaf_basis, child
    )
    back_l = lax.ppermute(near_l, AXES, down_perm)
    back_r = lax.ppermute(near_r, AXES, up_perm)
    r1, near_own, leaf_moments, mid_moments, top_moments = lax.optimization_barrier(
        (r1, near_own, leaf_moments, mid_moments, top_moments)
    )
    ids = r1[:, 27, 0:24].astype(i32).reshape(3072)
    r1 = r1.reshape(4096, 128)
    pay2 = far(ids, r1, nodes_t, nodes_mid, leaf_moments, mid_moments, top_moments)
    r2 = swap(pay2.reshape(128, 5, 2, 128)).reshape(1280, 128)
    near_own = near_self(flat, charges, near_own)
    return final(far_top, [tab, r1, r2, nodes_top, parent_transfer, near_own, back_l, back_r], leaf_basis, child)


def solution(mesh):
    placed = (
        P(AXES, None),
        P(None, AXES, None),
        P(AXES, None, None),
        P(AXES, None, None),
        P(AXES, None, None),
        P(None, AXES, None),
        P(None, AXES, None),
        P(None, AXES, None),
        P(AXES, None),
        P(AXES, None),
        P(AXES, None),
        P(AXES, None),
    )
    return jax.shard_map(local, mesh=mesh, in_specs=placed, out_specs=P(AXES, None), check_vma=False)
```

```python
import jax
import jax.numpy as jnp
from jax import lax
from jax.experimental import pallas as pl
from jax.experimental.pallas import tpu as pltpu
from jax.sharding import PartitionSpec as P


f32 = jnp.float32
bf16 = jnp.bfloat16
i32 = jnp.int32
soften = 0.25
AXES = ("dom", "sub")
NB = 8
SELF = 32
TRANS = (((1,), (1,)), ((), ()))


def dot(a, b):
    return jnp.dot(a, b, preferred_element_type=f32)


def dot_t(a, b):
    return lax.dot_general(a, b, TRANS, preferred_element_type=f32)


def split3(v):
    h = v.astype(bf16).astype(f32)
    r = v - h
    m = r.astype(bf16).astype(f32)
    return h, m, (r - m).astype(bf16).astype(f32)


def iota(shape, dim):
    return lax.broadcasted_iota(i32, shape, dim)


def upper(n):
    return jnp.where(iota((n, n), 0) <= iota((n, n), 1), 1.0, 0.0).astype(bf16)


def slots(owner_rows, wanted_rows, ids, caps):
    width = owner_rows[0].shape[1]
    tri = upper(width)
    half = caps // 2
    r = iota((caps, width), 0)
    slot = jnp.where(r < half, 2 * r, 2 * (r - half) + 1)
    row = jnp.zeros((2 * caps, 128), f32)
    carry = jnp.zeros((128, 1), f32)
    for own, want in zip(owner_rows, wanted_rows):
        hit = jnp.where(own == iota((128, width), 0), 1.0, 0.0)
        hit_b = hit.astype(bf16)
        cum = dot(hit_b, tri) + carry
        carry = cum[:, width - 1 : width]
        rank = jnp.sum(hit * cum, axis=0, keepdims=True).astype(i32) - 1
        place = jnp.where(rank == slot, 1.0, 0.0)
        vals = jnp.concatenate([place * (ids + 1.0), place * (want + 1.0)], axis=0).astype(bf16)
        row = row + dot_t(vals, hit_b)
    return row, carry


def plan_kernel(
    me_ref, far_ref, mid_ref, near_ref, nl_ref, nm_ref, nt_ref, pts_ref, pay_ref, tab_ref, own_ref, hl_ref, hr_ref, oh_ref
):
    me = me_ref[0]
    lane = iota((1, 128), 1)
    ids = lane.astype(f32)
    far = far_ref[...]
    own = far >> 7
    want = (far & 127).astype(f32)
    row, live = slots([own[c : c + 1] for c in range(16)], [want[c : c + 1] for c in range(16)], ids, 16)
    eye = jnp.where(iota((16, 16), 0) == iota((16, 16), 1), 1.0, 0.0).astype(bf16)
    mid = mid_ref[...]
    mown = dot_t(eye, (mid >> 4).astype(f32).astype(bf16)).astype(i32)
    mwant = dot_t(eye, (mid & 15).astype(f32).astype(bf16))
    mrow, mlive = slots(
        [mown[c : c + 1] for c in range(16)], [mwant[c : c + 1] for c in range(16)], ids[:, 0:16], 2
    )
    col = jnp.concatenate([row, mrow, jnp.zeros((92, 128), f32)], axis=0).T
    mcol = col[:, 32:36]
    tab_ref[0:16, :] = row[0:16]
    tab_ref[16:18, :] = mrow[0:2]
    tab_ref[18:32, :] = jnp.zeros((14, 128), f32)
    even, odd = row[0:8], row[8:16]
    line = jnp.broadcast_to(ids + 1.0, (8, 128))
    for o in range(128):
        a = jnp.broadcast_to(even[:, o : o + 1], (8, 128))
        b = jnp.broadcast_to(odd[:, o : o + 1], (8, 128))
        oh_ref[o * 8 : o * 8 + 8, 0:128] = jnp.where(a == line, 1.0, 0.0)
        oh_ref[o * 8 : o * 8 + 8, 128:256] = jnp.where(b == line, 1.0, 0.0)
    oh = oh_ref[...].astype(bf16)
    z = jnp.zeros((64, 128), f32)
    blocks = []
    for c in range(3):
        x = nl_ref[c]
        big = jnp.concatenate([jnp.concatenate([x, z], axis=1), jnp.concatenate([z, x], axis=1)], axis=0)
        blocks += [v.astype(bf16) for v in split3(big)]
    for c in range(3):
        h, m, l = blocks[3 * c : 3 * c + 3]
        both = dot_t(oh, jnp.concatenate([h, m], axis=0))
        pay_ref[:, c * 8 : c * 8 + 8, :] = (both[:, 0:128] + both[:, 128:256]).reshape(128, 8, 128)
    both = dot_t(oh, jnp.concatenate([blocks[2], blocks[5]], axis=0))
    pay_ref[:, 0:8, :] = pay_ref[:, 0:8, :] + both[:, 0:128].reshape(128, 8, 128)
    pay_ref[:, 8:16, :] = pay_ref[:, 8:16, :] + both[:, 128:256].reshape(128, 8, 128)
    pay_ref[:, 16:24, :] = pay_ref[:, 16:24, :] + dot_t(oh, blocks[8]).reshape(128, 8, 128)
    tops = [jnp.concatenate([nt_ref[c, 0:1], nt_ref[c, 1:2]], axis=1) for c in range(3)]
    zero = jnp.zeros((1, 128), f32)
    last = jnp.concatenate([zero] * 4 + tops + [zero], axis=0)
    pay_ref[:, 24:32, :] = jnp.broadcast_to(last[None], (128, 8, 128))
    la = jnp.where(mcol[:, 0:1] == ids[:, 0:16] + 1.0, 1.0, 0.0)
    lb = jnp.where(mcol[:, 1:2] == ids[:, 0:16] + 1.0, 1.0, 0.0)
    ohm = jnp.concatenate([la, lb], axis=1).astype(bf16)
    for c in range(3):
        xm = nm_ref[c]
        zm = jnp.zeros((16, 64), f32)
        bigm = jnp.concatenate([jnp.concatenate([xm, zm], axis=1), jnp.concatenate([zm, xm], axis=1)], axis=0)
        h, m, l = split3(bigm)
        resm = dot(ohm, h.astype(bf16)) + dot(ohm, m.astype(bf16)) + dot(ohm, l.astype(bf16))
        pay_ref[:, 24 + c : 25 + c, :] = resm[:, None, :]
    idrow = jnp.concatenate(
        [col[:, 16:32] - 1.0, mcol[:, 2:4] - 1.0, live, mlive, jnp.zeros((128, 108), f32)], axis=1
    )
    pay_ref[:, 27:28, :] = idrow[:, None, :]
    near = near_ref[...]
    nown = near >> 7
    nloc = (near & 127).astype(f32)
    tri = upper(128)
    outs = []
    for d in (-1, 0, 1):
        hit = jnp.where((nown == me + d) & (near >= 0), 1.0, 0.0)
        cum = dot(hit.astype(bf16), tri)
        base = jnp.zeros((1, 1), f32)
        acc = jnp.zeros((16, 128), f32)
        for c in range(6):
            pos = (cum[c : c + 1] + base).astype(i32) - 1
            base = base + cum[c : c + 1, 127:128]
            bm = jnp.where((pos & 127) == iota((128, 128), 0), hit[c : c + 1], 0.0).astype(bf16)
            am = jnp.where((pos >> 7) == iota((8, 128), 0), 1.0, 0.0)
            vals = jnp.concatenate([am * (ids + 1.0), am * nloc[c : c + 1]], axis=0).astype(bf16)
            acc = acc + dot_t(vals, bm)
        outs.append((jnp.where(iota((8, 128), 0) == 7, base, acc[0:8]), acc[8:16]))
    own_ref[:, 0:128] = outs[1][0].astype(i32)
    own_ref[:, 128:256] = outs[1][1].astype(i32)
    for ref, k in ((hl_ref, 0), (hr_ref, 2)):
        for c in range(3):
            ref[c * 128 : (c + 1) * 128, :] = pts_ref[c]
        ref[384:392, 0:128] = outs[k][0]
        ref[384:392, 128:256] = outs[k][1]


def plan(me, far_t, far_mid, near_t, nodes_t, nodes_mid, nodes_top, points):
    vm = pl.BlockSpec(memory_space=pltpu.VMEM)
    return pl.pallas_call(
        plan_kernel,
        out_shape=(
            jax.ShapeDtypeStruct((128, 32, 128), f32),
            jax.ShapeDtypeStruct((32, 128), f32),
            jax.ShapeDtypeStruct((8, 256), i32),
            jax.ShapeDtypeStruct((392, 256), f32),
            jax.ShapeDtypeStruct((392, 256), f32),
        ),
        in_specs=[pl.BlockSpec(memory_space=pltpu.SMEM)] + [vm] * 7,
        out_specs=(vm,) * 5,
        scratch_shapes=[pltpu.VMEM((1024, 256), f32)],
        compiler_params=pltpu.CompilerParams(vmem_limit_bytes=60 << 20),
        name="plan",
    )(me, far_t, far_mid, near_t, nodes_t, nodes_mid, nodes_top, points)


def dot3(a, b):
    return sum(dot(v.astype(bf16), b) for v in split3(a))


def moments_tail(part, child, q_ref, pt_ref, lm_ref, mm_ref, top_ref, lb_ref, ct_ref):
    lane = iota((64, 128), 1)
    lmt = jnp.zeros((64, 128), f32)
    for k in range(8):
        part(k).wait()

        def leaf(it, acc):
            for u in range(4):
                n = k * 16 + it * 4 + u
                prod = lb_ref[n] * q_ref[pl.ds(n, 1), :]
                col = jnp.sum(prod[:, 0:128] + prod[:, 128:256], axis=1, keepdims=True)
                acc = jnp.where(lane == n, col, acc)
            return acc

        lmt = lax.fori_loop(0, 4, leaf, lmt)
    lm_ref[...] = lmt.T
    child.wait()
    rows = []
    for i in range(64):
        rows.append(jnp.sum(ct_ref[i] * lmt, axis=0, keepdims=True))
    per_leaf = jnp.concatenate(rows, axis=0)
    group = jnp.where((iota((128, 128), 0) >> 3) == iota((128, 128), 1), 1.0, 0.0).astype(bf16)
    mm = dot3(per_leaf, group).T
    mm_ref[...] = mm[0:16, :]
    tops = []
    for g in range(2):
        acc = jnp.zeros((64, 64), f32)
        for c in range(g * 8, g * 8 + 8):
            acc = acc + pt_ref[c] * mm[c : c + 1, :]
        tops.append(jnp.broadcast_to(jnp.sum(acc, axis=1, keepdims=True), (64, 128)).T[0:1])
    top_ref[...] = jnp.concatenate(tops, axis=1)


def tile_rows(x, y, z, a, b):
    r = iota((8, 256), 0)
    v = jnp.where(r == 0, x, jnp.where(r == 1, y, jnp.where(r == 2, z, jnp.where(r == 3, a, b))))
    return jnp.where(r < 5, v, 0.0)


def near_tables(pts_ref, q_ref, sf_ref, qb_ref, count):
    r = iota((64, 128), 0)
    spread = jnp.where((r >= 48) & (r < 51), 1.0, 0.0).astype(bf16)
    r8 = iota((8, 256), 0)

    def factors(n):
        x = pts_ref[pl.ds(n, 1), :]
        y = pts_ref[pl.ds(128 + n, 1), :]
        z = pts_ref[pl.ds(256 + n, 1), :]
        norm = x * x + y * y + z * z + soften
        h, m, l = split3(tile_rows(x, y, z, jnp.ones_like(x), norm))
        qh, qm, ql = split3(jnp.broadcast_to(q_ref[pl.ds(n, 1), :], (8, 256)))
        q = jnp.where(r8 == 0, qh, jnp.where(r8 == 1, qm, jnp.where(r8 == 2, ql, 0.0)))
        return jnp.concatenate([h, m, l, h, m, h, q, jnp.zeros_like(q)], axis=0).T.astype(bf16)

    for n in range(8):
        sf_ref[n] = factors(n)

    def prepare(it, carry):
        for u in range(8):
            qb_ref[it * 8 + u] = dot(sf_ref[it * 8 + u], spread)
        ahead = jnp.minimum(it + 1, count // 8 - 1)
        made = [factors(ahead * 8 + u) for u in range(8)]
        for u in range(8):
            sf_ref[ahead * 8 + u] = made[u]
        return carry

    lax.fori_loop(0, count // 8, prepare, 0)


def near_pairs(entry, total, tgt, sf_ref, qb_ref, rhs_ref, d_ref, acc_ref):
    def factors(i, u):
        lv, _ = entry(i)
        lrow = jnp.maximum(lv - 1, 0)
        x = tgt[pl.ds(lrow, 1), :]
        y = tgt[pl.ds(128 + lrow, 1), :]
        z = tgt[pl.ds(256 + lrow, 1), :]
        norm = x * x + y * y + z * z
        h, m, l = split3(tile_rows(-2.0 * x, -2.0 * y, -2.0 * z, norm, jnp.ones_like(x)))
        rhs_ref[u] = jnp.concatenate([h, h, h, m, m, l], axis=0).astype(bf16)

    def distances(i, u):
        _, n = entry(i)
        d_ref[u] = dot(sf_ref[n, :, 0:48], rhs_ref[u])

    def sums(i, u):
        lv, n = entry(i)
        acc = jnp.zeros((8, 256), f32)
        for j in range(0, 256, 64):
            w = lax.rsqrt(d_ref[u, j : j + 64, :])
            q = qb_ref[n, j : j + 64, :]
            acc = acc + jnp.sum((w * jnp.concatenate([q, q], axis=1)).reshape(8, 8, 256), axis=0)
        row = jnp.where(lv > 0, lv - 1, 128)
        return row, jnp.sum(acc, axis=0, keepdims=True)

    for u in range(NB):
        factors(u, u)
    for u in range(NB):
        distances(u, u)
        factors(NB + u, u)

    def step(it, carry):
        i = it * NB
        got = [sums(i + u, u) for u in range(NB)]
        for u in range(NB):
            distances(i + NB + u, u)
        for u in range(NB):
            factors(i + 2 * NB + u, u)
        for row, val in got:
            acc_ref[pl.ds(row, 1), :] = acc_ref[pl.ds(row, 1), :] + val
        return carry

    lax.fori_loop(0, (total + NB - 1) // NB, step, 0)


def near_kernel(
    lst, tgt_l, tgt_r, pts_ref, q_ref, pt_ref, lb_hbm, ct_hbm,
    out_own, out_l, out_r, lm_ref, mm_ref, top_ref,
    sf_ref, qb_ref, rhs_ref, d_ref, acc_ref, lb_ref, ct_ref, sem,
):
    def part(k):
        rows = pl.ds(k * 16, 16)
        return pltpu.make_async_copy(lb_hbm.at[rows], lb_ref.at[rows], sem.at[k])

    child = pltpu.make_async_copy(ct_hbm, ct_ref, sem.at[8])
    for k in range(8):
        part(k).start()
    child.start()
    near_tables(pts_ref, q_ref, sf_ref, qb_ref, 128)
    for k, (tgt, out) in enumerate(((pts_ref, out_own), (tgt_l, out_l), (tgt_r, out_r))):
        acc_ref[...] = jnp.zeros((136, 256), f32)
        skip = SELF if k == 0 else 0

        def entry(i, first=k * 2048 + skip):
            return lst[first + i], lst[first + 1024 + i]

        near_pairs(entry, lst[k * 2048 + 896] - skip, tgt, sf_ref, qb_ref, rhs_ref, d_ref, acc_ref)
        out[...] = acc_ref[0:128, :]
    moments_tail(part, child, q_ref, pt_ref, lm_ref, mm_ref, top_ref, lb_ref, ct_ref)


def near(lists, arrays, leaf_basis, child):
    vm = pl.BlockSpec(memory_space=pltpu.VMEM)
    hbm = pl.BlockSpec(memory_space=pl.ANY)
    return pl.pallas_call(
        near_kernel,
        out_shape=tuple(jax.ShapeDtypeStruct((128, 256), f32) for _ in range(3))
        + (
            jax.ShapeDtypeStruct((128, 64), f32),
            jax.ShapeDtypeStruct((16, 64), f32),
            jax.ShapeDtypeStruct((1, 128), f32),
        ),
        in_specs=[pl.BlockSpec(memory_space=pltpu.SMEM)] + [vm] * 5 + [hbm] * 2,
        out_specs=(vm,) * 6,
        scratch_shapes=[
            pltpu.VMEM((128, 256, 64), bf16),
            pltpu.VMEM((128, 256, 128), f32),
            pltpu.VMEM((NB, 48, 256), bf16),
            pltpu.VMEM((NB, 256, 256), f32),
            pltpu.VMEM((136, 256), f32),
            pltpu.VMEM((128, 64, 256), f32),
            pltpu.VMEM((64, 64, 128), f32),
            pltpu.SemaphoreType.DMA((9,)),
        ],
        compiler_params=pltpu.CompilerParams(vmem_limit_bytes=60 << 20),
        name="near",
    )(lists, *arrays, leaf_basis, child)


def near_self_kernel(pts_ref, q_ref, part_ref, out, sf_ref, qb_ref, rhs_ref, d_ref, acc_ref):
    near_tables(pts_ref, q_ref, sf_ref, qb_ref, SELF)
    acc_ref[0:128, :] = part_ref[...]
    acc_ref[128:136, :] = jnp.zeros((8, 256), f32)

    def entry(i):
        n = jnp.minimum(i, SELF - 1)
        return n + 1, n

    near_pairs(entry, SELF, pts_ref, sf_ref, qb_ref, rhs_ref, d_ref, acc_ref)
    out[...] = acc_ref[0:128, :]


def near_self(points, charges, part):
    vm = pl.BlockSpec(memory_space=pltpu.VMEM)
    return pl.pallas_call(
        near_self_kernel,
        out_shape=jax.ShapeDtypeStruct((128, 256), f32),
        in_specs=[vm] * 3,
        out_specs=vm,
        scratch_shapes=[
            pltpu.VMEM((SELF, 256, 64), bf16),
            pltpu.VMEM((SELF, 256, 128), f32),
            pltpu.VMEM((NB, 48, 256), bf16),
            pltpu.VMEM((NB, 256, 256), f32),
            pltpu.VMEM((136, 256), f32),
        ],
        compiler_params=pltpu.CompilerParams(vmem_limit_bytes=60 << 20),
        name="near_self",
    )(points, charges, part)


def halves(x):
    h = x.astype(bf16).astype(f32)
    return h, (x - h).astype(bf16).astype(f32)


def features(x, y, z, source):
    parts = [halves(v) for v in (x, y, z)]
    norm = sum((h + m) * (h + m) for h, m in parts)
    one = jnp.ones_like(x)
    if source:
        nh, nm = halves(norm + soften)
        return [v for h, m in parts for v in (h, m, h, m)] + [one, one, nh, nm]
    nh, nm = halves(norm)
    return [v for h, m in parts for v in (-2.0 * h, -2.0 * h, -2.0 * m, -2.0 * m)] + [nh, nm, one, one]


def far_kernel(
    ids_ref, r1_ref, nl_ref, nm_ref, lm_ref, mm_ref, top_ref, out_ref, v_ref, u_ref, rep_ref, one_ref, mask_ref, ra_ref, mb_ref, full_ref
):
    for c in range(8):
        r = iota((128, 128), 0) - c * 16
        k = iota((128, 128), 1)
        lanes = slice((c % 2) * 128, (c % 2) * 128 + 128)
        rep_ref[c // 2, :, lanes] = jnp.where(r == (k >> 3), 1.0, 0.0).astype(bf16)
        one_ref[c // 2, :, lanes] = jnp.where((r >= 0) & (r < 3), 1.0, 0.0).astype(bf16)
        mask_ref[c] = jnp.where((iota((64, 128), 1) & 7) == c, 1.0, 0.0).astype(bf16)
    u_ref[...] = jnp.zeros((18 * 128, 64), f32)
    leaf = features(nl_ref[0].T, nl_ref[1].T, nl_ref[2].T, True)
    mid = features(nm_ref[0], nm_ref[1], nm_ref[2], True)
    for f in range(16):
        for blk in range(16):
            v_ref[pl.ds(blk * 128 + f, 8, stride=16), :] = leaf[f][blk * 8 : blk * 8 + 8]
        for blk in range(2):
            v_ref[pl.ds((16 + blk) * 128 + f, 8, stride=16), :] = mid[f][blk * 8 : blk * 8 + 8]

    for blk in range(18):
        src = lm_ref[blk * 8 : blk * 8 + 8, :] if blk < 16 else mm_ref[blk * 8 - 128 : blk * 8 - 120, :]
        for f, v in enumerate(split3(src)):
            u_ref[pl.ds(blk * 128 + f, 8, stride=16), :] = v

    def prepare(it, carry):
        for blk in (it * 3, it * 3 + 1, it * 3 + 2):
            rows = pl.ds(pl.multiple_of(blk * 128, 128), 128)
            v = v_ref[rows, :].T.astype(bf16)
            u = u_ref[rows, :].T.astype(bf16)
            for i in range(4):
                both = dot(v, rep_ref[i]).astype(bf16)
                ra_ref[blk * 8 + 2 * i] = both[:, 0:128]
                ra_ref[blk * 8 + 2 * i + 1] = both[:, 128:256]
                both = dot(u, one_ref[i])
                mb_ref[blk * 8 + 2 * i] = both[:, 0:128]
                mb_ref[blk * 8 + 2 * i + 1] = both[:, 128:256]
        return carry

    lax.fori_loop(0, 6, prepare, 0)
    low = iota((128, 128), 1) < 64
    low64 = iota((64, 128), 1) < 64

    def weights(x, y, z):
        tf = jnp.concatenate(features(x, y, z, False), axis=0)
        return jnp.concatenate([jnp.where(low, tf, 0.0), jnp.where(low, 0.0, tf)], axis=0).astype(bf16)

    def group(rhs, g, t0, t1):
        t0 = jnp.maximum(t0, 0)
        t1 = jnp.maximum(t1, 0)
        mask = mask_ref[g]
        lhs = jnp.concatenate([ra_ref[t0] * mask, ra_ref[t1] * mask], axis=1)
        m = jnp.where(low64, mb_ref[t0], mb_ref[t1])
        w = lax.rsqrt(dot(lhs, rhs)) * m
        return jnp.sum(jnp.sum(w.reshape(8, 8, 128), axis=0), axis=0, keepdims=True)

    def leaf_groups(p, groups):
        rhs = weights(*(r1_ref[pl.ds(pl.multiple_of(p * 32 + 8 * c, 8), 8), :] for c in range(3)))
        return [(p, g, group(rhs, g, ids_ref[p * 24 + g], ids_ref[p * 24 + 8 + g])) for g in groups]

    out_ref[...] = jnp.zeros((1280, 128), f32)
    out_ref[pl.ds(9, 128, stride=10), :] = jnp.broadcast_to(top_ref[...], (128, 128))

    def first(it, carry):
        got = []
        for u in range(4):
            got += leaf_groups(it * 4 + u, range(4))
        for p, g, val in got:
            out_ref[pl.ds(p * 10 + g, 1), :] = val
        return carry

    lax.fori_loop(0, 32, first, 0)

    def scan(it, pos):
        for u in range(8):
            p = it * 8 + u
            full_ref[pos] = p
            pos = pos + (ids_ref[p * 24 + 18] > 8).astype(i32)
        return pos

    full = lax.fori_loop(0, 16, scan, jnp.int32(0))
    full_ref[full] = 0

    def second(it, carry):
        got = []
        for u in range(2):
            got += leaf_groups(full_ref[it * 2 + u], range(4, 8))
        for p, g, val in got:
            out_ref[pl.ds(p * 10 + g, 1), :] = val
        return carry

    lax.fori_loop(0, (full + 1) // 2, second, 0)

    def mids(it, carry):
        got = []
        for u in range(2):
            b = (it * 2 + u) * 256 + 24
            rhs = weights(*(r1_ref[pl.ds(b + c, 8, stride=32), :] for c in range(3)))
            for g in range(8):
                p = (it * 2 + u) * 8 + g
                got.append((p, group(rhs, g, 128 + ids_ref[p * 24 + 16], 128 + ids_ref[p * 24 + 17])))
        for p, val in got:
            out_ref[pl.ds(p * 10 + 8, 1), :] = val
        return carry

    lax.fori_loop(0, 8, mids, 0)


def far(ids, r1, nodes_t, nodes_mid, moments, mid_moments, top_row):
    vm = pl.BlockSpec(memory_space=pltpu.VMEM)
    return pl.pallas_call(
        far_kernel,
        out_shape=jax.ShapeDtypeStruct((1280, 128), f32),
        in_specs=[pl.BlockSpec(memory_space=pltpu.SMEM)] + [vm] * 6,
        out_specs=vm,
        scratch_shapes=[
            pltpu.VMEM((18 * 128, 64), f32),
            pltpu.VMEM((18 * 128, 64), f32),
            pltpu.VMEM((4, 128, 256), bf16),
            pltpu.VMEM((4, 128, 256), bf16),
            pltpu.VMEM((8, 64, 128), bf16),
            pltpu.VMEM((144, 64, 128), bf16),
            pltpu.VMEM((144, 64, 128), f32),
            pltpu.SMEM((136,), i32),
        ],
        compiler_params=pltpu.CompilerParams(vmem_limit_bytes=60 << 20),
        name="far",
    )(ids, r1, nodes_t, nodes_mid, moments, mid_moments, top_row)


def final_kernel(
    top_ids, tab_ref, r1_ref, r2_ref, nt_ref, pt_ref, near_ref, bl_ref, br_ref, lb_hbm, ct_hbm, out_ref, lb_ref, ct_ref, sem
):
    def part(k):
        rows = pl.ds(k * 16, 16)
        return pltpu.make_async_copy(lb_hbm.at[rows], lb_ref.at[rows], sem.at[k])

    child = pltpu.make_async_copy(ct_hbm, ct_ref, sem.at[8])
    child.start()
    for k in range(8):
        part(k).start()
    tag = (iota((128, 128), 0) + 1).astype(f32)

    def lines(k, rows):
        return jnp.where(tab_ref[k : k + 1, :] == tag[0:rows], 1.0, 0.0)

    def two(x):
        return jnp.concatenate(halves(x), axis=1).astype(bf16)

    acc = [jnp.zeros((128, 256), f32), jnp.zeros((128, 256), f32)]
    for g in range(0, 8, 2):
        vals = jnp.concatenate([two(r2_ref[pl.ds(g + k, 128, stride=10), :]) for k in range(2)], axis=0)
        for h in range(2):
            oh = jnp.concatenate([lines(8 * h + g, 128), lines(8 * h + g + 1, 128)], axis=1).astype(bf16)
            acc[h] = acc[h] + dot(oh, vals)
    acc = [a[:, 0:128] + a[:, 128:256] for a in acc]
    local_t = acc[0].T[0:64] + acc[1].T[64:128]
    vals = two(r2_ref[pl.ds(8, 128, stride=10), :])
    res = [dot(lines(16 + h, 16).astype(bf16), vals) for h in range(2)]
    res = [a[:, 0:128] + a[:, 128:256] for a in res]
    mid_local = res[0][:, 0:64] + res[1][:, 64:128]
    half = iota((1, 128), 1) >> 6
    pad = jnp.zeros((6, 64), f32)
    cols = [jnp.concatenate([nt_ref[c], pad], axis=0).T for c in range(3)]
    rows = []
    for g in range(2):
        tx, ty, tz = (jnp.broadcast_to(cols[c][:, g : g + 1], (64, 128)) for c in range(3))

        def entry(it, total):
            for u in range(4):
                t = top_ids[g, it * 4 + u]
                p = jnp.maximum(t, 0) >> 1
                h = jnp.where(t < 0, 2, t & 1)
                m = jnp.where(half == h, r2_ref[pl.ds(p * 10 + 9, 1), :], 0.0)
                dx = tx - r1_ref[pl.ds(p * 32 + 28, 1), :]
                dy = ty - r1_ref[pl.ds(p * 32 + 29, 1), :]
                dz = tz - r1_ref[pl.ds(p * 32 + 30, 1), :]
                total = total + lax.rsqrt(dx * dx + dy * dy + dz * dz + soften) * m
            return total

        total = lax.fori_loop(0, 4, entry, jnp.zeros((64, 128), f32))
        top = jnp.broadcast_to(jnp.sum(total, axis=1, keepdims=True), (64, 64))
        for c in range(g * 8, g * 8 + 8):
            rows.append(jnp.sum(pt_ref[c] * top, axis=0, keepdims=True))
    mid_down = mid_local + jnp.concatenate(rows, axis=0)
    mid_t = jnp.concatenate([mid_down, jnp.zeros((112, 64), f32)], axis=0).T
    spread = jnp.where(iota((128, 128), 0) == (iota((128, 128), 1) >> 3), 1.0, 0.0).astype(bf16)
    mid_t = dot3(mid_t, spread)
    child.wait()
    down = local_t
    for i in range(64):
        down = down + ct_ref[i] * mid_t[i : i + 1, :]
    h, m = halves(down)
    pick = jnp.where((iota((32, 2048), 0) & 15) == (iota((32, 2048), 1) >> 7), 1.0, 0.0).astype(bf16)
    for k in range(8):
        part(k).wait()
        ks = slice(16 * k, 16 * k + 16)
        cols16 = dot(jnp.concatenate([h[:, ks], m[:, ks]], axis=1).astype(bf16), pick)
        for u in range(16):
            d = cols16[:, u * 128 : u * 128 + 128]
            n = 16 * k + u
            out_ref[n : n + 1, :] = jnp.sum(lb_ref[n] * jnp.concatenate([d, d], axis=1), axis=0, keepdims=True)
    out_ref[...] = out_ref[...] + near_ref[...] + bl_ref[...] + br_ref[...]


def final(far_top, arrays, leaf_basis, child):
    vm = pl.BlockSpec(memory_space=pltpu.VMEM)
    hbm = pl.BlockSpec(memory_space=pl.ANY)
    return pl.pallas_call(
        final_kernel,
        out_shape=jax.ShapeDtypeStruct((128, 256), f32),
        in_specs=[pl.BlockSpec(memory_space=pltpu.SMEM)] + [vm] * 8 + [hbm] * 2,
        out_specs=vm,
        scratch_shapes=[
            pltpu.VMEM((128, 64, 256), f32),
            pltpu.VMEM((64, 64, 128), f32),
            pltpu.SemaphoreType.DMA((9,)),
        ],
        compiler_params=pltpu.CompilerParams(vmem_limit_bytes=60 << 20),
        name="final",
    )(far_top, *arrays, leaf_basis, child)


def swap(x):
    return lax.all_to_all(x, AXES, split_axis=0, concat_axis=0, tiled=True)


def local(
    charges,
    points,
    leaf_basis,
    child_transfer,
    parent_transfer,
    nodes_leaf,
    nodes_mid,
    nodes_top,
    near_list,
    far_leaf,
    far_mid,
    far_top,
):
    shards = lax.axis_size(AXES)
    me = lax.axis_index(AXES).astype(i32).reshape(1)
    down_perm = [(i + 1, i) for i in range(shards - 1)]
    up_perm = [(i, i + 1) for i in range(shards - 1)]
    nodes_t = jnp.transpose(nodes_leaf, (0, 2, 1))
    pay, tab, own_list, to_left, to_right = plan(
        me, far_leaf.T, far_mid, near_list.T, nodes_t, nodes_mid, nodes_top, points
    )
    from_right = lax.ppermute(to_left, AXES, down_perm)
    from_left = lax.ppermute(to_right, AXES, up_perm)
    r1 = swap(pay)
    child = jnp.transpose(child_transfer, (1, 2, 0))
    lists = jnp.stack([own_list, from_left[384:392].astype(i32), from_right[384:392].astype(i32)])
    lists = jnp.transpose(lists.reshape(3, 8, 2, 128), (0, 2, 1, 3)).reshape(6144)
    flat = points.reshape(384, 256)
    near_own, near_l, near_r, leaf_moments, mid_moments, top_moments = near(
        lists, [from_left, from_right, flat, charges, parent_transfer], leaf_basis, child
    )
    r1, near_own, leaf_moments, mid_moments, top_moments = lax.optimization_barrier(
        (r1, near_own, leaf_moments, mid_moments, top_moments)
    )
    ids = r1[:, 27, 0:24].astype(i32).reshape(3072)
    r1 = r1.reshape(4096, 128)
    pay2 = far(ids, r1, nodes_t, nodes_mid, leaf_moments, mid_moments, top_moments)
    r2 = swap(pay2.reshape(128, 5, 2, 128)).reshape(1280, 128)
    back_l = lax.ppermute(near_l, AXES, down_perm)
    back_r = lax.ppermute(near_r, AXES, up_perm)
    near_own = near_self(flat, charges, near_own)
    return final(far_top, [tab, r1, r2, nodes_top, parent_transfer, near_own, back_l, back_r], leaf_basis, child)


def solution(mesh):
    placed = (
        P(AXES, None),
        P(None, AXES, None),
        P(AXES, None, None),
        P(AXES, None, None),
        P(AXES, None, None),
        P(None, AXES, None),
        P(None, AXES, None),
        P(None, AXES, None),
        P(AXES, None),
        P(AXES, None),
        P(AXES, None),
        P(AXES, None),
    )
    return jax.shard_map(local, mesh=mesh, in_specs=placed, out_specs=P(AXES, None), check_vma=False)
```

```python
import jax
import jax.numpy as jnp
from jax import lax
from jax.experimental import pallas as pl
from jax.experimental.pallas import tpu as pltpu
from jax.sharding import PartitionSpec as P


f32 = jnp.float32
bf16 = jnp.bfloat16
i32 = jnp.int32
soften = 0.25
AXES = ("dom", "sub")
NB = 8
SELF = 32
TRANS = (((1,), (1,)), ((), ()))


def dot(a, b):
    return jnp.dot(a, b, preferred_element_type=f32)


def dot_t(a, b):
    return lax.dot_general(a, b, TRANS, preferred_element_type=f32)


def split3(v):
    h = v.astype(bf16).astype(f32)
    r = v - h
    m = r.astype(bf16).astype(f32)
    return h, m, (r - m).astype(bf16).astype(f32)


def iota(shape, dim):
    return lax.broadcasted_iota(i32, shape, dim)


def upper(n):
    return jnp.where(iota((n, n), 0) <= iota((n, n), 1), 1.0, 0.0).astype(bf16)


def slots(owner_rows, wanted_rows, ids, caps):
    width = owner_rows[0].shape[1]
    tri = upper(width)
    half = caps // 2
    r = iota((caps, width), 0)
    slot = jnp.where(r < half, 2 * r, 2 * (r - half) + 1)
    row = jnp.zeros((2 * caps, 128), f32)
    carry = jnp.zeros((128, 1), f32)
    for own, want in zip(owner_rows, wanted_rows):
        hit = jnp.where(own == iota((128, width), 0), 1.0, 0.0)
        hit_b = hit.astype(bf16)
        cum = dot(hit_b, tri) + carry
        carry = cum[:, width - 1 : width]
        rank = jnp.sum(hit * cum, axis=0, keepdims=True).astype(i32) - 1
        place = jnp.where(rank == slot, 1.0, 0.0)
        vals = jnp.concatenate([place * (ids + 1.0), place * (want + 1.0)], axis=0).astype(bf16)
        row = row + dot_t(vals, hit_b)
    return row, carry


def plan_kernel(
    me_ref, far_ref, mid_ref, near_ref, nl_ref, nm_ref, nt_ref, pts_ref, pay_ref, tab_ref, own_ref, hl_ref, hr_ref, oh_ref
):
    me = me_ref[0]
    lane = iota((1, 128), 1)
    ids = lane.astype(f32)
    far = far_ref[...]
    own = far >> 7
    want = (far & 127).astype(f32)
    row, live = slots([own[c : c + 1] for c in range(16)], [want[c : c + 1] for c in range(16)], ids, 16)
    eye = jnp.where(iota((16, 16), 0) == iota((16, 16), 1), 1.0, 0.0).astype(bf16)
    mid = mid_ref[...]
    mown = dot_t(eye, (mid >> 4).astype(f32).astype(bf16)).astype(i32)
    mwant = dot_t(eye, (mid & 15).astype(f32).astype(bf16))
    mrow, mlive = slots(
        [mown[c : c + 1] for c in range(16)], [mwant[c : c + 1] for c in range(16)], ids[:, 0:16], 2
    )
    col = jnp.concatenate([row, mrow, jnp.zeros((92, 128), f32)], axis=0).T
    mcol = col[:, 32:36]
    tab_ref[0:16, :] = row[0:16]
    tab_ref[16:18, :] = mrow[0:2]
    tab_ref[18:32, :] = jnp.zeros((14, 128), f32)
    even, odd = row[0:8], row[8:16]
    line = jnp.broadcast_to(ids + 1.0, (8, 128))
    for o in range(128):
        a = jnp.broadcast_to(even[:, o : o + 1], (8, 128))
        b = jnp.broadcast_to(odd[:, o : o + 1], (8, 128))
        oh_ref[o * 8 : o * 8 + 8, 0:128] = jnp.where(a == line, 1.0, 0.0)
        oh_ref[o * 8 : o * 8 + 8, 128:256] = jnp.where(b == line, 1.0, 0.0)
    oh = oh_ref[...].astype(bf16)
    z = jnp.zeros((64, 128), f32)
    blocks = []
    for c in range(3):
        x = nl_ref[c]
        big = jnp.concatenate([jnp.concatenate([x, z], axis=1), jnp.concatenate([z, x], axis=1)], axis=0)
        blocks += [v.astype(bf16) for v in split3(big)]
    for c in range(3):
        h, m, l = blocks[3 * c : 3 * c + 3]
        both = dot_t(oh, jnp.concatenate([h, m], axis=0))
        pay_ref[:, c * 8 : c * 8 + 8, :] = (both[:, 0:128] + both[:, 128:256]).reshape(128, 8, 128)
    both = dot_t(oh, jnp.concatenate([blocks[2], blocks[5]], axis=0))
    pay_ref[:, 0:8, :] = pay_ref[:, 0:8, :] + both[:, 0:128].reshape(128, 8, 128)
    pay_ref[:, 8:16, :] = pay_ref[:, 8:16, :] + both[:, 128:256].reshape(128, 8, 128)
    pay_ref[:, 16:24, :] = pay_ref[:, 16:24, :] + dot_t(oh, blocks[8]).reshape(128, 8, 128)
    tops = [jnp.concatenate([nt_ref[c, 0:1], nt_ref[c, 1:2]], axis=1) for c in range(3)]
    zero = jnp.zeros((1, 128), f32)
    last = jnp.concatenate([zero] * 4 + tops + [zero], axis=0)
    pay_ref[:, 24:32, :] = jnp.broadcast_to(last[None], (128, 8, 128))
    la = jnp.where(mcol[:, 0:1] == ids[:, 0:16] + 1.0, 1.0, 0.0)
    lb = jnp.where(mcol[:, 1:2] == ids[:, 0:16] + 1.0, 1.0, 0.0)
    ohm = jnp.concatenate([la, lb], axis=1).astype(bf16)
    for c in range(3):
        xm = nm_ref[c]
        zm = jnp.zeros((16, 64), f32)
        bigm = jnp.concatenate([jnp.concatenate([xm, zm], axis=1), jnp.concatenate([zm, xm], axis=1)], axis=0)
        h, m, l = split3(bigm)
        resm = dot(ohm, h.astype(bf16)) + dot(ohm, m.astype(bf16)) + dot(ohm, l.astype(bf16))
        pay_ref[:, 24 + c : 25 + c, :] = resm[:, None, :]
    idrow = jnp.concatenate(
        [col[:, 16:32] - 1.0, mcol[:, 2:4] - 1.0, live, mlive, jnp.zeros((128, 108), f32)], axis=1
    )
    pay_ref[:, 27:28, :] = idrow[:, None, :]
    near = near_ref[...]
    nown = near >> 7
    nloc = (near & 127).astype(f32)
    tri = upper(128)
    outs = []
    for d in (-1, 0, 1):
        hit = jnp.where((nown == me + d) & (near >= 0), 1.0, 0.0)
        cum = dot(hit.astype(bf16), tri)
        base = jnp.zeros((1, 1), f32)
        acc = jnp.zeros((16, 128), f32)
        for c in range(6):
            pos = (cum[c : c + 1] + base).astype(i32) - 1
            base = base + cum[c : c + 1, 127:128]
            bm = jnp.where((pos & 127) == iota((128, 128), 0), hit[c : c + 1], 0.0).astype(bf16)
            am = jnp.where((pos >> 7) == iota((8, 128), 0), 1.0, 0.0)
            vals = jnp.concatenate([am * (ids + 1.0), am * nloc[c : c + 1]], axis=0).astype(bf16)
            acc = acc + dot_t(vals, bm)
        outs.append((jnp.where(iota((8, 128), 0) == 7, base, acc[0:8]), acc[8:16]))
    own_ref[:, 0:128] = outs[1][0].astype(i32)
    own_ref[:, 128:256] = outs[1][1].astype(i32)
    for ref, k in ((hl_ref, 0), (hr_ref, 2)):
        for c in range(3):
            ref[c * 128 : (c + 1) * 128, :] = pts_ref[c]
        ref[384:392, 0:128] = outs[k][0]
        ref[384:392, 128:256] = outs[k][1]


def plan(me, far_t, far_mid, near_t, nodes_t, nodes_mid, nodes_top, points):
    vm = pl.BlockSpec(memory_space=pltpu.VMEM)
    return pl.pallas_call(
        plan_kernel,
        out_shape=(
            jax.ShapeDtypeStruct((128, 32, 128), f32),
            jax.ShapeDtypeStruct((32, 128), f32),
            jax.ShapeDtypeStruct((8, 256), i32),
            jax.ShapeDtypeStruct((392, 256), f32),
            jax.ShapeDtypeStruct((392, 256), f32),
        ),
        in_specs=[pl.BlockSpec(memory_space=pltpu.SMEM)] + [vm] * 7,
        out_specs=(vm,) * 5,
        scratch_shapes=[pltpu.VMEM((1024, 256), f32)],
        compiler_params=pltpu.CompilerParams(vmem_limit_bytes=60 << 20),
        name="plan",
    )(me, far_t, far_mid, near_t, nodes_t, nodes_mid, nodes_top, points)


def dot3(a, b):
    return sum(dot(v.astype(bf16), b) for v in split3(a))


def moments_tail(part, child, q_ref, pt_ref, lm_ref, mm_ref, top_ref, lb_ref, ct_ref):
    lane = iota((64, 128), 1)
    lmt = jnp.zeros((64, 128), f32)
    for k in range(8):
        part(k).wait()

        def leaf(it, acc):
            for u in range(4):
                n = k * 16 + it * 4 + u
                prod = lb_ref[n] * q_ref[pl.ds(n, 1), :]
                col = jnp.sum(prod[:, 0:128] + prod[:, 128:256], axis=1, keepdims=True)
                acc = jnp.where(lane == n, col, acc)
            return acc

        lmt = lax.fori_loop(0, 4, leaf, lmt)
    lm_ref[...] = lmt.T
    child.wait()
    rows = []
    for i in range(64):
        rows.append(jnp.sum(ct_ref[i] * lmt, axis=0, keepdims=True))
    per_leaf = jnp.concatenate(rows, axis=0)
    group = jnp.where((iota((128, 128), 0) >> 3) == iota((128, 128), 1), 1.0, 0.0).astype(bf16)
    mm = dot3(per_leaf, group).T
    mm_ref[...] = mm[0:16, :]
    tops = []
    for g in range(2):
        acc = jnp.zeros((64, 64), f32)
        for c in range(g * 8, g * 8 + 8):
            acc = acc + pt_ref[c] * mm[c : c + 1, :]
        tops.append(jnp.broadcast_to(jnp.sum(acc, axis=1, keepdims=True), (64, 128)).T[0:1])
    top_ref[...] = jnp.concatenate(tops, axis=1)


def tile_rows(x, y, z, a, b):
    r = iota((8, 256), 0)
    v = jnp.where(r == 0, x, jnp.where(r == 1, y, jnp.where(r == 2, z, jnp.where(r == 3, a, b))))
    return jnp.where(r < 5, v, 0.0)


def near_tables(pts_ref, q_ref, sf_ref, qb_ref, count):
    r = iota((64, 128), 0)
    spread = jnp.where((r >= 48) & (r < 51), 1.0, 0.0).astype(bf16)
    r8 = iota((8, 256), 0)

    def factors(n):
        x = pts_ref[pl.ds(n, 1), :]
        y = pts_ref[pl.ds(128 + n, 1), :]
        z = pts_ref[pl.ds(256 + n, 1), :]
        norm = x * x + y * y + z * z + soften
        h, m, l = split3(tile_rows(x, y, z, jnp.ones_like(x), norm))
        qh, qm, ql = split3(jnp.broadcast_to(q_ref[pl.ds(n, 1), :], (8, 256)))
        q = jnp.where(r8 == 0, qh, jnp.where(r8 == 1, qm, jnp.where(r8 == 2, ql, 0.0)))
        return jnp.concatenate([h, m, l, h, m, h, q, jnp.zeros_like(q)], axis=0).T.astype(bf16)

    for n in range(8):
        sf_ref[n] = factors(n)

    def prepare(it, carry):
        for u in range(8):
            qb_ref[it * 8 + u] = dot(sf_ref[it * 8 + u], spread)
        ahead = jnp.minimum(it + 1, count // 8 - 1)
        made = [factors(ahead * 8 + u) for u in range(8)]
        for u in range(8):
            sf_ref[ahead * 8 + u] = made[u]
        return carry

    lax.fori_loop(0, count // 8, prepare, 0)


def near_pairs(entry, total, tgt, sf_ref, qb_ref, rhs_ref, d_ref, acc_ref):
    def factors(i, u):
        lv, _ = entry(i)
        lrow = jnp.maximum(lv - 1, 0)
        x = tgt[pl.ds(lrow, 1), :]
        y = tgt[pl.ds(128 + lrow, 1), :]
        z = tgt[pl.ds(256 + lrow, 1), :]
        norm = x * x + y * y + z * z
        h, m, l = split3(tile_rows(-2.0 * x, -2.0 * y, -2.0 * z, norm, jnp.ones_like(x)))
        rhs_ref[u] = jnp.concatenate([h, h, h, m, m, l], axis=0).astype(bf16)

    def distances(i, u):
        _, n = entry(i)
        d_ref[u] = dot(sf_ref[n, :, 0:48], rhs_ref[u])

    def sums(i, u):
        lv, n = entry(i)
        acc = jnp.zeros((8, 256), f32)
        for j in range(0, 256, 64):
            w = lax.rsqrt(d_ref[u, j : j + 64, :])
            q = qb_ref[n, j : j + 64, :]
            acc = acc + jnp.sum((w * jnp.concatenate([q, q], axis=1)).reshape(8, 8, 256), axis=0)
        row = jnp.where(lv > 0, lv - 1, 128)
        return row, jnp.sum(acc, axis=0, keepdims=True)

    for u in range(NB):
        factors(u, u)
    for u in range(NB):
        distances(u, u)
        factors(NB + u, u)

    def step(it, carry):
        i = it * NB
        got = [sums(i + u, u) for u in range(NB)]
        for u in range(NB):
            distances(i + NB + u, u)
        for u in range(NB):
            factors(i + 2 * NB + u, u)
        for row, val in got:
            acc_ref[pl.ds(row, 1), :] = acc_ref[pl.ds(row, 1), :] + val
        return carry

    lax.fori_loop(0, (total + NB - 1) // NB, step, 0)


def near_kernel(
    lst, tgt_l, tgt_r, pts_ref, q_ref, pt_ref, lb_hbm, ct_hbm,
    out_own, out_l, out_r, lm_ref, mm_ref, top_ref,
    sf_ref, qb_ref, rhs_ref, d_ref, acc_ref, lb_ref, ct_ref, sem,
):
    def part(k):
        rows = pl.ds(k * 16, 16)
        return pltpu.make_async_copy(lb_hbm.at[rows], lb_ref.at[rows], sem.at[k])

    child = pltpu.make_async_copy(ct_hbm, ct_ref, sem.at[8])
    for k in range(8):
        part(k).start()
    child.start()
    near_tables(pts_ref, q_ref, sf_ref, qb_ref, 128)
    for k, (tgt, out) in enumerate(((pts_ref, out_own), (tgt_l, out_l), (tgt_r, out_r))):
        acc_ref[...] = jnp.zeros((136, 256), f32)
        skip = SELF if k == 0 else 0

        def entry(i, first=k * 2048 + skip):
            return lst[first + i], lst[first + 1024 + i]

        near_pairs(entry, lst[k * 2048 + 896] - skip, tgt, sf_ref, qb_ref, rhs_ref, d_ref, acc_ref)
        out[...] = acc_ref[0:128, :]
    moments_tail(part, child, q_ref, pt_ref, lm_ref, mm_ref, top_ref, lb_ref, ct_ref)


def near(lists, arrays, leaf_basis, child):
    vm = pl.BlockSpec(memory_space=pltpu.VMEM)
    hbm = pl.BlockSpec(memory_space=pl.ANY)
    return pl.pallas_call(
        near_kernel,
        out_shape=tuple(jax.ShapeDtypeStruct((128, 256), f32) for _ in range(3))
        + (
            jax.ShapeDtypeStruct((128, 64), f32),
            jax.ShapeDtypeStruct((16, 64), f32),
            jax.ShapeDtypeStruct((1, 128), f32),
        ),
        in_specs=[pl.BlockSpec(memory_space=pltpu.SMEM)] + [vm] * 5 + [hbm] * 2,
        out_specs=(vm,) * 6,
        scratch_shapes=[
            pltpu.VMEM((128, 256, 64), bf16),
            pltpu.VMEM((128, 256, 128), f32),
            pltpu.VMEM((NB, 48, 256), bf16),
            pltpu.VMEM((NB, 256, 256), f32),
            pltpu.VMEM((136, 256), f32),
            pltpu.VMEM((128, 64, 256), f32),
            pltpu.VMEM((64, 64, 128), f32),
            pltpu.SemaphoreType.DMA((9,)),
        ],
        compiler_params=pltpu.CompilerParams(vmem_limit_bytes=60 << 20),
        name="near",
    )(lists, *arrays, leaf_basis, child)


def near_self(pts_ref, q_ref, part_ref, sf_ref, qb_ref, rhs_ref, d_ref, acc_ref):
    near_tables(pts_ref, q_ref, sf_ref, qb_ref, SELF)
    acc_ref[0:128, :] = part_ref[...]
    acc_ref[128:136, :] = jnp.zeros((8, 256), f32)

    def entry(i):
        n = jnp.minimum(i, SELF - 1)
        return n + 1, n

    near_pairs(entry, SELF, pts_ref, sf_ref, qb_ref, rhs_ref, d_ref, acc_ref)


def halves(x):
    h = x.astype(bf16).astype(f32)
    return h, (x - h).astype(bf16).astype(f32)


def features(x, y, z, source):
    parts = [halves(v) for v in (x, y, z)]
    norm = sum((h + m) * (h + m) for h, m in parts)
    one = jnp.ones_like(x)
    if source:
        nh, nm = halves(norm + soften)
        return [v for h, m in parts for v in (h, m, h, m)] + [one, one, nh, nm]
    nh, nm = halves(norm)
    return [v for h, m in parts for v in (-2.0 * h, -2.0 * h, -2.0 * m, -2.0 * m)] + [nh, nm, one, one]


def far_kernel(
    ids_ref, r1_ref, nl_ref, nm_ref, lm_ref, mm_ref, top_ref, out_ref, v_ref, u_ref, rep_ref, one_ref, mask_ref, ra_ref, mb_ref, full_ref
):
    for c in range(8):
        r = iota((128, 128), 0) - c * 16
        k = iota((128, 128), 1)
        lanes = slice((c % 2) * 128, (c % 2) * 128 + 128)
        rep_ref[c // 2, :, lanes] = jnp.where(r == (k >> 3), 1.0, 0.0).astype(bf16)
        one_ref[c // 2, :, lanes] = jnp.where((r >= 0) & (r < 3), 1.0, 0.0).astype(bf16)
        mask_ref[c] = jnp.where((iota((64, 128), 1) & 7) == c, 1.0, 0.0).astype(bf16)
    u_ref[...] = jnp.zeros((18 * 128, 64), f32)
    leaf = features(nl_ref[0].T, nl_ref[1].T, nl_ref[2].T, True)
    mid = features(nm_ref[0], nm_ref[1], nm_ref[2], True)
    for f in range(16):
        for blk in range(16):
            v_ref[pl.ds(blk * 128 + f, 8, stride=16), :] = leaf[f][blk * 8 : blk * 8 + 8]
        for blk in range(2):
            v_ref[pl.ds((16 + blk) * 128 + f, 8, stride=16), :] = mid[f][blk * 8 : blk * 8 + 8]

    for blk in range(18):
        src = lm_ref[blk * 8 : blk * 8 + 8, :] if blk < 16 else mm_ref[blk * 8 - 128 : blk * 8 - 120, :]
        for f, v in enumerate(split3(src)):
            u_ref[pl.ds(blk * 128 + f, 8, stride=16), :] = v

    def prepare(it, carry):
        for blk in (it * 3, it * 3 + 1, it * 3 + 2):
            rows = pl.ds(pl.multiple_of(blk * 128, 128), 128)
            v = v_ref[rows, :].T.astype(bf16)
            u = u_ref[rows, :].T.astype(bf16)
            for i in range(4):
                both = dot(v, rep_ref[i]).astype(bf16)
                ra_ref[blk * 8 + 2 * i] = both[:, 0:128]
                ra_ref[blk * 8 + 2 * i + 1] = both[:, 128:256]
                both = dot(u, one_ref[i])
                mb_ref[blk * 8 + 2 * i] = both[:, 0:128]
                mb_ref[blk * 8 + 2 * i + 1] = both[:, 128:256]
        return carry

    lax.fori_loop(0, 6, prepare, 0)
    low = iota((128, 128), 1) < 64
    low64 = iota((64, 128), 1) < 64

    def weights(x, y, z):
        tf = jnp.concatenate(features(x, y, z, False), axis=0)
        return jnp.concatenate([jnp.where(low, tf, 0.0), jnp.where(low, 0.0, tf)], axis=0).astype(bf16)

    def group(rhs, g, t0, t1):
        t0 = jnp.maximum(t0, 0)
        t1 = jnp.maximum(t1, 0)
        mask = mask_ref[g]
        lhs = jnp.concatenate([ra_ref[t0] * mask, ra_ref[t1] * mask], axis=1)
        m = jnp.where(low64, mb_ref[t0], mb_ref[t1])
        w = lax.rsqrt(dot(lhs, rhs)) * m
        return jnp.sum(jnp.sum(w.reshape(8, 8, 128), axis=0), axis=0, keepdims=True)

    def leaf_groups(p, groups):
        rhs = weights(*(r1_ref[pl.ds(pl.multiple_of(p * 32 + 8 * c, 8), 8), :] for c in range(3)))
        return [(p, g, group(rhs, g, ids_ref[p * 24 + g], ids_ref[p * 24 + 8 + g])) for g in groups]

    out_ref[...] = jnp.zeros((1280, 128), f32)
    out_ref[pl.ds(9, 128, stride=10), :] = jnp.broadcast_to(top_ref[...], (128, 128))

    def first(it, carry):
        got = []
        for u in range(4):
            got += leaf_groups(it * 4 + u, range(4))
        for p, g, val in got:
            out_ref[pl.ds(p * 10 + g, 1), :] = val
        return carry

    lax.fori_loop(0, 32, first, 0)

    def scan(it, pos):
        for u in range(8):
            p = it * 8 + u
            full_ref[pos] = p
            pos = pos + (ids_ref[p * 24 + 18] > 8).astype(i32)
        return pos

    full = lax.fori_loop(0, 16, scan, jnp.int32(0))
    full_ref[full] = 0

    def second(it, carry):
        got = []
        for u in range(2):
            got += leaf_groups(full_ref[it * 2 + u], range(4, 8))
        for p, g, val in got:
            out_ref[pl.ds(p * 10 + g, 1), :] = val
        return carry

    lax.fori_loop(0, (full + 1) // 2, second, 0)

    def mids(it, carry):
        got = []
        for u in range(2):
            b = (it * 2 + u) * 256 + 24
            rhs = weights(*(r1_ref[pl.ds(b + c, 8, stride=32), :] for c in range(3)))
            for g in range(8):
                p = (it * 2 + u) * 8 + g
                got.append((p, group(rhs, g, 128 + ids_ref[p * 24 + 16], 128 + ids_ref[p * 24 + 17])))
        for p, val in got:
            out_ref[pl.ds(p * 10 + 8, 1), :] = val
        return carry

    lax.fori_loop(0, 8, mids, 0)


def far(ids, r1, nodes_t, nodes_mid, moments, mid_moments, top_row):
    vm = pl.BlockSpec(memory_space=pltpu.VMEM)
    return pl.pallas_call(
        far_kernel,
        out_shape=jax.ShapeDtypeStruct((1280, 128), f32),
        in_specs=[pl.BlockSpec(memory_space=pltpu.SMEM)] + [vm] * 6,
        out_specs=vm,
        scratch_shapes=[
            pltpu.VMEM((18 * 128, 64), f32),
            pltpu.VMEM((18 * 128, 64), f32),
            pltpu.VMEM((4, 128, 256), bf16),
            pltpu.VMEM((4, 128, 256), bf16),
            pltpu.VMEM((8, 64, 128), bf16),
            pltpu.VMEM((144, 64, 128), bf16),
            pltpu.VMEM((144, 64, 128), f32),
            pltpu.SMEM((136,), i32),
        ],
        compiler_params=pltpu.CompilerParams(vmem_limit_bytes=60 << 20),
        name="far",
    )(ids, r1, nodes_t, nodes_mid, moments, mid_moments, top_row)


def final_kernel(
    top_ids, tab_ref, r1_ref, r2_ref, nt_ref, pt_ref, near_ref, bl_ref, br_ref, pts_ref, q_ref, lb_hbm, ct_hbm,
    out_ref,
    lb_ref, ct_ref, sf_ref, qb_ref, rhs_ref, d_ref, acc_ref, sem,
):
    def part(k):
        rows = pl.ds(k * 16, 16)
        return pltpu.make_async_copy(lb_hbm.at[rows], lb_ref.at[rows], sem.at[k])

    child = pltpu.make_async_copy(ct_hbm, ct_ref, sem.at[8])
    child.start()
    for k in range(8):
        part(k).start()
    near_self(pts_ref, q_ref, near_ref, sf_ref, qb_ref, rhs_ref, d_ref, acc_ref)
    tag = (iota((128, 128), 0) + 1).astype(f32)

    def lines(k, rows):
        return jnp.where(tab_ref[k : k + 1, :] == tag[0:rows], 1.0, 0.0)

    def two(x):
        return jnp.concatenate(halves(x), axis=1).astype(bf16)

    acc = [jnp.zeros((128, 256), f32), jnp.zeros((128, 256), f32)]
    for g in range(0, 8, 2):
        vals = jnp.concatenate([two(r2_ref[pl.ds(g + k, 128, stride=10), :]) for k in range(2)], axis=0)
        for h in range(2):
            oh = jnp.concatenate([lines(8 * h + g, 128), lines(8 * h + g + 1, 128)], axis=1).astype(bf16)
            acc[h] = acc[h] + dot(oh, vals)
    acc = [a[:, 0:128] + a[:, 128:256] for a in acc]
    local_t = acc[0].T[0:64] + acc[1].T[64:128]
    vals = two(r2_ref[pl.ds(8, 128, stride=10), :])
    res = [dot(lines(16 + h, 16).astype(bf16), vals) for h in range(2)]
    res = [a[:, 0:128] + a[:, 128:256] for a in res]
    mid_local = res[0][:, 0:64] + res[1][:, 64:128]
    half = iota((1, 128), 1) >> 6
    pad = jnp.zeros((6, 64), f32)
    cols = [jnp.concatenate([nt_ref[c], pad], axis=0).T for c in range(3)]
    rows = []
    for g in range(2):
        tx, ty, tz = (jnp.broadcast_to(cols[c][:, g : g + 1], (64, 128)) for c in range(3))

        def entry(it, total):
            for u in range(4):
                t = top_ids[g, it * 4 + u]
                p = jnp.maximum(t, 0) >> 1
                h = jnp.where(t < 0, 2, t & 1)
                m = jnp.where(half == h, r2_ref[pl.ds(p * 10 + 9, 1), :], 0.0)
                dx = tx - r1_ref[pl.ds(p * 32 + 28, 1), :]
                dy = ty - r1_ref[pl.ds(p * 32 + 29, 1), :]
                dz = tz - r1_ref[pl.ds(p * 32 + 30, 1), :]
                total = total + lax.rsqrt(dx * dx + dy * dy + dz * dz + soften) * m
            return total

        total = lax.fori_loop(0, 4, entry, jnp.zeros((64, 128), f32))
        top = jnp.broadcast_to(jnp.sum(total, axis=1, keepdims=True), (64, 64))
        for c in range(g * 8, g * 8 + 8):
            rows.append(jnp.sum(pt_ref[c] * top, axis=0, keepdims=True))
    mid_down = mid_local + jnp.concatenate(rows, axis=0)
    mid_t = jnp.concatenate([mid_down, jnp.zeros((112, 64), f32)], axis=0).T
    spread = jnp.where(iota((128, 128), 0) == (iota((128, 128), 1) >> 3), 1.0, 0.0).astype(bf16)
    mid_t = dot3(mid_t, spread)
    child.wait()
    down = local_t
    for i in range(64):
        down = down + ct_ref[i] * mid_t[i : i + 1, :]
    h, m = halves(down)
    pick = jnp.where((iota((32, 2048), 0) & 15) == (iota((32, 2048), 1) >> 7), 1.0, 0.0).astype(bf16)
    for k in range(8):
        part(k).wait()
        ks = slice(16 * k, 16 * k + 16)
        cols16 = dot(jnp.concatenate([h[:, ks], m[:, ks]], axis=1).astype(bf16), pick)
        for u in range(16):
            d = cols16[:, u * 128 : u * 128 + 128]
            n = 16 * k + u
            out_ref[n : n + 1, :] = jnp.sum(lb_ref[n] * jnp.concatenate([d, d], axis=1), axis=0, keepdims=True)
    out_ref[...] = out_ref[...] + acc_ref[0:128, :] + bl_ref[...] + br_ref[...]


def final(far_top, arrays, leaf_basis, child):
    vm = pl.BlockSpec(memory_space=pltpu.VMEM)
    hbm = pl.BlockSpec(memory_space=pl.ANY)
    return pl.pallas_call(
        final_kernel,
        out_shape=jax.ShapeDtypeStruct((128, 256), f32),
        in_specs=[pl.BlockSpec(memory_space=pltpu.SMEM)] + [vm] * 10 + [hbm] * 2,
        out_specs=vm,
        scratch_shapes=[
            pltpu.VMEM((128, 64, 256), f32),
            pltpu.VMEM((64, 64, 128), f32),
            pltpu.VMEM((SELF, 256, 64), bf16),
            pltpu.VMEM((SELF, 256, 128), f32),
            pltpu.VMEM((NB, 48, 256), bf16),
            pltpu.VMEM((NB, 256, 256), f32),
            pltpu.VMEM((136, 256), f32),
            pltpu.SemaphoreType.DMA((9,)),
        ],
        compiler_params=pltpu.CompilerParams(vmem_limit_bytes=60 << 20),
        name="final",
    )(far_top, *arrays, leaf_basis, child)


def swap(x):
    return lax.all_to_all(x, AXES, split_axis=0, concat_axis=0, tiled=True)


def local(
    charges,
    points,
    leaf_basis,
    child_transfer,
    parent_transfer,
    nodes_leaf,
    nodes_mid,
    nodes_top,
    near_list,
    far_leaf,
    far_mid,
    far_top,
):
    shards = lax.axis_size(AXES)
    me = lax.axis_index(AXES).astype(i32).reshape(1)
    down_perm = [(i + 1, i) for i in range(shards - 1)]
    up_perm = [(i, i + 1) for i in range(shards - 1)]
    nodes_t = jnp.transpose(nodes_leaf, (0, 2, 1))
    pay, tab, own_list, to_left, to_right = plan(
        me, far_leaf.T, far_mid, near_list.T, nodes_t, nodes_mid, nodes_top, points
    )
    from_right = lax.ppermute(to_left, AXES, down_perm)
    from_left = lax.ppermute(to_right, AXES, up_perm)
    r1 = swap(pay)
    child = jnp.transpose(child_transfer, (1, 2, 0))
    lists = jnp.stack([own_list, from_left[384:392].astype(i32), from_right[384:392].astype(i32)])
    lists = jnp.transpose(lists.reshape(3, 8, 2, 128), (0, 2, 1, 3)).reshape(6144)
    flat = points.reshape(384, 256)
    near_own, near_l, near_r, leaf_moments, mid_moments, top_moments = near(
        lists, [from_left, from_right, flat, charges, parent_transfer], leaf_basis, child
    )
    r1, near_own, leaf_moments, mid_moments, top_moments = lax.optimization_barrier(
        (r1, near_own, leaf_moments, mid_moments, top_moments)
    )
    ids = r1[:, 27, 0:24].astype(i32).reshape(3072)
    r1 = r1.reshape(4096, 128)
    pay2 = far(ids, r1, nodes_t, nodes_mid, leaf_moments, mid_moments, top_moments)
    r2 = swap(pay2.reshape(128, 5, 2, 128)).reshape(1280, 128)
    back_l = lax.ppermute(near_l, AXES, down_perm)
    back_r = lax.ppermute(near_r, AXES, up_perm)
    return final(far_top, [tab, r1, r2, nodes_top, parent_transfer, near_own, back_l, back_r, flat, charges], leaf_basis, child)


def solution(mesh):
    placed = (
        P(AXES, None),
        P(None, AXES, None),
        P(AXES, None, None),
        P(AXES, None, None),
        P(AXES, None, None),
        P(None, AXES, None),
        P(None, AXES, None),
        P(None, AXES, None),
        P(AXES, None),
        P(AXES, None),
        P(AXES, None),
        P(AXES, None),
    )
    return jax.shard_map(local, mesh=mesh, in_specs=placed, out_specs=P(AXES, None), check_vma=False)
```

```python
import jax
import jax.numpy as jnp
from jax import lax
from jax.experimental import pallas as pl
from jax.experimental.pallas import tpu as pltpu
from jax.sharding import PartitionSpec as P


f32 = jnp.float32
bf16 = jnp.bfloat16
i32 = jnp.int32
soften = 0.25
AXES = ("dom", "sub")
NB = 8
SELF = 32
TRANS = (((1,), (1,)), ((), ()))


def dot(a, b):
    return jnp.dot(a, b, preferred_element_type=f32)


def dot_t(a, b):
    return lax.dot_general(a, b, TRANS, preferred_element_type=f32)


def split3(v):
    h = v.astype(bf16).astype(f32)
    r = v - h
    m = r.astype(bf16).astype(f32)
    return h, m, (r - m).astype(bf16).astype(f32)


def iota(shape, dim):
    return lax.broadcasted_iota(i32, shape, dim)


def upper(n):
    return jnp.where(iota((n, n), 0) <= iota((n, n), 1), 1.0, 0.0).astype(bf16)


def slots(owner_rows, wanted_rows, ids, caps):
    width = owner_rows[0].shape[1]
    tri = upper(width)
    half = caps // 2
    r = iota((caps, width), 0)
    slot = jnp.where(r < half, 2 * r, 2 * (r - half) + 1)
    row = jnp.zeros((2 * caps, 128), f32)
    carry = jnp.zeros((128, 1), f32)
    for own, want in zip(owner_rows, wanted_rows):
        hit = jnp.where(own == iota((128, width), 0), 1.0, 0.0)
        hit_b = hit.astype(bf16)
        cum = dot(hit_b, tri) + carry
        carry = cum[:, width - 1 : width]
        rank = jnp.sum(hit * cum, axis=0, keepdims=True).astype(i32) - 1
        place = jnp.where(rank == slot, 1.0, 0.0)
        vals = jnp.concatenate([place * (ids + 1.0), place * (want + 1.0)], axis=0).astype(bf16)
        row = row + dot_t(vals, hit_b)
    return row, carry


def plan_kernel(
    me_ref, far_ref, mid_ref, near_ref, nl_ref, nm_ref, nt_ref, pts_ref, pay_ref, tab_ref, own_ref, hl_ref, hr_ref, oh_ref
):
    me = me_ref[0]
    lane = iota((1, 128), 1)
    ids = lane.astype(f32)
    far = far_ref[...]
    own = far >> 7
    want = (far & 127).astype(f32)
    row, live = slots([own[c : c + 1] for c in range(16)], [want[c : c + 1] for c in range(16)], ids, 16)
    eye = jnp.where(iota((16, 16), 0) == iota((16, 16), 1), 1.0, 0.0).astype(bf16)
    mid = mid_ref[...]
    mown = dot_t(eye, (mid >> 4).astype(f32).astype(bf16)).astype(i32)
    mwant = dot_t(eye, (mid & 15).astype(f32).astype(bf16))
    mrow, mlive = slots(
        [mown[c : c + 1] for c in range(16)], [mwant[c : c + 1] for c in range(16)], ids[:, 0:16], 2
    )
    col = jnp.concatenate([row, mrow, jnp.zeros((92, 128), f32)], axis=0).T
    mcol = col[:, 32:36]
    tab_ref[0:16, :] = row[0:16]
    tab_ref[16:18, :] = mrow[0:2]
    tab_ref[18:32, :] = jnp.zeros((14, 128), f32)
    even, odd = row[0:8], row[8:16]
    line = jnp.broadcast_to(ids + 1.0, (8, 128))
    for o in range(128):
        a = jnp.broadcast_to(even[:, o : o + 1], (8, 128))
        b = jnp.broadcast_to(odd[:, o : o + 1], (8, 128))
        oh_ref[o * 8 : o * 8 + 8, 0:128] = jnp.where(a == line, 1.0, 0.0)
        oh_ref[o * 8 : o * 8 + 8, 128:256] = jnp.where(b == line, 1.0, 0.0)
    oh = oh_ref[...].astype(bf16)
    z = jnp.zeros((64, 128), f32)
    blocks = []
    for c in range(3):
        x = nl_ref[c]
        big = jnp.concatenate([jnp.concatenate([x, z], axis=1), jnp.concatenate([z, x], axis=1)], axis=0)
        blocks += [v.astype(bf16) for v in split3(big)]
    for c in range(3):
        h, m, l = blocks[3 * c : 3 * c + 3]
        both = dot_t(oh, jnp.concatenate([h, m], axis=0))
        pay_ref[:, c * 8 : c * 8 + 8, :] = (both[:, 0:128] + both[:, 128:256]).reshape(128, 8, 128)
    both = dot_t(oh, jnp.concatenate([blocks[2], blocks[5]], axis=0))
    pay_ref[:, 0:8, :] = pay_ref[:, 0:8, :] + both[:, 0:128].reshape(128, 8, 128)
    pay_ref[:, 8:16, :] = pay_ref[:, 8:16, :] + both[:, 128:256].reshape(128, 8, 128)
    pay_ref[:, 16:24, :] = pay_ref[:, 16:24, :] + dot_t(oh, blocks[8]).reshape(128, 8, 128)
    tops = [jnp.concatenate([nt_ref[c, 0:1], nt_ref[c, 1:2]], axis=1) for c in range(3)]
    zero = jnp.zeros((1, 128), f32)
    last = jnp.concatenate([zero] * 4 + tops + [zero], axis=0)
    pay_ref[:, 24:32, :] = jnp.broadcast_to(last[None], (128, 8, 128))
    la = jnp.where(mcol[:, 0:1] == ids[:, 0:16] + 1.0, 1.0, 0.0)
    lb = jnp.where(mcol[:, 1:2] == ids[:, 0:16] + 1.0, 1.0, 0.0)
    ohm = jnp.concatenate([la, lb], axis=1).astype(bf16)
    for c in range(3):
        xm = nm_ref[c]
        zm = jnp.zeros((16, 64), f32)
        bigm = jnp.concatenate([jnp.concatenate([xm, zm], axis=1), jnp.concatenate([zm, xm], axis=1)], axis=0)
        h, m, l = split3(bigm)
        resm = dot(ohm, h.astype(bf16)) + dot(ohm, m.astype(bf16)) + dot(ohm, l.astype(bf16))
        pay_ref[:, 24 + c : 25 + c, :] = resm[:, None, :]
    idrow = jnp.concatenate(
        [col[:, 16:32] - 1.0, mcol[:, 2:4] - 1.0, live, mlive, jnp.zeros((128, 108), f32)], axis=1
    )
    pay_ref[:, 27:28, :] = idrow[:, None, :]
    near = near_ref[...]
    nown = near >> 7
    nloc = (near & 127).astype(f32)
    tri = upper(128)
    outs = []
    for d in (-1, 0, 1):
        hit = jnp.where((nown == me + d) & (near >= 0), 1.0, 0.0)
        cum = dot(hit.astype(bf16), tri)
        base = jnp.zeros((1, 1), f32)
        acc = jnp.zeros((16, 128), f32)
        for c in range(6):
            pos = (cum[c : c + 1] + base).astype(i32) - 1
            base = base + cum[c : c + 1, 127:128]
            bm = jnp.where((pos & 127) == iota((128, 128), 0), hit[c : c + 1], 0.0).astype(bf16)
            am = jnp.where((pos >> 7) == iota((8, 128), 0), 1.0, 0.0)
            vals = jnp.concatenate([am * (ids + 1.0), am * nloc[c : c + 1]], axis=0).astype(bf16)
            acc = acc + dot_t(vals, bm)
        outs.append((jnp.where(iota((8, 128), 0) == 7, base, acc[0:8]), acc[8:16]))
    own_ref[:, 0:128] = outs[1][0].astype(i32)
    own_ref[:, 128:256] = outs[1][1].astype(i32)
    for ref, k in ((hl_ref, 0), (hr_ref, 2)):
        for c in range(3):
            ref[c * 128 : (c + 1) * 128, :] = pts_ref[c]
        ref[384:392, 0:128] = outs[k][0]
        ref[384:392, 128:256] = outs[k][1]


def plan(me, far_t, far_mid, near_t, nodes_t, nodes_mid, nodes_top, points):
    vm = pl.BlockSpec(memory_space=pltpu.VMEM)
    return pl.pallas_call(
        plan_kernel,
        out_shape=(
            jax.ShapeDtypeStruct((128, 32, 128), f32),
            jax.ShapeDtypeStruct((32, 128), f32),
            jax.ShapeDtypeStruct((8, 256), i32),
            jax.ShapeDtypeStruct((392, 256), f32),
            jax.ShapeDtypeStruct((392, 256), f32),
        ),
        in_specs=[pl.BlockSpec(memory_space=pltpu.SMEM)] + [vm] * 7,
        out_specs=(vm,) * 5,
        scratch_shapes=[pltpu.VMEM((1024, 256), f32)],
        compiler_params=pltpu.CompilerParams(vmem_limit_bytes=60 << 20),
        name="plan",
    )(me, far_t, far_mid, near_t, nodes_t, nodes_mid, nodes_top, points)


def dot3(a, b):
    return sum(dot(v.astype(bf16), b) for v in split3(a))


def moments_tail(part, child, q_ref, pt_ref, lm_ref, mm_ref, top_ref, lb_ref, ct_ref):
    lane = iota((64, 128), 1)
    lmt = jnp.zeros((64, 128), f32)
    for k in range(8):
        part(k).wait()

        def leaf(it, acc):
            for u in range(4):
                n = k * 16 + it * 4 + u
                prod = lb_ref[n] * q_ref[pl.ds(n, 1), :]
                col = jnp.sum(prod[:, 0:128] + prod[:, 128:256], axis=1, keepdims=True)
                acc = jnp.where(lane == n, col, acc)
            return acc

        lmt = lax.fori_loop(0, 4, leaf, lmt)
    lm_ref[...] = lmt.T
    child.wait()
    rows = []
    for i in range(64):
        rows.append(jnp.sum(ct_ref[i] * lmt, axis=0, keepdims=True))
    per_leaf = jnp.concatenate(rows, axis=0)
    group = jnp.where((iota((128, 128), 0) >> 3) == iota((128, 128), 1), 1.0, 0.0).astype(bf16)
    mm = dot3(per_leaf, group).T
    mm_ref[...] = mm[0:16, :]
    tops = []
    for g in range(2):
        acc = jnp.zeros((64, 64), f32)
        for c in range(g * 8, g * 8 + 8):
            acc = acc + pt_ref[c] * mm[c : c + 1, :]
        tops.append(jnp.broadcast_to(jnp.sum(acc, axis=1, keepdims=True), (64, 128)).T[0:1])
    top_ref[...] = jnp.concatenate(tops, axis=1)


def tile_rows(x, y, z, a, b):
    r = iota((8, 256), 0)
    v = jnp.where(r == 0, x, jnp.where(r == 1, y, jnp.where(r == 2, z, jnp.where(r == 3, a, b))))
    return jnp.where(r < 5, v, 0.0)


def near_tables(pts_ref, q_ref, sf_ref, qb_ref, count):
    r = iota((64, 128), 0)
    spread = jnp.where((r >= 48) & (r < 51), 1.0, 0.0).astype(bf16)
    r8 = iota((8, 256), 0)

    def factors(n):
        x = pts_ref[pl.ds(n, 1), :]
        y = pts_ref[pl.ds(128 + n, 1), :]
        z = pts_ref[pl.ds(256 + n, 1), :]
        norm = x * x + y * y + z * z + soften
        h, m, l = split3(tile_rows(x, y, z, jnp.ones_like(x), norm))
        qh, qm, ql = split3(jnp.broadcast_to(q_ref[pl.ds(n, 1), :], (8, 256)))
        q = jnp.where(r8 == 0, qh, jnp.where(r8 == 1, qm, jnp.where(r8 == 2, ql, 0.0)))
        return jnp.concatenate([h, m, l, h, m, h, q, jnp.zeros_like(q)], axis=0).T.astype(bf16)

    for n in range(8):
        sf_ref[n] = factors(n)

    def prepare(it, carry):
        for u in range(8):
            qb_ref[it * 8 + u] = dot(sf_ref[it * 8 + u], spread)
        ahead = jnp.minimum(it + 1, count // 8 - 1)
        made = [factors(ahead * 8 + u) for u in range(8)]
        for u in range(8):
            sf_ref[ahead * 8 + u] = made[u]
        return carry

    lax.fori_loop(0, count // 8, prepare, 0)


def near_pairs(entry, total, tgt, sf_ref, qb_ref, rhs_ref, d_ref, acc_ref):
    def factors(i, u):
        lv, _ = entry(i)
        lrow = jnp.maximum(lv - 1, 0)
        x = tgt[pl.ds(lrow, 1), :]
        y = tgt[pl.ds(128 + lrow, 1), :]
        z = tgt[pl.ds(256 + lrow, 1), :]
        norm = x * x + y * y + z * z
        h, m, l = split3(tile_rows(-2.0 * x, -2.0 * y, -2.0 * z, norm, jnp.ones_like(x)))
        rhs_ref[u] = jnp.concatenate([h, h, h, m, m, l], axis=0).astype(bf16)

    def distances(i, u):
        _, n = entry(i)
        d_ref[u] = dot(sf_ref[n, :, 0:48], rhs_ref[u])

    def sums(i, u):
        lv, n = entry(i)
        acc = jnp.zeros((8, 256), f32)
        for j in range(0, 256, 64):
            w = lax.rsqrt(d_ref[u, j : j + 64, :])
            q = qb_ref[n, j : j + 64, :]
            acc = acc + jnp.sum((w * jnp.concatenate([q, q], axis=1)).reshape(8, 8, 256), axis=0)
        row = jnp.where(lv > 0, lv - 1, 128)
        return row, jnp.sum(acc, axis=0, keepdims=True)

    for u in range(NB):
        factors(u, u)
    for u in range(NB):
        distances(u, u)
        factors(NB + u, u)

    def step(it, carry):
        i = it * NB
        got = [sums(i + u, u) for u in range(NB)]
        for u in range(NB):
            distances(i + NB + u, u)
        for u in range(NB):
            factors(i + 2 * NB + u, u)
        for row, val in got:
            acc_ref[pl.ds(row, 1), :] = acc_ref[pl.ds(row, 1), :] + val
        return carry

    lax.fori_loop(0, (total + NB - 1) // NB, step, 0)


def near_kernel(
    lst, tgt_l, tgt_r, pts_ref, q_ref, pt_ref, lb_hbm, ct_hbm,
    out_own, out_l, out_r, lm_ref, mm_ref, top_ref,
    sf_ref, qb_ref, rhs_ref, d_ref, acc_ref, lb_ref, ct_ref, sem,
):
    def part(k):
        rows = pl.ds(k * 16, 16)
        return pltpu.make_async_copy(lb_hbm.at[rows], lb_ref.at[rows], sem.at[k])

    child = pltpu.make_async_copy(ct_hbm, ct_ref, sem.at[8])
    for k in range(8):
        part(k).start()
    child.start()
    near_tables(pts_ref, q_ref, sf_ref, qb_ref, 128)
    for k, (tgt, out) in enumerate(((pts_ref, out_own), (tgt_l, out_l), (tgt_r, out_r))):
        acc_ref[...] = jnp.zeros((136, 256), f32)
        skip = SELF if k == 0 else 0

        def entry(i, first=k * 2048 + skip):
            return lst[first + i], lst[first + 1024 + i]

        near_pairs(entry, lst[k * 2048 + 896] - skip, tgt, sf_ref, qb_ref, rhs_ref, d_ref, acc_ref)
        out[...] = acc_ref[0:128, :]
    moments_tail(part, child, q_ref, pt_ref, lm_ref, mm_ref, top_ref, lb_ref, ct_ref)


def near(lists, arrays, leaf_basis, child):
    vm = pl.BlockSpec(memory_space=pltpu.VMEM)
    hbm = pl.BlockSpec(memory_space=pl.ANY)
    return pl.pallas_call(
        near_kernel,
        out_shape=tuple(jax.ShapeDtypeStruct((128, 256), f32) for _ in range(3))
        + (
            jax.ShapeDtypeStruct((128, 64), f32),
            jax.ShapeDtypeStruct((16, 64), f32),
            jax.ShapeDtypeStruct((1, 128), f32),
        ),
        in_specs=[pl.BlockSpec(memory_space=pltpu.SMEM)] + [vm] * 5 + [hbm] * 2,
        out_specs=(vm,) * 6,
        scratch_shapes=[
            pltpu.VMEM((128, 256, 64), bf16),
            pltpu.VMEM((128, 256, 128), f32),
            pltpu.VMEM((NB, 48, 256), bf16),
            pltpu.VMEM((NB, 256, 256), f32),
            pltpu.VMEM((136, 256), f32),
            pltpu.VMEM((128, 64, 256), f32),
            pltpu.VMEM((64, 64, 128), f32),
            pltpu.SemaphoreType.DMA((9,)),
        ],
        compiler_params=pltpu.CompilerParams(vmem_limit_bytes=60 << 20),
        name="near",
    )(lists, *arrays, leaf_basis, child)


def near_self_kernel(pts_ref, q_ref, part_ref, out, sf_ref, qb_ref, rhs_ref, d_ref, acc_ref):
    near_tables(pts_ref, q_ref, sf_ref, qb_ref, SELF)
    acc_ref[0:128, :] = part_ref[...]
    acc_ref[128:136, :] = jnp.zeros((8, 256), f32)

    def entry(i):
        n = jnp.minimum(i, SELF - 1)
        return n + 1, n

    near_pairs(entry, SELF, pts_ref, sf_ref, qb_ref, rhs_ref, d_ref, acc_ref)
    out[...] = acc_ref[0:128, :]


def near_self(points, charges, part):
    vm = pl.BlockSpec(memory_space=pltpu.VMEM)
    return pl.pallas_call(
        near_self_kernel,
        out_shape=jax.ShapeDtypeStruct((128, 256), f32),
        in_specs=[vm] * 3,
        out_specs=vm,
        scratch_shapes=[
            pltpu.VMEM((SELF, 256, 64), bf16),
            pltpu.VMEM((SELF, 256, 128), f32),
            pltpu.VMEM((NB, 48, 256), bf16),
            pltpu.VMEM((NB, 256, 256), f32),
            pltpu.VMEM((136, 256), f32),
        ],
        compiler_params=pltpu.CompilerParams(vmem_limit_bytes=60 << 20),
        name="near_self",
    )(points, charges, part)


def halves(x):
    h = x.astype(bf16).astype(f32)
    return h, (x - h).astype(bf16).astype(f32)


def features(x, y, z, source):
    parts = [halves(v) for v in (x, y, z)]
    norm = sum((h + m) * (h + m) for h, m in parts)
    one = jnp.ones_like(x)
    if source:
        nh, nm = halves(norm + soften)
        return [v for h, m in parts for v in (h, m, h, m)] + [one, one, nh, nm]
    nh, nm = halves(norm)
    return [v for h, m in parts for v in (-2.0 * h, -2.0 * h, -2.0 * m, -2.0 * m)] + [nh, nm, one, one]


def far_kernel(
    ids_ref, r1_ref, nl_ref, nm_ref, lm_ref, mm_ref, top_ref, out_ref, tops_ref, v_ref, u_ref, rep_ref, one_ref, mask_ref, ra_ref, mb_ref, full_ref
):
    for c in range(8):
        r = iota((128, 128), 0) - c * 16
        k = iota((128, 128), 1)
        lanes = slice((c % 2) * 128, (c % 2) * 128 + 128)
        rep_ref[c // 2, :, lanes] = jnp.where(r == (k >> 3), 1.0, 0.0).astype(bf16)
        one_ref[c // 2, :, lanes] = jnp.where((r >= 0) & (r < 3), 1.0, 0.0).astype(bf16)
        mask_ref[c] = jnp.where((iota((64, 128), 1) & 7) == c, 1.0, 0.0).astype(bf16)
    u_ref[...] = jnp.zeros((18 * 128, 64), f32)
    leaf = features(nl_ref[0].T, nl_ref[1].T, nl_ref[2].T, True)
    mid = features(nm_ref[0], nm_ref[1], nm_ref[2], True)
    for f in range(16):
        for blk in range(16):
            v_ref[pl.ds(blk * 128 + f, 8, stride=16), :] = leaf[f][blk * 8 : blk * 8 + 8]
        for blk in range(2):
            v_ref[pl.ds((16 + blk) * 128 + f, 8, stride=16), :] = mid[f][blk * 8 : blk * 8 + 8]

    for blk in range(18):
        src = lm_ref[blk * 8 : blk * 8 + 8, :] if blk < 16 else mm_ref[blk * 8 - 128 : blk * 8 - 120, :]
        for f, v in enumerate(split3(src)):
            u_ref[pl.ds(blk * 128 + f, 8, stride=16), :] = v

    def prepare(it, carry):
        for blk in (it * 3, it * 3 + 1, it * 3 + 2):
            rows = pl.ds(pl.multiple_of(blk * 128, 128), 128)
            v = v_ref[rows, :].T.astype(bf16)
            u = u_ref[rows, :].T.astype(bf16)
            for i in range(4):
                both = dot(v, rep_ref[i]).astype(bf16)
                ra_ref[blk * 8 + 2 * i] = both[:, 0:128]
                ra_ref[blk * 8 + 2 * i + 1] = both[:, 128:256]
                both = dot(u, one_ref[i])
                mb_ref[blk * 8 + 2 * i] = both[:, 0:128]
                mb_ref[blk * 8 + 2 * i + 1] = both[:, 128:256]
        return carry

    lax.fori_loop(0, 6, prepare, 0)
    low = iota((128, 128), 1) < 64
    low64 = iota((64, 128), 1) < 64

    def weights(x, y, z):
        tf = jnp.concatenate(features(x, y, z, False), axis=0)
        return jnp.concatenate([jnp.where(low, tf, 0.0), jnp.where(low, 0.0, tf)], axis=0).astype(bf16)

    def group(rhs, g, t0, t1):
        t0 = jnp.maximum(t0, 0)
        t1 = jnp.maximum(t1, 0)
        mask = mask_ref[g]
        lhs = jnp.concatenate([ra_ref[t0] * mask, ra_ref[t1] * mask], axis=1)
        m = jnp.where(low64, mb_ref[t0], mb_ref[t1])
        w = lax.rsqrt(dot(lhs, rhs)) * m
        return jnp.sum(jnp.sum(w.reshape(8, 8, 128), axis=0), axis=0, keepdims=True)

    def leaf_groups(p, groups):
        rhs = weights(*(r1_ref[pl.ds(pl.multiple_of(p * 32 + 8 * c, 8), 8), :] for c in range(3)))
        return [(p, g, group(rhs, g, ids_ref[p * 24 + g], ids_ref[p * 24 + 8 + g])) for g in groups]

    for c in range(3):
        tops_ref[c * 128 : (c + 1) * 128, :] = r1_ref[pl.ds(28 + c, 128, stride=32), :]
    out_ref[...] = jnp.zeros((1280, 128), f32)
    out_ref[pl.ds(9, 128, stride=10), :] = jnp.broadcast_to(top_ref[...], (128, 128))

    def first(it, carry):
        got = []
        for u in range(4):
            got += leaf_groups(it * 4 + u, range(4))
        for p, g, val in got:
            out_ref[pl.ds(p * 10 + g, 1), :] = val
        return carry

    lax.fori_loop(0, 32, first, 0)

    def scan(it, pos):
        for u in range(8):
            p = it * 8 + u
            full_ref[pos] = p
            pos = pos + (ids_ref[p * 24 + 18] > 8).astype(i32)
        return pos

    full = lax.fori_loop(0, 16, scan, jnp.int32(0))
    full_ref[full] = 0

    def second(it, carry):
        got = []
        for u in range(2):
            got += leaf_groups(full_ref[it * 2 + u], range(4, 8))
        for p, g, val in got:
            out_ref[pl.ds(p * 10 + g, 1), :] = val
        return carry

    lax.fori_loop(0, (full + 1) // 2, second, 0)

    def mids(it, carry):
        got = []
        for u in range(2):
            b = (it * 2 + u) * 256 + 24
            rhs = weights(*(r1_ref[pl.ds(b + c, 8, stride=32), :] for c in range(3)))
            for g in range(8):
                p = (it * 2 + u) * 8 + g
                got.append((p, group(rhs, g, 128 + ids_ref[p * 24 + 16], 128 + ids_ref[p * 24 + 17])))
        for p, val in got:
            out_ref[pl.ds(p * 10 + 8, 1), :] = val
        return carry

    lax.fori_loop(0, 8, mids, 0)


def far(ids, r1, nodes_t, nodes_mid, moments, mid_moments, top_row):
    vm = pl.BlockSpec(memory_space=pltpu.VMEM)
    return pl.pallas_call(
        far_kernel,
        out_shape=(jax.ShapeDtypeStruct((1280, 128), f32), jax.ShapeDtypeStruct((384, 128), f32)),
        in_specs=[pl.BlockSpec(memory_space=pltpu.SMEM)] + [vm] * 6,
        out_specs=(vm, vm),
        scratch_shapes=[
            pltpu.VMEM((18 * 128, 64), f32),
            pltpu.VMEM((18 * 128, 64), f32),
            pltpu.VMEM((4, 128, 256), bf16),
            pltpu.VMEM((4, 128, 256), bf16),
            pltpu.VMEM((8, 64, 128), bf16),
            pltpu.VMEM((144, 64, 128), bf16),
            pltpu.VMEM((144, 64, 128), f32),
            pltpu.SMEM((136,), i32),
        ],
        compiler_params=pltpu.CompilerParams(vmem_limit_bytes=60 << 20),
        name="far",
    )(ids, r1, nodes_t, nodes_mid, moments, mid_moments, top_row)


def final_kernel(
    top_ids, tab_ref, tops_ref, r2_ref, nt_ref, pt_ref, near_ref, bl_ref, br_ref, lb_hbm, ct_hbm, out_ref, lb_ref, ct_ref, sem
):
    def part(k):
        rows = pl.ds(k * 16, 16)
        return pltpu.make_async_copy(lb_hbm.at[rows], lb_ref.at[rows], sem.at[k])

    child = pltpu.make_async_copy(ct_hbm, ct_ref, sem.at[8])
    child.start()
    for k in range(8):
        part(k).start()
    tag = (iota((128, 128), 0) + 1).astype(f32)

    def lines(k, rows):
        return jnp.where(tab_ref[k : k + 1, :] == tag[0:rows], 1.0, 0.0)

    def two(x):
        return jnp.concatenate(halves(x), axis=1).astype(bf16)

    acc = [jnp.zeros((128, 256), f32), jnp.zeros((128, 256), f32)]
    for g in range(0, 8, 2):
        vals = jnp.concatenate([two(r2_ref[pl.ds(g + k, 128, stride=10), :]) for k in range(2)], axis=0)
        for h in range(2):
            oh = jnp.concatenate([lines(8 * h + g, 128), lines(8 * h + g + 1, 128)], axis=1).astype(bf16)
            acc[h] = acc[h] + dot(oh, vals)
    acc = [a[:, 0:128] + a[:, 128:256] for a in acc]
    local_t = acc[0].T[0:64] + acc[1].T[64:128]
    vals = two(r2_ref[pl.ds(8, 128, stride=10), :])
    res = [dot(lines(16 + h, 16).astype(bf16), vals) for h in range(2)]
    res = [a[:, 0:128] + a[:, 128:256] for a in res]
    mid_local = res[0][:, 0:64] + res[1][:, 64:128]
    half = iota((1, 128), 1) >> 6
    pad = jnp.zeros((6, 64), f32)
    cols = [jnp.concatenate([nt_ref[c], pad], axis=0).T for c in range(3)]
    rows = []
    for g in range(2):
        tx, ty, tz = (jnp.broadcast_to(cols[c][:, g : g + 1], (64, 128)) for c in range(3))

        def entry(it, total):
            for u in range(4):
                t = top_ids[g, it * 4 + u]
                p = jnp.maximum(t, 0) >> 1
                h = jnp.where(t < 0, 2, t & 1)
                m = jnp.where(half == h, r2_ref[pl.ds(p * 10 + 9, 1), :], 0.0)
                dx = tx - tops_ref[pl.ds(p, 1), :]
                dy = ty - tops_ref[pl.ds(128 + p, 1), :]
                dz = tz - tops_ref[pl.ds(256 + p, 1), :]
                total = total + lax.rsqrt(dx * dx + dy * dy + dz * dz + soften) * m
            return total

        total = lax.fori_loop(0, 4, entry, jnp.zeros((64, 128), f32))
        top = jnp.broadcast_to(jnp.sum(total, axis=1, keepdims=True), (64, 64))
        for c in range(g * 8, g * 8 + 8):
            rows.append(jnp.sum(pt_ref[c] * top, axis=0, keepdims=True))
    mid_down = mid_local + jnp.concatenate(rows, axis=0)
    mid_t = jnp.concatenate([mid_down, jnp.zeros((112, 64), f32)], axis=0).T
    spread = jnp.where(iota((128, 128), 0) == (iota((128, 128), 1) >> 3), 1.0, 0.0).astype(bf16)
    mid_t = dot3(mid_t, spread)
    child.wait()
    down = local_t
    for i in range(64):
        down = down + ct_ref[i] * mid_t[i : i + 1, :]
    h, m = halves(down)
    pick = jnp.where((iota((32, 2048), 0) & 15) == (iota((32, 2048), 1) >> 7), 1.0, 0.0).astype(bf16)
    for k in range(8):
        part(k).wait()
        ks = slice(16 * k, 16 * k + 16)
        cols16 = dot(jnp.concatenate([h[:, ks], m[:, ks]], axis=1).astype(bf16), pick)
        for u in range(16):
            d = cols16[:, u * 128 : u * 128 + 128]
            n = 16 * k + u
            out_ref[n : n + 1, :] = jnp.sum(lb_ref[n] * jnp.concatenate([d, d], axis=1), axis=0, keepdims=True)
    out_ref[...] = out_ref[...] + near_ref[...] + bl_ref[...] + br_ref[...]


def final(far_top, arrays, leaf_basis, child):
    vm = pl.BlockSpec(memory_space=pltpu.VMEM)
    hbm = pl.BlockSpec(memory_space=pl.ANY)
    return pl.pallas_call(
        final_kernel,
        out_shape=jax.ShapeDtypeStruct((128, 256), f32),
        in_specs=[pl.BlockSpec(memory_space=pltpu.SMEM)] + [vm] * 8 + [hbm] * 2,
        out_specs=vm,
        scratch_shapes=[
            pltpu.VMEM((128, 64, 256), f32),
            pltpu.VMEM((64, 64, 128), f32),
            pltpu.SemaphoreType.DMA((9,)),
        ],
        compiler_params=pltpu.CompilerParams(vmem_limit_bytes=60 << 20),
        name="final",
    )(far_top, *arrays, leaf_basis, child)


def swap(x):
    return lax.all_to_all(x, AXES, split_axis=0, concat_axis=0, tiled=True)


def local(
    charges,
    points,
    leaf_basis,
    child_transfer,
    parent_transfer,
    nodes_leaf,
    nodes_mid,
    nodes_top,
    near_list,
    far_leaf,
    far_mid,
    far_top,
):
    shards = lax.axis_size(AXES)
    me = lax.axis_index(AXES).astype(i32).reshape(1)
    down_perm = [(i + 1, i) for i in range(shards - 1)]
    up_perm = [(i, i + 1) for i in range(shards - 1)]
    nodes_t = jnp.transpose(nodes_leaf, (0, 2, 1))
    pay, tab, own_list, to_left, to_right = plan(
        me, far_leaf.T, far_mid, near_list.T, nodes_t, nodes_mid, nodes_top, points
    )
    from_right = lax.ppermute(to_left, AXES, down_perm)
    from_left = lax.ppermute(to_right, AXES, up_perm)
    r1 = swap(pay)
    child = jnp.transpose(child_transfer, (1, 2, 0))
    lists = jnp.stack([own_list, from_left[384:392].astype(i32), from_right[384:392].astype(i32)])
    lists = jnp.transpose(lists.reshape(3, 8, 2, 128), (0, 2, 1, 3)).reshape(6144)
    flat = points.reshape(384, 256)
    near_own, near_l, near_r, leaf_moments, mid_moments, top_moments = near(
        lists, [from_left, from_right, flat, charges, parent_transfer], leaf_basis, child
    )
    r1, near_own, leaf_moments, mid_moments, top_moments = lax.optimization_barrier(
        (r1, near_own, leaf_moments, mid_moments, top_moments)
    )
    ids = r1[:, 27, 0:24].astype(i32).reshape(3072)
    r1 = r1.reshape(4096, 128)
    pay2, tops = far(ids, r1, nodes_t, nodes_mid, leaf_moments, mid_moments, top_moments)
    r2 = swap(pay2.reshape(128, 5, 2, 128)).reshape(1280, 128)
    back_l = lax.ppermute(near_l, AXES, down_perm)
    back_r = lax.ppermute(near_r, AXES, up_perm)
    near_own = near_self(flat, charges, near_own)
    return final(far_top, [tab, tops, r2, nodes_top, parent_transfer, near_own, back_l, back_r], leaf_basis, child)


def solution(mesh):
    placed = (
        P(AXES, None),
        P(None, AXES, None),
        P(AXES, None, None),
        P(AXES, None, None),
        P(AXES, None, None),
        P(None, AXES, None),
        P(None, AXES, None),
        P(None, AXES, None),
        P(AXES, None),
        P(AXES, None),
        P(AXES, None),
        P(AXES, None),
    )
    return jax.shard_map(local, mesh=mesh, in_specs=placed, out_specs=P(AXES, None), check_vma=False)
```
